32 devices in a mesh: dp: 8 (over z, y), tensor: 4 (over x, core).
Axes of the slice: x: 2, y: 2, z: 4, core: 2. Of those that a mesh axis runs over, the one named last changes fastest.
Arguments:
- tokens: bfloat16 [1024, 32, 512], P('dp', 'tensor'), may hold values from -6 to 6
- cotangent: bfloat16 [1024, 32, 512], P('dp', 'tensor'), may hold values from -6 to 6
- lengths: int32 [32], replicated, may hold values from 1 to 1024, 20480 in all
- ln_gain: float32 [512], P('dp'), may hold values from 0.5 to 1.5
- ln_bias: float32 [512], P('dp'), may hold values from -3 to 3
- lam_log: float32 [512, 64], P('tensor', 'dp'), may hold values from -2.3 to 0
- lam_im: float32 [512, 64], P('tensor', 'dp'), may hold values from 0 to 3
- w_re: float32 [512, 64], P('tensor', 'dp'), may hold values from -6 to 6
- w_im: float32 [512, 64], P('tensor', 'dp'), may hold values from -6 to 6
- log_dt: float32 [512], P('dp'), may hold values from -6.9 to -2.3
- skip_gain: float32 [512], P('dp'), may hold values from -4 to 4
- w_out: bfloat16 [512, 1024], P('tensor', 'dp'), may hold values from -0.5 to 0.5
- b_out: float32 [1024], P('dp'), may hold values from -3 to 3
Outputs:
- out: bfloat16 [1024, 32, 512], P('dp', 'tensor')
- grad_tokens: bfloat16 [1024, 32, 512], P('dp', 'tensor')
- grad_ln_gain: float32 [512], P('dp')
- grad_ln_bias: float32 [512], P('dp')
- grad_lam_log: float32 [512, 64], P('tensor', 'dp')
- grad_lam_im: float32 [512, 64], P('tensor', 'dp')
- grad_w_re: float32 [512, 64], P('tensor', 'dp')
- grad_w_im: float32 [512, 64], P('tensor', 'dp')
- grad_log_dt: float32 [512], P('dp')
- grad_skip_gain: float32 [512], P('dp')
- grad_w_out: float32 [512, 1024], P('tensor', 'dp')
- grad_b_out: float32 [1024], P('dp')
The draws below stay inside these ranges and needn't reach their ends.
Inputs may be any that keep to these rules, and one draw needn't show every extreme that they name: lengths[s] is sequence s's length; its positions at or past it are padding.
All inputs are finite; a program needn't handle non-finite values.
Results may differ from the reference program's by a relative error of at most 0.02.
Values may be sent and summed in bfloat16 or wider, within the bound.
No kernel may reach another device: no remote copies, remote signals or barrier semaphores. Data moves between devices by JAX's collectives and lax.ppermute only.
A program may use at most 256 MiB of HBM per device.

```python
import math
import jax
import jax.numpy as jnp
import numpy as np
from jax import lax

D = 512
NS = 64
LMAX = 1024
SEQ_DEV = 1
SEQS = 32
N_TENSOR = 4


def steps_of(own_key, extent, split, low, high):
    loudness, own = 1.0, jax.random.fold_in(own_key, 6)
    for dim, parts in split:
        steps = jnp.exp(jax.random.uniform(jax.random.fold_in(own, dim), (parts,), jnp.float32, low / len(split), high / len(split)))
        loudness = loudness * jnp.repeat(steps, extent[dim] // parts).reshape([-1 if axis == dim else 1 for axis in range(len(extent))])
    return loudness


def length_profile(number_of, total, reach, slope):
    loads = [(1 << 20) // math.isqrt(standing ** slope) + 1 for standing in range(2, number_of + 1)]
    surplus, given = total - reach - (number_of - 1), [1] * (number_of - 1)
    while surplus > 0:
        free = [i for i in range(number_of - 1) if given[i] < reach]
        whole, remaining = sum([loads[i] for i in free]), surplus
        for i in free:
            extra = min(reach - given[i], max(1, remaining * loads[i] // whole), surplus)
            given[i] = given[i] + extra
            surplus = surplus - extra
    return np.array([reach] + given)


def ragged(stream_key, count, total, most, skew):
    if count == 2:
        one = jax.random.randint(stream_key, (), max(1, total - most), min(most, total - 1) + 1)
        return jnp.stack([one, total - one])
    sizes = jnp.asarray(length_profile(count, total, most, skew), jnp.int32)
    couples = (count - 1) // 2
    donor, taker = sizes[1:1 + 2 * couples:2], sizes[2:2 + 2 * couples:2]
    slack = jnp.minimum(donor - 1, most - taker)
    moved = jax.random.randint(jax.random.fold_in(stream_key, 1), (couples,), 0, 1 << 20) % (slack + 1)
    sizes = sizes.at[1:1 + 2 * couples:2].set(donor - moved).at[2:2 + 2 * couples:2].set(taker + moved)
    return sizes[jax.random.permutation(jax.random.fold_in(stream_key, 2), count)]


def noise(own_key, dims, width, limit, split=(), kind=jnp.bfloat16):
    drawn = width * jax.random.normal(own_key, dims, jnp.float32)
    if split:
        drawn = drawn * steps_of(own_key, dims, split, -0.22, 0.18)
    return jnp.clip(drawn, -limit, limit).astype(kind)


def setup_inputs(seed: int = 0) -> dict:
    splits = jax.random.split(jax.random.key(seed), 14)
    return {
        "tokens": noise(splits[0], (LMAX, SEQS, D), 1.0, 6.0, ((0, 8), (1, 4))),
        "cotangent": noise(splits[1], (LMAX, SEQS, D), 1.0, 6.0, ((0, 8), (1, 4))),
        "lengths": ragged(splits[2], SEQS, SEQS * LMAX * 5 // 8, LMAX, 1).astype(jnp.int32),
        "ln_gain": jnp.clip(1.0 + 0.1 * jax.random.normal(splits[3], (D,), jnp.float32), 0.5, 1.5),
        "ln_bias": noise(splits[4], (D,), 0.5, 3.0, ((0, 8),), jnp.float32),
        "lam_log": jnp.clip(-2.3 + 2.3 * jax.random.uniform(splits[5], (D, NS), jnp.float32) ** steps_of(splits[5], (D, NS), ((0, 4), (1, 8)), -0.2, 0.2), -2.3, 0.0),
        "lam_im": jnp.clip(3.0 * jax.random.uniform(splits[6], (D, NS), jnp.float32) ** steps_of(splits[6], (D, NS), ((0, 4), (1, 8)), -0.2, 0.2), 0.0, 3.0),
        "w_re": noise(splits[7], (D, NS), 1.0, 6.0, ((0, 4), (1, 8)), jnp.float32),
        "w_im": noise(splits[8], (D, NS), 1.0, 6.0, ((0, 4), (1, 8)), jnp.float32),
        "log_dt": jnp.clip(-6.9 + 4.6000001430511475 * jax.random.uniform(splits[9], (D,), jnp.float32) ** steps_of(splits[9], (D,), ((0, 8),), -0.2, 0.2), -6.9, -2.3),
        "skip_gain": noise(splits[10], (D,), 1.0, 4.0, ((0, 8),), jnp.float32),
        "w_out": noise(splits[11], (D, 2 * D), (D // 4) ** -0.5, 0.5, ((0, 4), (1, 8))),
        "b_out": noise(splits[12], (2 * D,), 0.5, 3.0, ((0, 8),), jnp.float32),
    }


epsilon = 1e-05

@jax.custom_vjp
def low(v):
    return lax.optimization_barrier(v.astype(jnp.bfloat16)).astype(jnp.float32)

@jax.custom_vjp
def low_back(v):
    return v

def low_keep(v):
    return (low(v), None)

def low_pass(kept, grad):
    return (grad,)

def back_keep(v):
    return (v, None)

def back_low(kept, grad):
    return (low(grad),)
low.defvjp(low_keep, low_pass)
low_back.defvjp(back_keep, back_low)

def layer_norm(values, gain_vec, bias_vec):
    average = lax.optimization_barrier(jnp.mean(values, axis=-1, keepdims=True))
    centred = values - average
    spread = lax.optimization_barrier(jnp.mean(centred * centred, axis=-1, keepdims=True))
    return centred * lax.rsqrt(spread + epsilon) * gain_vec + bias_vec

def dss_kernel(lam_log, lam_im, w_re, w_im, log_dt, length):
    step_size = jnp.exp(log_dt)
    places = jnp.arange(length, dtype=jnp.float32)[:, None, None]
    decay_rate = jnp.exp(lam_log) * step_size[:, None]
    turning = lam_im * step_size[:, None]
    angles = places * turning
    summands = jnp.exp(-(places * decay_rate)) * (w_re * jnp.cos(angles) - w_im * jnp.sin(angles))
    return step_size * lax.optimization_barrier(jnp.sum(summands, axis=-1))

def reference(tokens, cotangent, lengths, ln_gain, ln_bias, lam_log, lam_im, w_re, w_im, log_dt, skip_gain, w_out, b_out):
    group_size = SEQ_DEV * N_TENSOR
    batches = SEQS // group_size
    live_mask = (jnp.arange(LMAX, dtype=jnp.int32)[:, None] < lengths[None, :]).astype(jnp.float32)
    mask_blocks = live_mask.reshape(LMAX, batches, group_size).transpose(1, 0, 2)
    token_data = tokens.astype(jnp.float32)
    weight_out = w_out.astype(jnp.float32)

    def forward(inputs, gain_vec, bias_vec, lam_log, lam_im, w_re, w_im, log_dt, skip_gain, weight_out, bias_out):
        kernel_low = low(dss_kernel(lam_log, lam_im, w_re, w_im, log_dt, LMAX))
        spectrum = jnp.fft.rfft(kernel_low, n=2 * LMAX, axis=0)

        def one_batch(packed):
            pieces, mask_piece = packed
            signal = low_back(low(layer_norm(pieces, gain_vec, bias_vec)))
            convolved = jnp.fft.irfft(jnp.fft.rfft(signal, n=2 * LMAX, axis=0) * spectrum[:, None, :], n=2 * LMAX, axis=0)[:LMAX]
            mixed_out = low_back(convolved + skip_gain * signal)
            active = low(low_back(jax.nn.gelu(mixed_out, approximate=True)))
            flat_pre = jnp.dot(active.reshape(-1, D), weight_out, precision=lax.Precision.HIGHEST)
            before = low_back(flat_pre.reshape(LMAX, group_size, 2 * D) + bias_out)
            gated_out = before[..., :D] * jax.nn.sigmoid(before[..., D:])
            return pieces + mask_piece[:, :, None] * gated_out
        batched = inputs.reshape(LMAX, batches, group_size, D).transpose(1, 0, 2, 3)
        results = lax.map(jax.checkpoint(one_batch), (batched, mask_blocks))
        return results.transpose(1, 0, 2, 3).reshape(LMAX, SEQS, D)
    result, pullback = jax.vjp(forward, token_data, ln_gain, ln_bias, lam_log, lam_im, w_re, w_im, log_dt, skip_gain, weight_out, b_out)
    gradients = pullback(cotangent.astype(jnp.float32))
    return (result.astype(jnp.bfloat16), gradients[0].astype(jnp.bfloat16), gradients[1], gradients[2], gradients[3], gradients[4], gradients[5], gradients[6], gradients[7], gradients[8], gradients[9], gradients[10])
```

```python
from functools import partial

import jax
import jax.numpy as jnp
import numpy as np
from jax import lax
from jax.experimental import pallas as pl
from jax.experimental.pallas import tpu as pltpu
from jax.sharding import PartitionSpec as P

epsilon = 1e-05
f32 = jnp.float32
bf16 = jnp.bfloat16


def params(mib):
    return pltpu.CompilerParams(vmem_limit_bytes=mib * 1024 * 1024)


def cost(us):
    return pl.CostEstimate(flops=0, bytes_accessed=int(us * 3.3e6), transcendentals=0)


def keep(shape, dtype):
    return pltpu.VMEM(shape, dtype)


def held_in_vmem(*arrays):
    return [pltpu.with_memory_space_constraint(a, pltpu.VMEM) for a in arrays]


def vspec():
    return pl.BlockSpec(memory_space=pltpu.VMEM)


def sspec():
    return pl.BlockSpec(memory_space=pltpu.SMEM)


def basis(block):
    freq = np.concatenate([np.arange(0, block, 2), np.arange(1, block, 2)])
    angle = np.pi * (2 * freq[:, None] + 1) * np.arange(block)[None, :] / (2 * block)
    forward = np.concatenate([np.cos(angle), -np.sin(angle)], axis=0)
    return forward.astype(np.float32)


def shift_exchange(pieces, axis, size):
    out = [pieces[0]]
    for s in range(1, size):
        out.append(lax.ppermute(pieces[s], axis, [(k, (k + s) % size) for k in range(size)]))
    return out


def flip_bit(value, axis, size, bit):
    return lax.ppermute(value, axis, [(k, k ^ bit) for k in range(size)])


WIDE = 128


def pad_to(value, multiple):
    return -(-value // multiple) * multiple


def split_kernel(n, states, par_ref, vec_ref, w_ref, out):
    rows = 4 * states
    base = 0
    for ref in (par_ref, vec_ref):
        rest = ref[...]
        count = rest.shape[0]
        for _ in range(3):
            plane = rest.astype(bf16)
            out[0, base : base + count, :] = plane
            rest = rest - plane.astype(f32)
            base += count
    top = out.shape[1] - w_ref.shape[0]
    out[0, top:, :] = w_ref[...]
    for d in range(1, n):
        out[d] = out[0]


def pack_weights(n, par, vec, w):
    states = par.shape[0] // 4
    rows = pad_to(3 * (par.shape[0] + vec.shape[0]), 16) + w.shape[0]
    return pl.pallas_call(
        partial(split_kernel, n, states),
        out_shape=jax.ShapeDtypeStruct((n, rows, WIDE), bf16),
        in_specs=[vspec()] * 3,
        out_specs=vspec(),
        compiler_params=params(4),
        name="pack_weights",
    )(par, vec, w)


INNER = 32


def powers(table_r, table_i, zr, zi, count):
    cr, ci = jnp.ones_like(zr), jnp.zeros_like(zi)
    for b in range(count):
        table_r[b] = cr
        table_i[b] = ci
        if b + 1 < count:
            cr, ci = cr * zr - ci * zi, cr * zi + ci * zr


def taps_kernel(n, states, channels, w_cols, sc, blob, out, w_out, par_out, vec_out, b_out, table_r, table_i, part):
    rank_t = sc[2]
    count = 4 * states
    vec_rows = (blob.shape[1] - w_out.shape[1]) // 3 - count
    per = vec_out.shape[1] // n
    plane = [blob[:, k * count : (k + 1) * count, :].astype(f32) for k in range(3)]
    par = plane[0] + plane[1] + plane[2]
    for d in range(n):
        for k in range(4):
            par_out[k, d * states : (d + 1) * states, :] = par[d, k * states : (k + 1) * states, :channels]
    vecs = VEC_ROWS(per)
    for d in range(n):
        vec = sum(
            blob[d, 3 * count + k * vecs : 3 * count + (k + 1) * vecs, :].astype(f32) for k in range(3)
        )
        for k in range(4):
            row, lane = divmod(k * per, WIDE)
            vec_out[k : k + 1, d * per : (d + 1) * per] = vec[row : row + 1, lane : lane + per]
        row, lane = divmod(4 * per, WIDE)
        b_out[:, 2 * d * per : 2 * (d + 1) * per] = vec[row : row + 1, lane : lane + 2 * per]
        w_out[d] = blob[d, blob.shape[1] - w_out.shape[1] :, :w_cols]
    log_step = vec_out[2:3, 0:channels]
    for t in range(1, vec_out.shape[1] // channels):
        log_step = jnp.where(rank_t == t, vec_out[2:3, t * channels : (t + 1) * channels], log_step)
    vec_out[4:5, 0:channels] = log_step
    step = jnp.exp(log_step)
    decay = jnp.exp(par_out[0]) * step
    turn = par_out[1] * step
    size = jnp.exp(-decay)
    powers(table_r, table_i, size * jnp.cos(turn), size * jnp.sin(turn), INNER)
    far = jnp.exp(-INNER * decay)
    far_r, far_i = far * jnp.cos(INNER * turn), far * jnp.sin(INNER * turn)
    total = decay.shape[0]

    def block(a, carry):
        ar, ai = carry
        for b in range(INNER):
            value = ar * table_r[b] - ai * table_i[b]
            part[b * 8 : (b + 1) * 8, :] = jnp.sum(value.reshape(total // 8, 8, channels), axis=0)
        summed = part[pl.ds(0, INNER, stride=8), :]
        for q in range(1, 8):
            summed = summed + part[pl.ds(q, INNER, stride=8), :]
        out[pl.ds(pl.multiple_of(a * INNER, INNER), INNER), :] = summed.astype(bf16)
        return ar * far_r - ai * far_i, ar * far_i + ai * far_r

    lax.fori_loop(0, out.shape[0] // INNER, block, (par_out[2] * step, par_out[3] * step))


def VEC_ROWS(per):
    return -(-6 * per // WIDE)


def make_taps(scalars, blob, states, length, width, channels, w_cols):
    n = blob.shape[0]
    total = n * states
    return pl.pallas_call(
        partial(taps_kernel, n, states, channels, w_cols),
        out_shape=[
            jax.ShapeDtypeStruct((length, channels), bf16),
            jax.ShapeDtypeStruct((n, channels, w_cols), bf16),
            jax.ShapeDtypeStruct((4, total, channels), f32),
            jax.ShapeDtypeStruct((8, width), f32),
            jax.ShapeDtypeStruct((1, 2 * width), f32),
        ],
        in_specs=[sspec(), vspec()],
        out_specs=[vspec()] * 5,
        scratch_shapes=[
            pltpu.VMEM((INNER, total, channels), f32),
            pltpu.VMEM((INNER, total, channels), f32),
            pltpu.VMEM((INNER * 8, channels), f32),
        ],
        compiler_params=params(8),
        cost_estimate=cost(7),
        name="taps",
    )(scalars, blob)


def taps_back_kernel(
    n, states, sc, par, vec, grad_a, grad_b, w_a, w_b, gain8, bias8, out8, msg, table_r, table_i, summed, held
):
    rank_t = sc[2]
    length, channels = summed.shape
    width = vec.shape[1]
    rate = jnp.exp(par[0])
    step = jnp.exp(vec[4:5, 0:channels])
    decay = rate * step
    turn = par[1] * step
    w_re, w_im = par[2], par[3]
    size = jnp.exp(-decay)
    powers(table_r, table_i, size * jnp.cos(turn), size * jnp.sin(turn), INNER)
    far = jnp.exp(-INNER * decay)
    far_r, far_i = far * jnp.cos(INNER * turn), far * jnp.sin(INNER * turn)
    total = decay.shape[0]
    summed[...] = grad_a[...].astype(f32) + grad_b[...].astype(f32)
    zero = jnp.zeros((total, channels), f32)

    def block(k, carry):
        a = length // INNER - 1 - k
        s0r, s0i, s1r, s1i = [held[q] for q in range(4)]
        s1r, s1i = s1r + INNER * s0r, s1i + INNER * s0i
        s0r, s0i = s0r * far_r - s0i * far_i, s0r * far_i + s0i * far_r
        s1r, s1i = s1r * far_r - s1i * far_i, s1r * far_i + s1i * far_r
        for q, value in enumerate((s0r, s0i, s1r, s1i)):
            held[q] = value
        rows = summed[pl.ds(pl.multiple_of(a * INNER, INNER), INNER), :]
        for c in range(total // 8):
            here = slice(c * 8, (c + 1) * 8)
            u0r, u0i, u1r, u1i = [held[q, here, :] for q in range(4)]
            for b in range(INNER):
                g = jnp.broadcast_to(rows[b : b + 1, :], (8, channels))
                tr, ti = g * table_r[b, here, :], g * table_i[b, here, :]
                u0r, u0i = u0r + tr, u0i + ti
                if b:
                    u1r, u1i = u1r + float(b) * tr, u1i + float(b) * ti
            for q, value in enumerate((u0r, u0i, u1r, u1i)):
                held[q, here, :] = value
        return carry

    for q in range(4):
        held[q] = zero
    lax.fori_loop(0, length // INNER, block, 0)
    s0r, s0i, s1r, s1i = [held[q] for q in range(4)]
    wr0 = w_re * s0r - w_im * s0i
    wr1 = w_re * s1r - w_im * s1i
    wi1 = w_re * s1i + w_im * s1r
    dt = jnp.sum(step * (wr0 - decay * wr1 - turn * wi1), axis=0, keepdims=True)
    held[0], held[1] = -step * decay * wr1, -step * step * wi1
    held[2], held[3] = step * s0r, -step * s0i
    rows_w = w_a.shape[1]
    lines = width // WIDE
    top = rows_w + 4 * states
    msg[...] = jnp.zeros_like(msg)
    for d in range(n):
        msg[d, 0:rows_w, : w_a.shape[2]] = (w_a[d].astype(f32) + w_b[d].astype(f32)).astype(bf16)
        for k in range(4):
            msg[d, rows_w + k * states : rows_w + (k + 1) * states, :channels] = held[
                k, d * states : (d + 1) * states, :
            ].astype(bf16)
    gain_sum = jnp.sum(gain8[...], axis=0, keepdims=True)
    bias_sum = jnp.sum(bias8[...], axis=0, keepdims=True)
    out_sum = jnp.sum(out8[...], axis=0, keepdims=True)
    copies = WIDE // channels
    lane = lax.broadcasted_iota(jnp.int32, (1, WIDE), 1) // channels
    skip_row = jnp.concatenate([summed[0:1, :]] * copies, axis=1) if copies > 1 else summed[0:1, :]
    dt_row = jnp.concatenate([dt] * copies, axis=1) if copies > 1 else dt
    for line in range(lines):
        at = slice(line * WIDE, (line + 1) * WIDE)
        mine = lane + line * copies == rank_t
        rows = [
            gain_sum[:, at],
            bias_sum[:, at],
            jnp.where(mine, dt_row, 0.0),
            jnp.where(mine, skip_row, 0.0),
            out_sum[:, at],
            out_sum[:, width + line * WIDE : width + (line + 1) * WIDE],
        ]
        for k, row in enumerate(rows):
            place = top + k * lines + line
            for d in range(n):
                msg[d, place : place + 1, :] = row.astype(bf16)


def taps_back(scalars, par, vec, grads, w_grads, gain8, bias8, out8, n, states):
    length, channels = grads[0].shape
    width = vec.shape[1]
    total = par.shape[1]
    w_grads = [w.reshape(n, channels, -1) for w in w_grads]
    rows = pad_to(channels + 4 * states + 6 * (width // WIDE), 16)
    return pl.pallas_call(
        partial(taps_back_kernel, n, states),
        out_shape=jax.ShapeDtypeStruct((n, rows, WIDE), bf16),
        in_specs=[sspec()] + [vspec()] * 9,
        out_specs=vspec(),
        scratch_shapes=[
            pltpu.VMEM((INNER, total, channels), f32),
            pltpu.VMEM((INNER, total, channels), f32),
            pltpu.VMEM((length, channels), f32),
            pltpu.VMEM((4, total, channels), f32),
        ],
        compiler_params=params(10),
        cost_estimate=cost(10),
        name="taps_back",
    )(scalars, par, vec, *grads, *w_grads, gain8, bias8, out8)


ROWS = 32
TILE = 16
LANES = 128


def normalize(x):
    width = x.shape[-1]
    mean = jnp.sum(x, axis=-1, keepdims=True) * (1.0 / width)
    centred = x - mean
    var = jnp.sum(centred * centred, axis=-1, keepdims=True) * (1.0 / width)
    scale = lax.rsqrt(var + epsilon)
    return centred * scale, scale


def tiles(first, last, width, body):
    def step(r, carry):
        row = pl.multiple_of(r * TILE, TILE)
        for c in range(width // LANES):
            body(row, slice(c * LANES, (c + 1) * LANES))
        return carry

    lax.fori_loop(first // TILE, last // TILE, step, 0)


def enter_kernel(n, blocks, block, sc, vec, basis_ref, *refs):
    pieces = refs[:n]
    tok_all, sig, xs = refs[n:]
    rank = sc[0]
    rows = pieces[0].shape[0]
    length, width = tok_all.shape
    for s in range(n):
        src = lax.rem(rank - s + n, n)
        tok_all[pl.ds(pl.multiple_of(src * rows, rows), rows), :] = pieces[s][...]

    def transform(j, carry):
        def norm(r, carry):
            at = pl.ds(pl.multiple_of(j * block + r * ROWS, ROWS), ROWS)
            xhat, _ = normalize(tok_all[at, :].astype(f32))
            sig[at, :] = (xhat * vec[0:1, :] + vec[1:2, :]).astype(bf16)
            return carry

        lax.fori_loop(0, block // ROWS, norm, 0)
        at = pl.ds(pl.multiple_of(j * block, block), block)
        xs[j] = jnp.dot(basis_ref[...], sig[at, :], preferred_element_type=f32)
        return carry

    lax.fori_loop(0, blocks, transform, 0)


def enter(scalars, vec, pieces, block):
    n = len(pieces)
    rows, width = pieces[0].shape
    length = rows * n
    blocks = length // block
    return pl.pallas_call(
        partial(enter_kernel, n, blocks, block),
        out_shape=[
            keep((length, width), bf16),
            keep((length, width), bf16),
            keep((blocks, 2 * block, width), f32),
        ],
        in_specs=[sspec()] + [vspec()] * (2 + n),
        out_specs=[vspec()] * 3,
        compiler_params=params(6),
        cost_estimate=cost(7),
        name="enter",
    )(scalars, vec, jnp.asarray(basis(block), bf16), *pieces)


def forward_kernel(n, n_t, blocks, block, sc, vec, b_out, basis_ref, basis_t, tok_all, sig, xs, *refs):
    tap_parts, w_parts = refs[:n_t], refs[n_t : 2 * n_t]
    outs = refs[2 * n_t : 2 * n_t + n]
    spec, w, active, slope, val_a, gate = refs[2 * n_t + n : 2 * n_t + n + 6]
    taps, raw, zs, mix, pre, out = refs[2 * n_t + n + 6 :]
    rank, seq_len, rank_t = sc[0], sc[1], sc[2]
    length, width = tok_all.shape
    channels = width // n_t
    half = block // 2
    scale = 1.0 / block
    for e in range(n_t):
        owner = rank_t ^ e
        at = pl.ds(pl.multiple_of(owner * channels, channels), channels)
        if channels % LANES == 0:
            taps[:, at] = tap_parts[e][...]
        else:
            for t in range(n_t):

                @pl.when(owner == t)
                def _(e=e, t=t):
                    taps[:, t * channels : (t + 1) * channels] = tap_parts[e][...]

        count, _, cols = w_parts[e].shape
        for d in range(count):
            w[at, d * cols : (d + 1) * cols] = w_parts[e][d]

    def spectrum(d, carry):
        at = pl.ds(pl.multiple_of(d * block, block), block)
        raw[d] = jnp.dot(basis_ref[...], taps[at, :], preferred_element_type=f32)
        return carry

    lax.fori_loop(0, blocks, spectrum, 0)

    def product(sign, row, lanes):
        re, im = pl.ds(row, TILE), pl.ds(pl.multiple_of(row + block, TILE), TILE)
        xr = [xs[j, re, lanes] for j in range(blocks)]
        xi = [xs[j, im, lanes] for j in range(blocks)]
        kr, ki = [], []
        for d in range(blocks):
            r, i = raw[d, re, lanes], raw[d, im, lanes]
            if d:
                pr, pi = raw[d - 1, re, lanes], raw[d - 1, im, lanes]
                r, i = (r - pi, i + pr) if sign > 0 else (r + pi, i - pr)
            kr.append(r * scale)
            ki.append(i * scale)
            spec[d, re, lanes] = kr[d].astype(bf16)
            spec[d, im, lanes] = ki[d].astype(bf16)
        for m in range(blocks):
            zr = zi = None
            for j in range(m + 1):
                d = m - j
                pr = xr[j] * kr[d] - xi[j] * ki[d]
                pi = xr[j] * ki[d] + xi[j] * kr[d]
                zr = pr if zr is None else zr + pr
                zi = pi if zi is None else zi + pi
            zs[m, re, lanes] = zr.astype(bf16)
            zs[m, im, lanes] = zi.astype(bf16)

    tiles(0, half, width, partial(product, 1))
    tiles(half, block, width, partial(product, -1))

    def tail(j, carry):
        mix[...] = jnp.dot(basis_t[...], zs[j], preferred_element_type=f32)

        def act(r, carry):
            at = pl.ds(pl.multiple_of(r * ROWS, ROWS), ROWS)
            to = pl.ds(pl.multiple_of(j * block + r * ROWS, ROWS), ROWS)
            v = mix[at, :] + vec[3:4, :] * sig[to, :].astype(f32)
            sq = v * v
            t = jnp.tanh(v * (0.7978845608 + (0.7978845608 * 0.044715) * sq))
            half_t = 0.5 + 0.5 * t
            active[to, :] = (v * half_t).astype(bf16)
            inner = 0.7978845608 + (0.7978845608 * 3.0 * 0.044715) * sq
            slope[to, :] = (half_t + 0.5 * v * (1.0 - t * t) * inner).astype(bf16)
            return carry

        lax.fori_loop(0, block // ROWS, act, 0)
        whole = pl.ds(pl.multiple_of(j * block, block), block)
        pre[...] = jnp.dot(active[whole, :], w[...], preferred_element_type=f32)

        def glu(r, carry):
            at = pl.ds(pl.multiple_of(r * ROWS, ROWS), ROWS)
            start = pl.multiple_of(j * block + r * ROWS, ROWS)
            to = pl.ds(start, ROWS)
            a = pre[at, :width] + b_out[:, :width]
            g = jax.nn.sigmoid(pre[at, width:] + b_out[:, width:])
            place = start + lax.broadcasted_iota(jnp.int32, (ROWS, width), 0)
            add = jnp.where(place < seq_len, a * g, 0.0)
            out[to, :] = (tok_all[to, :].astype(f32) + add).astype(bf16)
            val_a[to, :] = a.astype(bf16)
            gate[to, :] = g.astype(bf16)
            return carry

        lax.fori_loop(0, block // ROWS, glu, 0)
        return carry

    lax.fori_loop(0, blocks, tail, 0)
    rows = length // n
    for s in range(n):
        dst = lax.rem(rank + s, n)
        outs[s][...] = out[pl.ds(pl.multiple_of(dst * rows, rows), rows), :]


def forward(scalars, vec, b_out, entered, tap_parts, w_parts, n, block):
    tok_all, sig, xs = entered
    n_t = len(tap_parts)
    length, width = tok_all.shape
    blocks = length // block
    table = basis(block)
    full = keep((length, width), bf16)
    return pl.pallas_call(
        partial(forward_kernel, n, n_t, blocks, block),
        out_shape=[jax.ShapeDtypeStruct((length // n, width), bf16)] * n
        + [
            keep((blocks, 2 * block, width), bf16),
            keep((width, 2 * width), bf16),
            full,
            full,
            full,
            full,
        ],
        in_specs=[sspec()] + [vspec()] * (7 + 2 * n_t),
        out_specs=[vspec()] * (n + 6),
        scratch_shapes=[
            pltpu.VMEM((length, width), bf16),
            pltpu.VMEM((blocks, 2 * block, width), f32),
            pltpu.VMEM((blocks, 2 * block, width), bf16),
            pltpu.VMEM((block, width), f32),
            pltpu.VMEM((block, 2 * width), f32),
            pltpu.VMEM((length, width), bf16),
        ],
        compiler_params=params(15),
        cost_estimate=cost(15),
        name="forward",
    )(
        scalars,
        vec,
        b_out,
        jnp.asarray(table, bf16),
        jnp.asarray(table.T, bf16),
        *held_in_vmem(tok_all, sig, xs),
        *tap_parts,
        *w_parts,
    )


def mix_back_kernel(n, blocks, block, sc, basis_ref, basis_t, w, xs, slope, val_a, gate, *refs):
    pieces = refs[:n]
    taps_keep, taps_send, grad_pre, grad_mix, spec_g, cot, bias_grad, act_f, comb = refs[n:]
    rank, seq_len, core = sc[0], sc[1], sc[2] & 1
    length, width = cot.shape
    rows = length // n
    for s in range(n):
        src = lax.rem(rank - s + n, n)
        cot[pl.ds(pl.multiple_of(src * rows, rows), rows), :] = pieces[s][...]
    half = block // 2
    bias_grad[...] = jnp.zeros_like(bias_grad)

    def front(j, carry):
        def glu(r, carry):
            start = pl.multiple_of(j * block + r * ROWS, ROWS)
            to = pl.ds(start, ROWS)
            place = start + lax.broadcasted_iota(jnp.int32, (ROWS, width), 0)
            q = jnp.where(place < seq_len, cot[to, :].astype(f32), 0.0)
            a, g = val_a[to, :].astype(f32), gate[to, :].astype(f32)
            qg = q * g
            ga = qg.astype(bf16)
            gb = (qg * a * (1.0 - g)).astype(bf16)
            grad_pre[to, :width] = ga
            grad_pre[to, width:] = gb
            ga, gb = ga.astype(f32), gb.astype(f32)
            bias_grad[:, :width] += jnp.sum(ga.reshape(ROWS // 8, 8, width), axis=0)
            bias_grad[:, width:] += jnp.sum(gb.reshape(ROWS // 8, 8, width), axis=0)
            return carry

        lax.fori_loop(0, block // ROWS, glu, 0)
        whole = pl.ds(pl.multiple_of(j * block, block), block)
        act_f[...] = lax.dot_general(
            grad_pre[whole, :], w[...], (((1,), (1,)), ((), ())), preferred_element_type=f32
        )

        def back(r, carry):
            at = pl.ds(pl.multiple_of(r * ROWS, ROWS), ROWS)
            to = pl.ds(pl.multiple_of(j * block + r * ROWS, ROWS), ROWS)
            grad = act_f[at, :].astype(bf16).astype(f32) * slope[to, :].astype(f32)
            grad_mix[to, :] = grad.astype(bf16)
            return carry

        lax.fori_loop(0, block // ROWS, back, 0)
        spec_g[j] = jnp.dot(basis_ref[...], grad_mix[whole, :], preferred_element_type=f32)
        return carry

    lax.fori_loop(0, blocks, front, 0)

    def correlate(sign, row, lanes):
        re, im = pl.ds(row, TILE), pl.ds(pl.multiple_of(row + block, TILE), TILE)
        xr = [xs[j, re, lanes] for j in range(blocks)]
        xi = [xs[j, im, lanes] for j in range(blocks)]
        gr = [spec_g[j, re, lanes] for j in range(blocks)]
        gi = [spec_g[j, im, lanes] for j in range(blocks)]
        next_r = next_i = None
        for d in reversed(range(blocks)):
            dr = di = None
            for m in range(d, blocks):
                j = m - d
                pr = xr[j] * gr[m] + xi[j] * gi[m]
                pi = xr[j] * gi[m] - xi[j] * gr[m]
                dr = pr if dr is None else dr + pr
                di = pi if di is None else di + pi
            cr, ci = dr, di
            if next_r is not None:
                cr = dr + next_i if sign > 0 else dr - next_i
                ci = di - next_r if sign > 0 else di + next_r
            comb[d, re, lanes] = cr.astype(bf16)
            comb[d, im, lanes] = ci.astype(bf16)
            next_r, next_i = dr, di

    tiles(0, half, width, partial(correlate, 1))
    tiles(half, block, width, partial(correlate, -1))
    groups, _, channels = taps_keep.shape

    def finish(d, carry):
        act_f[...] = jnp.dot(basis_t[...], comb[d], preferred_element_type=f32)
        to = pl.ds(pl.multiple_of(d * block, block), block)
        for t in range(2 * groups):
            part = (act_f[:, t * channels : (t + 1) * channels] * (1.0 / block)).astype(bf16)

            @pl.when(core == t & 1)
            def _(t=t, part=part):
                taps_keep[t >> 1, to, :] = part

            @pl.when(core != t & 1)
            def _(t=t, part=part):
                taps_send[t >> 1, to, :] = part

        return carry

    lax.fori_loop(0, blocks, finish, 0)


def mix_back(scalars, pieces, w, xs, slope, val_a, gate, block, n_t):
    n = len(pieces)
    length, width = slope.shape
    blocks = length // block
    table = basis(block)
    halves = jax.ShapeDtypeStruct((n_t // 2, length, width // n_t), bf16)
    return pl.pallas_call(
        partial(mix_back_kernel, n, blocks, block),
        out_shape=[
            halves,
            halves,
            keep((length, 2 * width), bf16),
            keep((length, width), bf16),
            keep((blocks, 2 * block, width), f32),
            keep((length, width), bf16),
            jax.ShapeDtypeStruct((8, 2 * width), f32),
        ],
        in_specs=[sspec()] + [vspec()] * (7 + n),
        out_specs=[vspec()] * 7,
        scratch_shapes=[
            pltpu.VMEM((block, width), f32),
            pltpu.VMEM((blocks, 2 * block, width), bf16),
        ],
        compiler_params=params(8),
        cost_estimate=cost(13),
        name="mix_back",
    )(
        scalars,
        jnp.asarray(table, bf16),
        jnp.asarray(table.T, bf16),
        *held_in_vmem(w, xs, slope, val_a, gate),
        *pieces,
    )


def weight_back_kernel(n, sc, active, grad_pre, w_keep, w_send):
    core = sc[2] & 1
    groups = w_keep.shape[0]
    _, _, channels, cols = w_keep.shape
    for t in range(2 * groups):
        part = lax.dot_general(
            active[:, t * channels : (t + 1) * channels],
            grad_pre[...],
            (((0,), (0,)), ((), ())),
            preferred_element_type=f32,
        ).astype(bf16)

        @pl.when(core == t & 1)
        def _(t=t, part=part):
            for d in range(n):
                w_keep[t >> 1, d] = part[:, d * cols : (d + 1) * cols]

        @pl.when(core != t & 1)
        def _(t=t, part=part):
            for d in range(n):
                w_send[t >> 1, d] = part[:, d * cols : (d + 1) * cols]


def weight_back(scalars, active, grad_pre, n, n_t):
    width = active.shape[1]
    halves = jax.ShapeDtypeStruct((n_t // 2, n, width // n_t, 2 * width // n), bf16)
    return pl.pallas_call(
        partial(weight_back_kernel, n),
        out_shape=[halves, halves],
        in_specs=[sspec()] + [vspec()] * 2,
        out_specs=[vspec()] * 2,
        compiler_params=params(6),
        cost_estimate=cost(4),
        name="weight_back",
    )(scalars, *held_in_vmem(active, grad_pre))


def norm_back_kernel(n, blocks, block, sc, vec, basis_t, spec, spec_g, grad_mix, tok_all, cot_all, *refs):
    outs = refs[:n]
    gain_grad, bias_grad = refs[n : n + 2]
    comb, sig_f, res = refs[n + 2 :]
    rank = sc[0]
    rows = outs[0].shape[0]
    length, width = tok_all.shape
    gain_grad[...] = jnp.zeros_like(gain_grad)
    bias_grad[...] = jnp.zeros_like(bias_grad)

    def correlate(row, lanes):
        re, im = pl.ds(row, TILE), pl.ds(pl.multiple_of(row + block, TILE), TILE)
        kr = [spec[j, re, lanes].astype(f32) for j in range(blocks)]
        ki = [spec[j, im, lanes].astype(f32) for j in range(blocks)]
        gr = [spec_g[j, re, lanes] for j in range(blocks)]
        gi = [spec_g[j, im, lanes] for j in range(blocks)]
        for j in range(blocks):
            dr = di = None
            for m in range(j, blocks):
                d = m - j
                pr = kr[d] * gr[m] + ki[d] * gi[m]
                pi = kr[d] * gi[m] - ki[d] * gr[m]
                dr = pr if dr is None else dr + pr
                di = pi if di is None else di + pi
            comb[j, re, lanes] = dr.astype(bf16)
            comb[j, im, lanes] = di.astype(bf16)

    tiles(0, block, width, correlate)

    def finish(j, carry):
        sig_f[...] = jnp.dot(basis_t[...], comb[j], preferred_element_type=f32)

        def norm(r, carry):
            at = pl.ds(pl.multiple_of(r * ROWS, ROWS), ROWS)
            to = pl.ds(pl.multiple_of(j * block + r * ROWS, ROWS), ROWS)
            grad = sig_f[at, :] + vec[3:4, :] * grad_mix[to, :].astype(f32)
            grad = grad.astype(bf16).astype(f32)
            xhat, scale = normalize(tok_all[to, :].astype(f32))
            gx = grad * xhat
            gain_grad[...] += jnp.sum(gx.reshape(ROWS // 8, 8, width), axis=0)
            bias_grad[...] += jnp.sum(grad.reshape(ROWS // 8, 8, width), axis=0)
            g = grad * vec[0:1, :]
            mean_g = jnp.sum(g, axis=-1, keepdims=True) * (1.0 / width)
            mean_gx = jnp.sum(g * xhat, axis=-1, keepdims=True) * (1.0 / width)
            out = cot_all[to, :].astype(f32) + (g - mean_g - xhat * mean_gx) * scale
            res[to, :] = out.astype(bf16)
            return carry

        lax.fori_loop(0, block // ROWS, norm, 0)
        return carry

    lax.fori_loop(0, blocks, finish, 0)
    for s in range(n):
        dst = lax.rem(rank + s, n)
        outs[s][...] = res[pl.ds(pl.multiple_of(dst * rows, rows), rows), :]


def norm_back(scalars, vec, spec, spec_g, grad_mix, tok_all, cot_all, n, block):
    length, width = tok_all.shape
    blocks = length // block
    rows = length // n
    res = pl.pallas_call(
        partial(norm_back_kernel, n, blocks, block),
        out_shape=[jax.ShapeDtypeStruct((rows, width), bf16)] * n
        + [jax.ShapeDtypeStruct((8, width), f32)] * 2,
        in_specs=[sspec()] + [vspec()] * 7,
        out_specs=[vspec()] * (n + 2),
        scratch_shapes=[
            pltpu.VMEM((blocks, 2 * block, width), bf16),
            pltpu.VMEM((block, width), f32),
            pltpu.VMEM((length, width), bf16),
        ],
        compiler_params=params(8),
        cost_estimate=cost(12),
        name="norm_back",
    )(
        scalars,
        vec,
        jnp.asarray(basis(block).T, bf16),
        *held_in_vmem(spec, spec_g, grad_mix, tok_all, cot_all),
    )
    return res[:n], res[n], res[n + 1]


def halve_kernel(shift, sc, kept, got, keep_out, send_out):
    here = (sc[2] >> shift) & 1
    for i in range(keep_out.shape[0]):
        for k in range(2):
            value = (kept[2 * i + k].astype(f32) + got[2 * i + k].astype(f32)).astype(bf16)

            @pl.when(here == k)
            def _(i=i, value=value):
                keep_out[i] = value

            @pl.when(here != k)
            def _(i=i, value=value):
                send_out[i] = value


def halve(scalars, kept, got, shift):
    shape = jax.ShapeDtypeStruct((kept.shape[0] // 2, *kept.shape[1:]), bf16)
    return pl.pallas_call(
        partial(halve_kernel, shift),
        out_shape=[shape, shape],
        in_specs=[sspec(), vspec(), vspec()],
        out_specs=[vspec()] * 2,
        compiler_params=params(5),
        cost_estimate=cost(1),
        name="halve",
    )(scalars, kept, got)


def weave_kernel(n, sc, *refs):
    pieces, out, held = refs[:n], refs[n], refs[n + 1]
    rank = sc[0]
    rows, width = pieces[0].shape
    step = min(rows, 32)

    def part(r, carry):
        at = pl.ds(pl.multiple_of(r * step, step), step)
        for s in range(n):
            src = lax.rem(rank - s + n, n)
            for c in range(width // LANES):
                lanes = slice(c * LANES, (c + 1) * LANES)
                held[c, pl.ds(src, step, stride=n), :] = pieces[s][at, lanes].astype(f32)
        for c in range(width // LANES):
            lanes = slice(c * LANES, (c + 1) * LANES)
            out[at, :, lanes] = held[c].reshape(step, n, LANES).astype(bf16)
        return carry

    lax.fori_loop(0, rows // step, part, 0)


def weave(scalars, pieces):
    n = len(pieces)
    rows, width = pieces[0].shape
    return pl.pallas_call(
        partial(weave_kernel, n),
        out_shape=jax.ShapeDtypeStruct((rows, n, width), bf16),
        in_specs=[sspec()] + [vspec()] * n,
        out_specs=vspec(),
        scratch_shapes=[pltpu.VMEM((width // LANES, min(rows, 32) * n, LANES), f32)],
        compiler_params=params(8),
        cost_estimate=cost(3),
        name="weave",
    )(scalars, *pieces)


def part_kernel(n, sc, whole, *refs):
    outs, held = refs[:n], refs[n]
    rank = sc[0]
    rows, _, width = whole.shape
    step = min(rows, 32)

    def part(r, carry):
        at = pl.ds(pl.multiple_of(r * step, step), step)
        for c in range(width // LANES):
            lanes = slice(c * LANES, (c + 1) * LANES)
            held[c] = whole[at, :, lanes].astype(f32).reshape(step * n, LANES)
        for s in range(n):
            dst = lax.rem(rank + s, n)
            for c in range(width // LANES):
                lanes = slice(c * LANES, (c + 1) * LANES)
                outs[s][at, lanes] = held[c, pl.ds(dst, step, stride=n), :].astype(bf16)
        return carry

    lax.fori_loop(0, rows // step, part, 0)


def part(scalars, whole):
    rows, n, width = whole.shape
    return pl.pallas_call(
        partial(part_kernel, n),
        out_shape=[jax.ShapeDtypeStruct((rows, width), bf16)] * n,
        in_specs=[sspec(), vspec()],
        out_specs=[vspec()] * n,
        scratch_shapes=[pltpu.VMEM((width // LANES, min(rows, 32) * n, LANES), f32)],
        compiler_params=params(8),
        cost_estimate=cost(3),
        name="part",
    )(scalars, whole)


def total_kernel(states, msg, w_out, g0, g1, g2, g3, vec_out):
    channels, cols = w_out.shape
    total = msg[0].astype(f32)
    for d in range(1, msg.shape[0]):
        total = total + msg[d].astype(f32)
    w_out[...] = total[:channels, :cols]
    for k, ref in enumerate((g0, g1, g2, g3)):
        ref[...] = total[channels + k * states : channels + (k + 1) * states, :channels].T
    top = channels + 4 * states
    vec_out[...] = total[top : top + vec_out.shape[0], :]


def totals(msg, channels, cols, states, lines):
    grad = jax.ShapeDtypeStruct((channels, states), f32)
    return pl.pallas_call(
        partial(total_kernel, states),
        out_shape=[jax.ShapeDtypeStruct((channels, cols), f32)]
        + [grad] * 4
        + [jax.ShapeDtypeStruct((6 * lines, WIDE), f32)],
        in_specs=[vspec()],
        out_specs=[vspec()] * 6,
        compiler_params=params(4),
        cost_estimate=cost(1),
        name="totals",
    )(msg)


def shares_kernel(lines, sc, *refs):
    count = len(refs) - 5
    outs = refs[count:]
    rank = sc[0]
    total = refs[0][...]
    for ref in refs[1:count]:
        total = total + ref[...]
    for k, out in enumerate(outs):
        per = out.shape[1]
        slots = (2 * lines if k == 4 else lines) * WIDE // per
        value = jnp.zeros((1, per), f32)
        for slot in range(slots):
            line, lane = divmod(slot * per, WIDE)
            here = total[k * lines + line : k * lines + line + 1, lane : lane + per]
            value = jnp.where(rank == slot, here, value)
        out[...] = value


def shares(scalars, vectors, per, lines):
    one = jax.ShapeDtypeStruct((1, per), f32)
    return pl.pallas_call(
        partial(shares_kernel, lines),
        out_shape=[one] * 4 + [jax.ShapeDtypeStruct((1, 2 * per), f32)],
        in_specs=[sspec()] + [vspec()] * len(vectors),
        out_specs=[vspec()] * 5,
        compiler_params=params(4),
        cost_estimate=cost(1),
        name="shares",
    )(scalars, *vectors)


def local(n_dp, n_t, tokens, cotangent, lengths, ln_gain, ln_bias, lam_log, lam_im, w_re, w_im, log_dt, skip_gain, w_out, b_out):
    rows, seqs, width = tokens.shape
    assert seqs == n_dp
    length = rows * n_dp
    block = min(256, length)
    rank = lax.axis_index("dp")
    rank_t = lax.axis_index("tensor")
    channels, states = lam_log.shape
    cols = w_out.shape[1]
    per = width // n_dp
    bits = [1 << k for k in range(n_t.bit_length() - 1)]
    seq_len = lax.dynamic_index_in_dim(lengths, rank_t * n_dp + rank, 0, keepdims=False)
    scalars = jnp.stack([rank, seq_len, rank_t]).astype(jnp.int32)

    vec = jnp.concatenate([ln_gain, ln_bias, log_dt, skip_gain, b_out])
    vec_rows = VEC_ROWS(per)
    vec = jnp.pad(vec, (0, vec_rows * WIDE - vec.shape[0])).reshape(vec_rows, WIDE)
    par = jnp.concatenate([lam_log.T, lam_im.T, w_re.T, w_im.T], axis=0)
    par = jnp.pad(par, ((0, 0), (0, WIDE - channels)))
    blob = pack_weights(n_dp, par, vec, jnp.pad(w_out, ((0, 0), (0, WIDE - cols))))
    blob = lax.all_to_all(blob, "dp", 0, 0, tiled=True)

    after = lambda value, *others: lax.optimization_barrier((value, others))[0]
    tok_pieces = shift_exchange(part(scalars, tokens), "dp", n_dp)
    cot_pieces = list(part(scalars, cotangent))
    depth = 5
    for s in range(1, min(depth + 1, n_dp)):
        cot_pieces[s] = after(cot_pieces[s], tok_pieces[min(s + 2, n_dp - 1)])
    blob = after(blob, tok_pieces[1])

    taps, w_own, par_all, vec, b_full = make_taps(
        scalars, blob, states, length, width, channels, cols
    )

    def spread(own):
        parts = {0: own}
        for bit in reversed(bits):
            for e in list(parts):
                parts[e | bit] = flip_bit(parts[e], "tensor", n_t, bit)
        return [parts[e] for e in range(n_t)]

    tap_parts = spread(taps)
    w_parts = spread(w_own)

    entered = enter(scalars, vec, tok_pieces, block)
    tok_all, sig, xs = entered
    for s in range(depth + 1, n_dp):
        cot_pieces[s] = after(cot_pieces[s], sig)
    cot_pieces = shift_exchange(cot_pieces, "dp", n_dp)
    first = cot_pieces[1 : min(3, n_dp)]
    res = forward(scalars, after(vec, first), b_full, entered, tap_parts, w_parts, n_dp, block)
    out_back = shift_exchange(list(res[:n_dp]), "dp", n_dp)
    spec, w_full, active, slope, val_a, gate = res[n_dp:]
    taps_keep, taps_send, grad_pre, grad_mix, spec_g, cot, out8 = mix_back(
        scalars, cot_pieces, w_full, xs, slope, val_a, gate, block, n_t
    )
    active = after(active, out_back[1:4])
    spec_g = after(spec_g, out_back[4 : depth + 1])
    w_keep, w_send = weight_back(scalars, active, grad_pre, n_dp, n_t)

    def reduce_groups(kept, sent):
        got = flip_bit(sent, "tensor", n_t, 1)
        for k, bit in enumerate(bits[1:]):
            kept, sent = halve(scalars, kept, got, k + 1)
            got = flip_bit(sent, "tensor", n_t, bit)
        return kept[0], got[0]

    taps_two = reduce_groups(taps_keep, taps_send)
    grad_pieces, gain8, bias8 = norm_back(
        scalars, vec, spec, spec_g, grad_mix, tok_all, cot, n_dp, block
    )
    grad_back = shift_exchange(grad_pieces, "dp", n_dp)
    out8 = after(out8, out_back[depth + 1 :])
    w_two = reduce_groups(w_keep, w_send)
    msg = taps_back(scalars, par_all, vec, taps_two, w_two, gain8, bias8, out8, n_dp, states)
    msg = after(msg, grad_back[1 : depth + 1])
    msg = lax.all_to_all(msg, "dp", 0, 0, tiled=True)
    lines = width // WIDE
    grad_w_out, g_lam_log, g_lam_im, g_w_re, g_w_im, vec_sum = totals(
        msg, channels, cols, states, lines
    )
    others = [
        lax.ppermute(vec_sum, "tensor", [(k, k ^ e) for k in range(n_t)]) for e in range(1, n_t)
    ]
    g_gain, g_bias, g_dt, g_skip, g_b = (
        v.reshape(-1) for v in shares(scalars, [vec_sum, *others], per, lines)
    )

    out = weave(scalars, out_back)
    grad_tokens = weave(scalars, grad_back)
    return (
        out,
        grad_tokens,
        g_gain,
        g_bias,
        g_lam_log,
        g_lam_im,
        g_w_re,
        g_w_im,
        g_dt,
        g_skip,
        grad_w_out,
        g_b,
    )


def solution(mesh):
    big = P("dp", "tensor", None)
    grid = P("tensor", "dp")
    line = P("dp")
    return jax.shard_map(
        partial(local, mesh.shape["dp"], mesh.shape["tensor"]),
        mesh=mesh,
        in_specs=(big, big, P(), line, line, grid, grid, grid, grid, line, line, grid, line),
        out_specs=(big, big, line, line, grid, grid, grid, grid, line, line, grid, line),
        check_vma=False,
    )
```

```python
from functools import partial

import jax
import jax.numpy as jnp
import ml_dtypes
import numpy as np
from jax import lax
from jax.experimental import pallas as pl
from jax.experimental.pallas import tpu as pltpu
from jax.sharding import PartitionSpec as P

epsilon = 1e-05
f32 = jnp.float32
bf16 = jnp.bfloat16


def params(mib):
    return pltpu.CompilerParams(vmem_limit_bytes=mib * 1024 * 1024)


def cost(us):
    return pl.CostEstimate(flops=0, bytes_accessed=int(us * 1e4), transcendentals=0)


def keep(shape, dtype):
    return pltpu.VMEM(shape, dtype)


def held_in_vmem(*arrays):
    return [pltpu.with_memory_space_constraint(a, pltpu.VMEM) for a in arrays]


def hbm(shape, dtype):
    return pltpu.HBM(shape, dtype)


def hspec():
    return pl.BlockSpec(memory_space=pltpu.HBM)


def copies(sems, index, block, j, pairs):
    at = pl.ds(pl.multiple_of(j * block, block), block)
    return [
        pltpu.make_async_copy(src.at[at], dst.at[at], sems.at[index + k, j])
        for k, (src, dst) in enumerate(pairs)
    ]


def gather_rows(rank, pieces, whole, sems):
    n = len(pieces)
    if n == 1:
        return [pltpu.make_async_copy(pieces[0], whole, sems.at[0])]
    rows = whole.shape[0] // n
    moves = []
    for s, piece in enumerate(pieces):
        to = pl.ds(pl.multiple_of(lax.rem(rank - s + n, n) * rows, rows), rows)
        moves.append(pltpu.make_async_copy(piece.at[pl.ds(0, rows)], whole.at[to], sems.at[s]))
    return moves


def held_in_hbm(*arrays):
    return [pltpu.with_memory_space_constraint(a, pltpu.HBM) for a in arrays]


def vspec():
    return pl.BlockSpec(memory_space=pltpu.VMEM)


def sspec():
    return pl.BlockSpec(memory_space=pltpu.SMEM)


def basis(block):
    freq = np.concatenate([np.arange(0, block, 2), np.arange(1, block, 2)])
    angle = np.pi * (2 * freq[:, None] + 1) * np.arange(block)[None, :] / (2 * block)
    forward = np.concatenate([np.cos(angle), -np.sin(angle)], axis=0)
    return forward.astype(np.float32)


def two_parts(value):
    high = value.astype(ml_dtypes.bfloat16)
    low = (value - high.astype(np.float32)).astype(ml_dtypes.bfloat16)
    return jnp.asarray(high), jnp.asarray(low)


def shift_exchange(pieces, axis, size):
    out = [pieces[0]]
    for s in range(1, size):
        out.append(lax.ppermute(pieces[s], axis, [(k, (k + s) % size) for k in range(size)]))
    return out


def flip_bit(value, axis, size, bit):
    return lax.ppermute(value, axis, [(k, k ^ bit) for k in range(size)])


WIDE = 128


def pad_to(value, multiple):
    return -(-value // multiple) * multiple


def planes(value):
    parts = []
    for _ in range(3):
        part = value.astype(bf16)
        parts.append(part)
        value = value - part.astype(f32)
    return parts


def split_kernel(rows_f, *refs):
    parts, vecs, w_ref, out, held = refs[:4], refs[4:9], refs[9], refs[10], refs[11]
    states, channels = parts[0].shape
    held[...] = jnp.zeros_like(held)
    for k, ref in enumerate(parts):
        held[k * states : (k + 1) * states, :channels] = ref[...]
    flat = 0
    for ref in vecs:
        row, lane = divmod(flat, WIDE)
        size = ref.shape[1]
        held[4 * states + row : 4 * states + row + 1, lane : lane + size] = ref[...]
        flat += size
    for p, plane in enumerate(planes(held[...])):
        out[0, p * rows_f : (p + 1) * rows_f, :] = plane
    if w_ref.shape[1] < WIDE:
        out[0, 3 * rows_f :, :] = jnp.zeros((w_ref.shape[0], WIDE), bf16)
    out[0, 3 * rows_f :, : w_ref.shape[1]] = w_ref[...]


def float_rows(states, vec_rows):
    return pad_to(4 * states + vec_rows, 8)


def pack(parts, vecs, w):
    vecs = [v.reshape(1, -1) for v in vecs]
    rows_f = float_rows(parts[0].shape[0], -(-sum(v.shape[1] for v in vecs) // WIDE))
    return pl.pallas_call(
        partial(split_kernel, rows_f),
        out_shape=jax.ShapeDtypeStruct((1, 3 * rows_f + w.shape[0], WIDE), bf16),
        in_specs=[vspec()] * 10,
        out_specs=vspec(),
        scratch_shapes=[pltpu.VMEM((rows_f, WIDE), f32)],
        compiler_params=params(4),
        name="pack",
    )(*held_in_hbm(*parts, *vecs, w))


def merge_kernel(which, shift, sc, own, got, out):
    here = (sc[which] >> shift) & 1
    for i in range(own.shape[0]):
        out[2 * i + here] = own[i]
        out[2 * i + 1 - here] = got[i]


def merge(scalars, own, got, which, shift):
    return pl.pallas_call(
        partial(merge_kernel, which, shift),
        out_shape=jax.ShapeDtypeStruct((2 * own.shape[0], *own.shape[1:]), own.dtype),
        in_specs=[sspec(), vspec(), vspec()],
        out_specs=vspec(),
        compiler_params=params(4),
        cost_estimate=cost(1),
        name="merge",
    )(scalars, own, got)


def collect_kernel(blob, out):
    for d in range(out.shape[0]):
        out[d] = blob[d, :, : out.shape[2]]


def collect(blob, channels, cols):
    n, rows, _ = blob.shape
    if (rows - channels) % channels:
        return blob[:, rows - channels :, :cols]
    return pl.pallas_call(
        collect_kernel,
        out_shape=jax.ShapeDtypeStruct((n, channels, cols), bf16),
        grid=(1,),
        in_specs=[pl.BlockSpec((n, channels, WIDE), lambda i: (0, rows // channels - 1, 0))],
        out_specs=pl.BlockSpec((n, channels, cols), lambda i: (0, 0, 0)),
        compiler_params=params(4),
        cost_estimate=cost(1),
        name="collect",
    )(blob)


INNER = 32


def powers(table_r, table_i, zr, zi, count):
    cr, ci = jnp.ones_like(zr), jnp.zeros_like(zi)
    for b in range(count):
        table_r[b] = cr
        table_i[b] = ci
        if b + 1 < count:
            cr, ci = cr * zr - ci * zi, cr * zi + ci * zr


def taps_kernel(n, states, channels, sc, blob, out, par_out, vec_out, b_out, table_r, table_i, part, held):
    rank_t = sc[1]
    per = vec_out.shape[1] // n
    rows_f = float_rows(states, VEC_ROWS(per))
    plane = [blob[:, k * rows_f : (k + 1) * rows_f, :].astype(f32) for k in range(3)]
    held[...] = plane[0] + plane[1] + plane[2]
    for d in range(n):
        for k in range(4):
            par_out[k, d * states : (d + 1) * states, :] = held[d, k * states : (k + 1) * states, :channels]
        top = 4 * states
        for k in range(4):
            row, lane = divmod(k * per, WIDE)
            vec_out[k : k + 1, d * per : (d + 1) * per] = held[d, top + row : top + row + 1, lane : lane + per]
        row, lane = divmod(4 * per, WIDE)
        b_out[:, 2 * d * per : 2 * (d + 1) * per] = held[d, top + row : top + row + 1, lane : lane + 2 * per]
    log_step = vec_out[2:3, 0:channels]
    for t in range(1, vec_out.shape[1] // channels):
        log_step = jnp.where(rank_t == t, vec_out[2:3, t * channels : (t + 1) * channels], log_step)
    vec_out[4:5, 0:channels] = log_step
    step = jnp.exp(log_step)
    decay = jnp.exp(par_out[0]) * step
    turn = par_out[1] * step
    size = jnp.exp(-decay)
    powers(table_r, table_i, size * jnp.cos(turn), size * jnp.sin(turn), INNER)
    far = jnp.exp(-INNER * decay)
    far_r, far_i = far * jnp.cos(INNER * turn), far * jnp.sin(INNER * turn)
    total = decay.shape[0]

    def block(a, carry):
        ar, ai = carry
        for b in range(INNER):
            value = ar * table_r[b] - ai * table_i[b]
            part[b * 8 : (b + 1) * 8, :] = jnp.sum(value.reshape(total // 8, 8, channels), axis=0)
        summed = part[pl.ds(0, INNER, stride=8), :]
        for q in range(1, 8):
            summed = summed + part[pl.ds(q, INNER, stride=8), :]
        out[pl.ds(pl.multiple_of(a * INNER, INNER), INNER), :] = summed.astype(bf16)
        return ar * far_r - ai * far_i, ar * far_i + ai * far_r

    lax.fori_loop(0, out.shape[0] // INNER, block, (par_out[2] * step, par_out[3] * step))


def VEC_ROWS(per):
    return -(-6 * per // WIDE)


def make_taps(scalars, blob, states, length, width, channels):
    n = blob.shape[0]
    total = n * states
    return pl.pallas_call(
        partial(taps_kernel, n, states, channels),
        out_shape=[
            jax.ShapeDtypeStruct((length, channels), bf16),
            jax.ShapeDtypeStruct((4, total, channels), f32),
            jax.ShapeDtypeStruct((8, width), f32),
            jax.ShapeDtypeStruct((1, 2 * width), f32),
        ],
        in_specs=[sspec(), vspec()],
        out_specs=[vspec()] * 4,
        scratch_shapes=[
            pltpu.VMEM((INNER, total, channels), f32),
            pltpu.VMEM((INNER, total, channels), f32),
            pltpu.VMEM((INNER * 8, channels), f32),
            pltpu.VMEM((n, float_rows(states, VEC_ROWS(width // n)), WIDE), f32),
        ],
        compiler_params=params(8),
        cost_estimate=cost(7),
        name="taps",
    )(scalars, blob)


def taps_back_kernel(
    n, states, sc, par, vec, grad_a, grad_b, gain8, bias8, out8, keep_out, send_out, vec_sum, table_r, table_i, summed, held, msg
):
    rank_t = sc[1]
    length, channels = summed.shape
    width = vec.shape[1]
    rate = jnp.exp(par[0])
    step = jnp.exp(vec[4:5, 0:channels])
    decay = rate * step
    turn = par[1] * step
    w_re, w_im = par[2], par[3]
    size = jnp.exp(-decay)
    powers(table_r, table_i, size * jnp.cos(turn), size * jnp.sin(turn), INNER)
    far = jnp.exp(-INNER * decay)
    far_r, far_i = far * jnp.cos(INNER * turn), far * jnp.sin(INNER * turn)
    total = decay.shape[0]
    summed[...] = grad_a[:length, :].astype(f32) + grad_b[:length, :].astype(f32)
    zero = jnp.zeros((total, channels), f32)

    def block(k, carry):
        a = length // INNER - 1 - k
        s0r, s0i, s1r, s1i = [held[q] for q in range(4)]
        s1r, s1i = s1r + INNER * s0r, s1i + INNER * s0i
        s0r, s0i = s0r * far_r - s0i * far_i, s0r * far_i + s0i * far_r
        s1r, s1i = s1r * far_r - s1i * far_i, s1r * far_i + s1i * far_r
        for q, value in enumerate((s0r, s0i, s1r, s1i)):
            held[q] = value
        rows = summed[pl.ds(pl.multiple_of(a * INNER, INNER), INNER), :]
        group = min(32, total)
        for c in range(total // group):
            here = slice(c * group, (c + 1) * group)
            u0r, u0i, u1r, u1i = [held[q, here, :] for q in range(4)]
            tail_r = tail_i = jnp.zeros((group, channels), f32)
            for b in reversed(range(INNER)):
                g = jnp.broadcast_to(rows[b : b + 1, :], (group, channels))
                if b:
                    tail_r, tail_i = tail_r + g * table_r[b, here, :], tail_i + g * table_i[b, here, :]
                    u1r, u1i = u1r + tail_r, u1i + tail_i
                else:
                    tail_r = tail_r + g
            u0r, u0i = u0r + tail_r, u0i + tail_i
            for q, value in enumerate((u0r, u0i, u1r, u1i)):
                held[q, here, :] = value
        return carry

    for q in range(4):
        held[q] = zero
    lax.fori_loop(0, length // INNER, block, 0)
    s0r, s0i, s1r, s1i = [held[q] for q in range(4)]
    wr0 = w_re * s0r - w_im * s0i
    wr1 = w_re * s1r - w_im * s1i
    wi1 = w_re * s1i + w_im * s1r
    dt = jnp.sum(step * (wr0 - decay * wr1 - turn * wi1), axis=0, keepdims=True)
    held[0], held[1] = -step * decay * wr1, -step * step * wi1
    held[2], held[3] = step * s0r, -step * s0i
    rows_w = channels
    lines = width // WIDE
    msg[...] = jnp.zeros_like(msg)
    for d in range(n):
        for k in range(4):
            msg[d, rows_w + k * states : rows_w + (k + 1) * states, :channels] = held[
                k, d * states : (d + 1) * states, :
            ].astype(bf16)
    gain_sum, bias_sum, out_sum = gain8[0:1, :], bias8[0:1, :], out8[0:1, :]
    copies = WIDE // channels
    lane = lax.broadcasted_iota(jnp.int32, (1, WIDE), 1) // channels
    skip_row = jnp.concatenate([summed[0:1, :]] * copies, axis=1) if copies > 1 else summed[0:1, :]
    dt_row = jnp.concatenate([dt] * copies, axis=1) if copies > 1 else dt
    for line in range(lines):
        at = slice(line * WIDE, (line + 1) * WIDE)
        mine = lane + line * copies == rank_t
        rows = [
            gain_sum[:, at],
            bias_sum[:, at],
            jnp.where(mine, dt_row, 0.0),
            jnp.where(mine, skip_row, 0.0),
            out_sum[:, at],
            out_sum[:, width + line * WIDE : width + (line + 1) * WIDE],
        ]
        for k, row in enumerate(rows):
            vec_sum[k * lines + line : k * lines + line + 1, :] = row
    here = sc[0] & 1
    for i in range(n // 2):
        keep_out[i] = msg[2 * i + here]
        send_out[i] = msg[2 * i + 1 - here]


def taps_back(scalars, par, vec, grads, gain8, bias8, out8, length, n, states):
    channels = grads[0].shape[1]
    width = vec.shape[1]
    total = par.shape[1]
    rows = pad_to(channels + 4 * states, 16)
    return pl.pallas_call(
        partial(taps_back_kernel, n, states),
        out_shape=[jax.ShapeDtypeStruct((n // 2, rows, WIDE), bf16)] * 2
        + [jax.ShapeDtypeStruct((6 * (width // WIDE), WIDE), f32)],
        in_specs=[sspec()] + [vspec()] * 7,
        out_specs=[vspec()] * 3,
        scratch_shapes=[
            pltpu.VMEM((INNER, total, channels), f32),
            pltpu.VMEM((INNER, total, channels), f32),
            pltpu.VMEM((length, channels), f32),
            pltpu.VMEM((4, total, channels), f32),
            pltpu.VMEM((n, rows, WIDE), bf16),
        ],
        compiler_params=params(10),
        cost_estimate=cost(10),
        name="taps_back",
    )(scalars, par, vec, *grads, gain8, bias8, out8)


ROWS = 32
TILE = 16
LANES = 128


def chunks(block, width):
    step = min(64, block)
    for r in range(block // step):
        for c in range(width // LANES):
            yield slice(r * step, (r + 1) * step), slice(c * LANES, (c + 1) * LANES)


def row_sums(x):
    ones = jnp.ones((x.shape[1], LANES), bf16)
    return jnp.dot(x, ones, preferred_element_type=f32)


def column_sums(x):
    ones = jnp.ones((8, x.shape[0]), bf16)
    return jnp.dot(ones, x, preferred_element_type=f32)


def shifted(rows, base):
    size = rows.stop - rows.start
    return pl.ds(pl.multiple_of(base + rows.start, size), size)


def tiles(first, last, width, body):
    def step(r, carry):
        row = pl.multiple_of(r * TILE, TILE)
        for c in range(width // LANES):
            body(row, slice(c * LANES, (c + 1) * LANES))
        return carry

    lax.fori_loop(first // TILE, last // TILE, step, 0)


def enter_kernel(n, blocks, block, sc, vec, basis_ref, basis_low, *refs):
    pieces = refs[:n]
    tok_all, sig, xs, sig_out, xhat_out, scale_out = refs[n : n + 6]
    xhat, scale, mean, square, sems, sem_in = refs[n + 6 :]
    length, width = tok_all.shape
    moves = gather_rows(sc[0], pieces, tok_all, sem_in)
    for move in moves:
        move.start()
    for move in moves:
        move.wait()
    saves = [(sig, sig_out), (xhat, xhat_out), (scale, scale_out)]

    def transform(j, carry):
        base = j * block
        at = pl.ds(pl.multiple_of(base, block), block)
        mean[...] = row_sums(tok_all[at, :]) * (1.0 / width)
        for r, c in chunks(block, width):
            centred = tok_all[shifted(r, base), c].astype(f32) - mean[r, :]
            square[r, c] = (centred * centred).astype(bf16)
        scale[at, :] = lax.rsqrt(row_sums(square[...]) * (1.0 / width) + epsilon)
        for r, c in chunks(block, width):
            to = shifted(r, base)
            value = (tok_all[to, c].astype(f32) - mean[r, :]) * scale[to, :]
            xhat[to, c] = value.astype(bf16)
            sig[to, c] = (value * vec[0:1, c] + vec[1:2, c]).astype(bf16)
        for copy in copies(sems, 0, block, j, saves):
            copy.start()
        value = sig[at, :]
        xs[j] = jnp.dot(basis_ref[...], value, preferred_element_type=f32)
        xs[j] += jnp.dot(basis_low[...], value, preferred_element_type=f32)
        return carry

    lax.fori_loop(0, blocks, transform, 0)
    for j in range(blocks):
        for copy in copies(sems, 0, block, j, saves):
            copy.wait()


def enter(scalars, vec, pieces, length, block):
    n = len(pieces)
    width = pieces[0].shape[1]
    blocks = length // block
    return pl.pallas_call(
        partial(enter_kernel, n, blocks, block),
        out_shape=[
            keep((length, width), bf16),
            keep((length, width), bf16),
            keep((blocks, 2 * block, width), f32),
            hbm((length, width), bf16),
            hbm((length, width), bf16),
            hbm((length, LANES), f32),
        ],
        in_specs=[sspec()] + [vspec()] * 3 + [hspec()] * n,
        out_specs=[vspec()] * 3 + [hspec()] * 3,
        scratch_shapes=[
            pltpu.VMEM((length, width), bf16),
            pltpu.VMEM((length, LANES), f32),
            pltpu.VMEM((block, LANES), f32),
            pltpu.VMEM((block, width), bf16),
            pltpu.SemaphoreType.DMA((3, blocks)),
            pltpu.SemaphoreType.DMA((n,)),
        ],
        compiler_params=params(8),
        cost_estimate=cost(7),
        name="enter",
    )(scalars, vec, *two_parts(basis(block)), *pieces)


def forward_kernel(n, n_t, blocks, block, sc, lengths, vec, b_out, basis_ref, basis_low, basis_t, basis_t_low, tok_all, sig, xs, *refs):
    tap_parts, w_parts = refs[:n_t], refs[n_t : 2 * n_t]
    out_h, spec_h, w_h, active_h, slope_h, val_h, gate_h = refs[2 * n_t : 2 * n_t + 7]
    taps, raw, zs, zs_low, mix, pre, spec, w, out, active, slope, val_a, gate, sems, sem_w = refs[2 * n_t + 7 :]
    rank_t = sc[1]
    seq_len = lengths[rank_t * n + sc[0]]
    results = [(out, out_h), (active, active_h), (slope, slope_h), (val_a, val_h), (gate, gate_h)]
    length, width = tok_all.shape
    channels = width // n_t
    half = block // 2
    scale = 1.0 / block
    for e in range(n_t):
        owner = rank_t ^ e
        at = pl.ds(pl.multiple_of(owner * channels, channels), channels)
        if channels % LANES == 0:
            taps[:, at] = tap_parts[e][...]
        else:
            for t in range(n_t):

                @pl.when(owner == t)
                def _(e=e, t=t):
                    taps[:, t * channels : (t + 1) * channels] = tap_parts[e][...]

        count, _, cols = w_parts[e].shape
        for d in range(count):
            w[at, d * cols : (d + 1) * cols] = w_parts[e][d]
    copy_w = pltpu.make_async_copy(w, w_h, sem_w.at[0])
    copy_w.start()

    def spectrum(d, carry):
        at = pl.ds(pl.multiple_of(d * block, block), block)
        value = taps[at, :]
        raw[d] = jnp.dot(basis_ref[...], value, preferred_element_type=f32)
        raw[d] += jnp.dot(basis_low[...], value, preferred_element_type=f32)
        return carry

    lax.fori_loop(0, blocks, spectrum, 0)

    def product(sign, row, lanes):
        re, im = pl.ds(row, TILE), pl.ds(pl.multiple_of(row + block, TILE), TILE)
        xr = [xs[j, re, lanes] for j in range(blocks)]
        xi = [xs[j, im, lanes] for j in range(blocks)]
        kr, ki = [], []
        for d in range(blocks):
            r, i = raw[d, re, lanes], raw[d, im, lanes]
            if d:
                pr, pi = raw[d - 1, re, lanes], raw[d - 1, im, lanes]
                r, i = (r - pi, i + pr) if sign > 0 else (r + pi, i - pr)
            kr.append(r * scale)
            ki.append(i * scale)
            spec[d, re, lanes] = kr[d].astype(bf16)
            spec[d, im, lanes] = ki[d].astype(bf16)
        for m in range(blocks):
            zr = zi = None
            for j in range(m + 1):
                d = m - j
                pr = xr[j] * kr[d] - xi[j] * ki[d]
                pi = xr[j] * ki[d] + xi[j] * kr[d]
                zr = pr if zr is None else zr + pr
                zi = pi if zi is None else zi + pi
            for at, value in ((re, zr), (im, zi)):
                high = value.astype(bf16)
                zs[m, at, lanes] = high
                zs_low[m, at, lanes] = (value - high.astype(f32)).astype(bf16)

    tiles(0, half, width, partial(product, 1))
    tiles(half, block, width, partial(product, -1))
    copy_spec = pltpu.make_async_copy(spec, spec_h, sem_w.at[1])
    copy_spec.start()

    def tail(j, carry):
        mix[...] = jnp.dot(basis_t[...], zs[j], preferred_element_type=f32)
        mix[...] += jnp.dot(basis_t_low[...], zs[j], preferred_element_type=f32)
        mix[...] += jnp.dot(basis_t[...], zs_low[j], preferred_element_type=f32)

        base = j * block
        for r, c in chunks(block, width):
            to = shifted(r, base)
            v = mix[r, c] + vec[3:4, c] * sig[to, c].astype(f32)
            sq = v * v
            t = jnp.tanh(v * (0.7978845608 + (0.7978845608 * 0.044715) * sq))
            half_t = 0.5 + 0.5 * t
            active[to, c] = (v * half_t).astype(bf16)
            inner = 0.7978845608 * 0.5 + (0.7978845608 * 1.5 * 0.044715) * sq
            slope[to, c] = (half_t + v * (1.0 - t * t) * inner).astype(bf16)
        whole = pl.ds(pl.multiple_of(base, block), block)
        pre[...] = jnp.dot(active[whole, :], w[...], preferred_element_type=f32)
        for r, c in chunks(block, width):
            to = shifted(r, base)
            far = slice(width + c.start, width + c.stop)
            a = pre[r, c] + b_out[:, c]
            t = 0.5 * jnp.tanh(0.5 * (pre[r, far] + b_out[:, far]))
            g = 0.5 + t
            place = base + r.start + lax.broadcasted_iota(jnp.int32, a.shape, 0)
            add = jnp.where(place < seq_len, a * g, 0.0)
            out[to, c] = (tok_all[to, c].astype(f32) + add).astype(bf16)
            val_a[to, c] = (a * (0.5 - t)).astype(bf16)
            gate[to, c] = g.astype(bf16)
        for c in copies(sems, 0, block, j, results):
            c.start()
        return carry

    lax.fori_loop(0, blocks, tail, 0)
    copy_w.wait()
    copy_spec.wait()
    for j in range(blocks):
        for c in copies(sems, 0, block, j, results):
            c.wait()


def forward(scalars, lengths, vec, b_out, entered, tap_parts, w_parts, n, block):
    tok_all, sig, xs = entered
    n_t = len(tap_parts)
    length, width = tok_all.shape
    blocks = length // block
    table = basis(block)
    full = hbm((length, width), bf16)
    buffer = pltpu.VMEM((length, width), bf16)
    return pl.pallas_call(
        partial(forward_kernel, n, n_t, blocks, block),
        out_shape=[
            full,
            hbm((blocks, 2 * block, width), bf16),
            hbm((width, 2 * width), bf16),
            full,
            full,
            full,
            full,
        ],
        in_specs=[sspec()] * 2 + [vspec()] * (9 + 2 * n_t),
        out_specs=[hspec()] * 7,
        scratch_shapes=[
            buffer,
            pltpu.VMEM((blocks, 2 * block, width), f32),
            pltpu.VMEM((blocks, 2 * block, width), bf16),
            pltpu.VMEM((blocks, 2 * block, width), bf16),
            pltpu.VMEM((block, width), f32),
            pltpu.VMEM((block, 2 * width), f32),
            pltpu.VMEM((blocks, 2 * block, width), bf16),
            pltpu.VMEM((width, 2 * width), bf16),
            buffer,
            buffer,
            buffer,
            buffer,
            buffer,
            pltpu.SemaphoreType.DMA((5, blocks)),
            pltpu.SemaphoreType.DMA((2,)),
        ],
        compiler_params=params(24),
        cost_estimate=cost(15),
        name="forward",
    )(
        scalars,
        lengths,
        vec,
        b_out,
        *two_parts(table),
        *two_parts(table.T),
        *held_in_vmem(tok_all, sig, xs),
        *tap_parts,
        *w_parts,
    )


def mix_back_kernel(n, n_t, blocks, block, sc, lengths, basis_ref, basis_t, w_h, *refs):
    inputs, pieces = refs[:4], refs[4:5]
    kept, sent, grad_pre, grad_mix, spec_g, bias_grad = refs[5:11]
    val_a, gate, slope, sig, w, cot, xs, act_f, comb, sems, sem_w, sem_in = refs[11:]
    loads = list(zip(inputs, (val_a, gate, slope, sig)))
    seq_len, core = lengths[sc[1] * n + sc[0]], sc[1] & 1
    moves = gather_rows(sc[0], pieces, cot, sem_in)
    for move in moves:
        move.start()
    for c in copies(sems, 0, block, 0, loads):
        c.start()
    copy_w = pltpu.make_async_copy(w_h, w, sem_w.at[0])
    copy_w.start()
    for j in range(1, blocks):
        for c in copies(sems, 0, block, j, loads):
            c.start()
    for move in moves:
        move.wait()
    length, width = cot.shape
    half = block // 2
    bias_grad[...] = jnp.zeros_like(bias_grad)

    def front(j, carry):
        for c in copies(sems, 0, block, j, loads):
            c.wait()

        base = j * block
        for r, c in chunks(block, width):
            to = shifted(r, base)
            far = slice(width + c.start, width + c.stop)
            q = cot[to, c].astype(f32)
            place = base + r.start + lax.broadcasted_iota(jnp.int32, q.shape, 0)
            g = gate[to, c].astype(f32)
            qg = jnp.where(place < seq_len, q * g, 0.0)
            grad_pre[to, c] = qg.astype(bf16)
            grad_pre[to, far] = (qg * val_a[to, c].astype(f32)).astype(bf16)

        @pl.when(j == 0)
        def _():
            copy_w.wait()

        whole = pl.ds(pl.multiple_of(base, block), block)
        bias_grad[...] += column_sums(grad_pre[whole, :])
        xs[j] = jnp.dot(basis_ref[...], sig[whole, :], preferred_element_type=f32)
        act_f[...] = lax.dot_general(
            grad_pre[whole, :], w[...], (((1,), (1,)), ((), ())), preferred_element_type=f32
        )

        for r, c in chunks(block, width):
            to = shifted(r, base)
            grad = act_f[r, c].astype(bf16).astype(f32) * slope[to, c].astype(f32)
            grad_mix[to, c] = grad.astype(bf16)
        spec_g[j] = jnp.dot(basis_ref[...], grad_mix[whole, :], preferred_element_type=f32)
        return carry

    lax.fori_loop(0, blocks, front, 0)

    def correlate(sign, row, lanes):
        re, im = pl.ds(row, TILE), pl.ds(pl.multiple_of(row + block, TILE), TILE)
        xr = [xs[j, re, lanes] for j in range(blocks)]
        xi = [xs[j, im, lanes] for j in range(blocks)]
        gr = [spec_g[j, re, lanes] for j in range(blocks)]
        gi = [spec_g[j, im, lanes] for j in range(blocks)]
        next_r = next_i = None
        for d in reversed(range(blocks)):
            dr = di = None
            for m in range(d, blocks):
                j = m - d
                pr = xr[j] * gr[m] + xi[j] * gi[m]
                pi = xr[j] * gi[m] - xi[j] * gr[m]
                dr = pr if dr is None else dr + pr
                di = pi if di is None else di + pi
            cr, ci = dr, di
            if next_r is not None:
                cr = dr + next_i if sign > 0 else dr - next_i
                ci = di - next_r if sign > 0 else di + next_r
            comb[d, re, lanes] = cr.astype(bf16)
            comb[d, im, lanes] = ci.astype(bf16)
            next_r, next_i = dr, di

    tiles(0, half, width, partial(correlate, 1))
    tiles(half, block, width, partial(correlate, -1))
    channels = width // n_t

    def store(t, to, value):
        @pl.when(core == t & 1)
        def _():
            kept[t >> 1, to, : value.shape[1]] = value

        @pl.when(core != t & 1)
        def _():
            sent[t >> 1, to, : value.shape[1]] = value

    def finish(d, carry):
        act_f[...] = jnp.dot(basis_t[...], comb[d], preferred_element_type=f32)
        to = pl.ds(pl.multiple_of(d * block, block), block)
        for t in range(n_t):
            part = act_f[:, t * channels : (t + 1) * channels] * (1.0 / block)
            store(t, to, part.astype(bf16))
        return carry

    lax.fori_loop(0, blocks, finish, 0)

def mix_back(scalars, lengths, w, saved, cot, block, n, n_t):
    length, width = saved[0].shape
    blocks = length // block
    channels = width // n_t
    table = basis(block)
    halves = jax.ShapeDtypeStruct((n_t // 2, length, channels), bf16)
    buffer = pltpu.VMEM((length, width), bf16)
    return pl.pallas_call(
        partial(mix_back_kernel, n, n_t, blocks, block),
        out_shape=[
            halves,
            halves,
            keep((length, 2 * width), bf16),
            keep((length, width), bf16),
            keep((blocks, 2 * block, width), f32),
            jax.ShapeDtypeStruct((8, 2 * width), f32),
        ],
        in_specs=[sspec()] * 2 + [vspec()] * 2 + [hspec()] * 6,
        out_specs=[vspec()] * 6,
        scratch_shapes=[
            buffer,
            buffer,
            buffer,
            buffer,
            pltpu.VMEM((width, 2 * width), bf16),
            buffer,
            pltpu.VMEM((blocks, 2 * block, width), f32),
            pltpu.VMEM((block, width), f32),
            pltpu.VMEM((blocks, 2 * block, width), bf16),
            pltpu.SemaphoreType.DMA((4, blocks)),
            pltpu.SemaphoreType.DMA((1,)),
            pltpu.SemaphoreType.DMA((1,)),
        ],
        compiler_params=params(20),
        cost_estimate=cost(12),
        name="mix_back",
    )(
        scalars,
        lengths,
        jnp.asarray(table, bf16),
        jnp.asarray(table.T, bf16),
        *held_in_hbm(w, *saved, cot),
    )


def weight_back_kernel(n, sc, active, grad_pre, w_keep, w_send):
    core = sc[1] & 1
    groups, _, channels, cols = w_keep.shape
    for t in range(2 * groups):
        value = lax.dot_general(
            active[:, t * channels : (t + 1) * channels],
            grad_pre[...],
            (((0,), (0,)), ((), ())),
            preferred_element_type=f32,
        ).astype(bf16)

        @pl.when(core == t & 1)
        def _(t=t, value=value):
            for d in range(n):
                w_keep[t >> 1, d] = value[:, d * cols : (d + 1) * cols]

        @pl.when(core != t & 1)
        def _(t=t, value=value):
            for d in range(n):
                w_send[t >> 1, d] = value[:, d * cols : (d + 1) * cols]


def weight_back(scalars, active, grad_pre, n, n_t):
    width = active.shape[1]
    halves = jax.ShapeDtypeStruct((n_t // 2, n, width // n_t, 2 * width // n), bf16)
    return pl.pallas_call(
        partial(weight_back_kernel, n),
        out_shape=[halves, halves],
        in_specs=[sspec()] + [vspec()] * 2,
        out_specs=[vspec()] * 2,
        compiler_params=params(8),
        cost_estimate=cost(3),
        name="weight_back",
    )(scalars, active, *held_in_vmem(grad_pre))


def join_kernel(sc, part_keep, part_send, w_a, w_b, keep_out, send_out):
    here = sc[0] & 1
    _, channels, cols = w_a.shape
    for i in range(keep_out.shape[0]):
        for ref, part, k in ((keep_out, part_keep, here), (send_out, part_send, 1 - here)):
            ref[i] = part[i]
            value = w_a[2 * i + k].astype(f32) + w_b[2 * i + k].astype(f32)
            ref[i, 0:channels, :cols] = value.astype(bf16)


def join(scalars, kept, sent, w_a, w_b):
    shape = jax.ShapeDtypeStruct(kept.shape, bf16)
    return pl.pallas_call(
        join_kernel,
        out_shape=[shape, shape],
        in_specs=[sspec()] + [vspec()] * 4,
        out_specs=[vspec()] * 2,
        compiler_params=params(6),
        cost_estimate=cost(1),
        name="join",
    )(scalars, kept, sent, w_a, w_b)


def norm_back_kernel(blocks, block, sc, vec, basis_t, spec_g, grad_mix, spec_h, xhat_h, scale_h, *refs):
    pieces, (res_h, gain_grad, bias_grad) = refs[:1], refs[1:4]
    comb, sig_f, res, spec, xhat, scale, cot_all, grad, cross, mean_g, mean_c, gain_all, sems, sem_w, sem_in = refs[4:]
    loads = [(xhat_h, xhat), (scale_h, scale)]
    copy_spec = pltpu.make_async_copy(spec_h, spec, sem_w.at[0])
    copy_spec.start()
    for j in range(blocks):
        for c in copies(sems, 0, block, j, loads):
            c.start()
    moves = gather_rows(sc[0], pieces, cot_all, sem_in)
    for move in moves:
        move.start()
    copy_spec.wait()
    for move in moves:
        move.wait()
    length, width = xhat.shape
    for k in range(width // LANES):
        gain_all[k * LANES : (k + 1) * LANES, :] = jnp.broadcast_to(
            vec[0:1, k * LANES : (k + 1) * LANES], (LANES, LANES)
        ).T.astype(bf16)
    gain_grad[...] = jnp.zeros_like(gain_grad)
    bias_grad[...] = jnp.zeros_like(bias_grad)

    def correlate(row, lanes):
        re, im = pl.ds(row, TILE), pl.ds(pl.multiple_of(row + block, TILE), TILE)
        kr = [spec[j, re, lanes].astype(f32) for j in range(blocks)]
        ki = [spec[j, im, lanes].astype(f32) for j in range(blocks)]
        gr = [spec_g[j, re, lanes] for j in range(blocks)]
        gi = [spec_g[j, im, lanes] for j in range(blocks)]
        for j in range(blocks):
            dr = di = None
            for m in range(j, blocks):
                d = m - j
                pr = kr[d] * gr[m] + ki[d] * gi[m]
                pi = kr[d] * gi[m] - ki[d] * gr[m]
                dr = pr if dr is None else dr + pr
                di = pi if di is None else di + pi
            comb[j, re, lanes] = dr.astype(bf16)
            comb[j, im, lanes] = di.astype(bf16)

    tiles(0, block, width, correlate)

    def finish(j, carry):
        for c in copies(sems, 0, block, j, loads):
            c.wait()
        sig_f[...] = jnp.dot(basis_t[...], comb[j], preferred_element_type=f32)

        base = j * block
        for r, c in chunks(block, width):
            to = shifted(r, base)
            value = sig_f[r, c] + vec[3:4, c] * grad_mix[to, c].astype(f32)
            value = value.astype(bf16)
            grad[r, c] = value
            cross[r, c] = (value.astype(f32) * xhat[to, c].astype(f32)).astype(bf16)
        gain_grad[...] += column_sums(cross[...])
        bias_grad[...] += column_sums(grad[...])
        weights = gain_all[...]
        mean_g[...] = jnp.dot(grad[...], weights, preferred_element_type=f32) * (1.0 / width)
        mean_c[...] = jnp.dot(cross[...], weights, preferred_element_type=f32) * (1.0 / width)
        for r, c in chunks(block, width):
            to = shifted(r, base)
            g = grad[r, c].astype(f32) * vec[0:1, c]
            g = g - mean_g[r, :] - xhat[to, c].astype(f32) * mean_c[r, :]
            res[to, c] = (cot_all[to, c].astype(f32) + g * scale[to, :]).astype(bf16)
        for copy in copies(sems, 2, block, j, [(res, res_h)]):
            copy.start()
        return carry

    lax.fori_loop(0, blocks, finish, 0)
    for j in range(blocks):
        for copy in copies(sems, 2, block, j, [(res, res_h)]):
            copy.wait()


def norm_back(scalars, vec, spec, spec_g, grad_mix, xhat, scale, cot, block):
    length, width = xhat.shape
    blocks = length // block
    buffer = pltpu.VMEM((length, width), bf16)
    return pl.pallas_call(
        partial(norm_back_kernel, blocks, block),
        out_shape=[hbm((length, width), bf16)] + [jax.ShapeDtypeStruct((8, width), f32)] * 2,
        in_specs=[sspec()] + [vspec()] * 4 + [hspec()] * 4,
        out_specs=[hspec()] + [vspec()] * 2,
        scratch_shapes=[
            pltpu.VMEM((blocks, 2 * block, width), bf16),
            pltpu.VMEM((block, width), f32),
            buffer,
            pltpu.VMEM((blocks, 2 * block, width), bf16),
            buffer,
            pltpu.VMEM((length, LANES), f32),
            buffer,
            pltpu.VMEM((block, width), bf16),
            pltpu.VMEM((block, width), bf16),
            pltpu.VMEM((block, LANES), f32),
            pltpu.VMEM((block, LANES), f32),
            pltpu.VMEM((width, LANES), bf16),
            pltpu.SemaphoreType.DMA((3, blocks)),
            pltpu.SemaphoreType.DMA((1,)),
            pltpu.SemaphoreType.DMA((1,)),
        ],
        compiler_params=params(14),
        cost_estimate=cost(10),
        name="norm_back",
    )(
        scalars,
        vec,
        jnp.asarray(basis(block).T, bf16),
        *held_in_vmem(spec_g, grad_mix),
        *held_in_hbm(spec, xhat, scale, cot),
    )


def halve_kernel(which, shift, sc, kept, got, keep_out, send_out):
    here = (sc[which] >> shift) & 1
    for i in range(keep_out.shape[0]):
        for k in range(2):
            value = (kept[2 * i + k].astype(f32) + got[2 * i + k].astype(f32)).astype(bf16)

            @pl.when(here == k)
            def _(i=i, value=value):
                keep_out[i] = value

            @pl.when(here != k)
            def _(i=i, value=value):
                send_out[i] = value


def deal_kernel(shift, place, vectors, sc, kept, got, *refs):
    vecs, outs = refs[:vectors], refs[vectors:]
    here = sc[0] >> shift
    vec = vecs[0][...]
    for ref in vecs[1:]:
        vec = vec + ref[...]
    for e, out in enumerate(outs):
        out[: kept.shape[1], :] = (kept[here ^ e].astype(f32) + got[here ^ e].astype(f32)).astype(bf16)
        out[place : place + vec.shape[0], :] = vec.astype(bf16)


def deal(scalars, kept, got, vecs, shift, place):
    rows = pad_to(place + vecs[0].shape[0], 16)
    shape = jax.ShapeDtypeStruct((rows, kept.shape[2]), bf16)
    return pl.pallas_call(
        partial(deal_kernel, shift, place, len(vecs)),
        out_shape=[shape] * kept.shape[0],
        in_specs=[sspec()] + [vspec()] * (2 + len(vecs)),
        out_specs=[vspec()] * kept.shape[0],
        compiler_params=params(5),
        cost_estimate=cost(1),
        name="deal",
    )(scalars, kept, got, *vecs)


def halve(scalars, kept, got, which, shift):
    shape = jax.ShapeDtypeStruct((kept.shape[0] // 2, *kept.shape[1:]), bf16)
    return pl.pallas_call(
        partial(halve_kernel, which, shift),
        out_shape=[shape, shape],
        in_specs=[sspec(), vspec(), vspec()],
        out_specs=[vspec()] * 2,
        compiler_params=params(5),
        cost_estimate=cost(1),
        name="halve",
    )(scalars, kept, got)


def weave_kernel(n, whole, sc, *refs):
    if whole:
        pieces, out, held = [refs[0].at[s] for s in range(n)], refs[1], refs[2]
    else:
        pieces, out, held = refs[:n], refs[n], refs[n + 1]
    rank = sc[0]
    rows, width = pieces[0].shape
    step = min(rows, 32)

    def part(r, carry):
        at = pl.ds(pl.multiple_of(r * step, step), step)
        for s in range(n):
            src = s if whole else lax.rem(rank - s + n, n)
            for c in range(width // LANES):
                lanes = slice(c * LANES, (c + 1) * LANES)
                held[c, pl.ds(src, step, stride=n), :] = pieces[s][at, lanes].astype(f32)
        for c in range(width // LANES):
            lanes = slice(c * LANES, (c + 1) * LANES)
            out[at, :, lanes] = held[c].reshape(step, n, LANES).astype(bf16)
        return carry

    lax.fori_loop(0, rows // step, part, 0)


def weave(scalars, pieces):
    whole = not isinstance(pieces, list)
    n = pieces.shape[0] if whole else len(pieces)
    rows, width = pieces[0].shape
    args = [pieces] if whole else pieces
    return pl.pallas_call(
        partial(weave_kernel, n, whole),
        out_shape=jax.ShapeDtypeStruct((rows, n, width), bf16),
        in_specs=[sspec()] + [vspec()] * len(args),
        out_specs=vspec(),
        scratch_shapes=[pltpu.VMEM((width // LANES, min(rows, 32) * n, LANES), f32)],
        compiler_params=params(8),
        cost_estimate=cost(3),
        name="weave",
    )(scalars, *args)


def part_kernel(n, ordered, sc, whole, *refs):
    if ordered:
        outs, held = [refs[0].at[s] for s in range(n)], refs[1]
    else:
        outs, held = refs[-n - 1 : -1], refs[-1]
    rank = sc[0]
    rows, _, width = whole.shape
    step = min(rows, 32)

    def part(r, carry):
        at = pl.ds(pl.multiple_of(r * step, step), step)
        for c in range(width // LANES):
            lanes = slice(c * LANES, (c + 1) * LANES)
            held[c] = whole[at, :, lanes].astype(f32).reshape(step * n, LANES)
        for s in range(n):
            dst = s if ordered else lax.rem(rank + s, n)
            for c in range(width // LANES):
                lanes = slice(c * LANES, (c + 1) * LANES)
                outs[s][at, lanes] = held[c, pl.ds(dst, step, stride=n), :].astype(bf16)
        return carry

    lax.fori_loop(0, rows // step, part, 0)
    if not ordered and len(refs) > n + 1:
        for s in range(n):
            outs[s][rows:, :] = refs[0][...]


def part(scalars, whole, *extra, ordered=False):
    rows, n, width = whole.shape
    more = extra[0].shape[0] if extra else 0
    if ordered:
        shapes = [jax.ShapeDtypeStruct((n, rows, width), bf16)]
    else:
        shapes = [jax.ShapeDtypeStruct((rows + more, width), bf16)] * n
    return pl.pallas_call(
        partial(part_kernel, n, ordered),
        out_shape=shapes,
        in_specs=[sspec(), vspec()] + [vspec()] * len(extra),
        out_specs=[vspec()] * len(shapes),
        scratch_shapes=[pltpu.VMEM((width // LANES, min(rows, 32) * n, LANES), f32)],
        compiler_params=params(8),
        cost_estimate=cost(3),
        name="part",
    )(scalars, *held_in_hbm(whole, *extra))


def total_kernel(states, lines, count, sc, *refs):
    w_out, *grads = refs[count : count + 5]
    outs = refs[count + 5 :]
    channels, cols = w_out.shape
    rank = sc[0]
    total = refs[0][...].astype(f32)
    for ref in refs[1:count]:
        total = total + ref[...].astype(f32)
    w_out[...] = total[:channels, :cols]
    for k, ref in enumerate(grads):
        ref[...] = total[channels + k * states : channels + (k + 1) * states, :channels]
    top = channels + 4 * states
    for k, out in enumerate(outs):
        per = out.shape[1]
        slots = (2 * lines if k == 4 else lines) * WIDE // per
        value = jnp.zeros((1, per), f32)
        for slot in range(slots):
            line, lane = divmod(slot * per, WIDE)
            row = top + k * lines + line
            value = jnp.where(rank == slot, total[row : row + 1, lane : lane + per], value)
        out[...] = value


def totals(scalars, terms, channels, cols, states, per, lines):
    grad = jax.ShapeDtypeStruct((states, channels), f32)
    one = jax.ShapeDtypeStruct((1, per), f32)
    return pl.pallas_call(
        partial(total_kernel, states, lines, len(terms)),
        out_shape=[jax.ShapeDtypeStruct((channels, cols), f32)]
        + [grad] * 4
        + [one] * 4
        + [jax.ShapeDtypeStruct((1, 2 * per), f32)],
        in_specs=[sspec()] + [vspec()] * len(terms),
        out_specs=[vspec()] * 10,
        compiler_params=params(4),
        cost_estimate=cost(1),
        name="totals",
    )(scalars, *terms)


def local(n_dp, n_t, tokens, cotangent, lengths, ln_gain, ln_bias, lam_log, lam_im, w_re, w_im, log_dt, skip_gain, w_out, b_out):
    rows, seqs, width = tokens.shape
    assert seqs == n_dp
    length = rows * n_dp
    block = min(256, length)
    rank = lax.axis_index("dp")
    rank_t = lax.axis_index("tensor")
    channels, states = lam_log.shape
    cols = w_out.shape[1]
    per = width // n_dp
    bits = [1 << k for k in range(n_t.bit_length() - 1)]
    scalars = jnp.stack([rank, rank_t]).astype(jnp.int32)

    after = lambda value, *others: lax.optimization_barrier((value, others))[0]
    pieces = list(part(scalars, tokens))
    vecs = [after(ln_gain, pieces), ln_bias, log_dt, skip_gain, b_out]
    blob = pack([lam_log.T, lam_im.T, w_re.T, w_im.T], vecs, w_out)
    tok_pieces = dict(enumerate(pieces[:1]))
    waits, needs = {0: [], 1: [1], 2: [2, 3, 4, 5, 6]}, {5: 0, 6: 1, 7: 1}
    merges = {-1: ()}
    steps = n_dp.bit_length() - 1

    def send(s):
        if s not in tok_pieces and s < n_dp:
            piece = after(pieces[s], merges[min(needs.get(s, -1), steps - 1)])
            pairs = [(k, (k + s) % n_dp) for k in range(n_dp)]
            tok_pieces[s] = lax.ppermute(piece, "dp", pairs)
        return tok_pieces.get(s, ())

    for k in range(steps):
        got = flip_bit(blob, "dp", n_dp, n_dp >> (k + 1))
        before = [send(s) for s in waits.get(k, [])]
        blob = merge(scalars, after(blob, before), got, 0, steps - 1 - k)
        merges[k] = blob
    tok_pieces = [send(s) for s in range(n_dp)]
    w_own = collect(blob, channels, cols)
    taps, par_all, vec, b_full = make_taps(
        scalars, after(blob, w_own), states, length, width, channels
    )
    cot = after(part(scalars, cotangent, ordered=True)[0], blob, tok_pieces)
    cot = lax.all_to_all(cot, "dp", 0, 0, tiled=True).reshape(length, width)
    tok_all, sig, xs, sig_keep, xhat, scale = enter(scalars, vec, tok_pieces, length, block)

    def spread(own):
        parts = {0: own}
        for bit in reversed(bits):
            for e in list(parts):
                value = after(parts[e], sig) if bit == 1 else parts[e]
                parts[e | bit] = flip_bit(value, "tensor", n_t, bit)
        return [parts[e] for e in range(n_t)]

    tap_parts = spread(taps)
    w_parts = spread(w_own)

    out_t, spec, w_full, *saved = forward(
        scalars, lengths, vec, b_full, (tok_all, sig, xs), tap_parts, w_parts, n_dp, block
    )
    active, slope, val_a, gate = saved
    out_back = lax.all_to_all(out_t.reshape(n_dp, rows, width), "dp", 0, 0, tiled=True)
    saved = [val_a, gate, slope, sig_keep]
    kept, sent, grad_pre, grad_mix, spec_g, out8 = mix_back(
        scalars, lengths, w_full, saved, cot, block, n_dp, n_t
    )

    def reduce_groups(kept, sent, axis, size, which, hook=lambda value: value):
        got = hook(flip_bit(sent, axis, size, 1))
        for shift in range(1, size.bit_length() - 1):
            kept, sent = halve(scalars, kept, got, which, shift)
            got = flip_bit(sent, axis, size, 1 << shift)
        return kept[0], got[0], sent

    w_keep, w_send = weight_back(scalars, active, grad_pre, n_dp, n_t)
    *grads, sent = reduce_groups(
        kept, sent, "tensor", n_t, 1, lambda got: after(got, w_keep)
    )
    spec_g = after(spec_g, sent)
    grad_rows, gain8, bias8 = norm_back(
        scalars, vec, spec, spec_g, grad_mix, xhat, scale, cot, block
    )
    *w_two, w_sent = reduce_groups(w_keep, w_send, "tensor", n_t, 1)
    grad_rows = after(grad_rows, out_back, grads, w_sent)
    grad_back = lax.all_to_all(grad_rows.reshape(n_dp, rows, width), "dp", 0, 0, tiled=True)
    kept, sent, vec_sum = taps_back(
        scalars, par_all, vec, grads, gain8, bias8, out8, length, n_dp, states
    )
    out = weave(scalars, after(out_back, kept))
    kept, sent = join(scalars, kept, sent, *w_two)
    others = [
        lax.ppermute(vec_sum, "tensor", [(k, k ^ e) for k in range(n_t)]) for e in range(1, n_t)
    ]
    vec_sum = sum(others, vec_sum)
    got = flip_bit(sent, "dp", n_dp, 1)
    got_vec = flip_bit(vec_sum, "dp", n_dp, 1)
    shift = 1
    while kept.shape[0] > 4:
        kept, sent = halve(scalars, after(kept, out), got, 0, shift)
        got = flip_bit(sent, "dp", n_dp, 1 << shift)
        vec_sum = vec_sum + got_vec
        got_vec = flip_bit(vec_sum, "dp", n_dp, 1 << shift)
        shift += 1
    vecs = [vec_sum, got_vec]
    terms = deal(scalars, after(kept, out), got, vecs, shift, channels + 4 * states)
    terms = list(terms[:1]) + [
        flip_bit(terms[e], "dp", n_dp, e << shift) for e in range(1, len(terms))
    ]
    grad_tokens = weave(scalars, after(grad_back, terms[0]))
    terms[0] = after(terms[0], grad_tokens)
    grad_w_out, *grads = totals(scalars, terms, channels, cols, states, per, width // WIDE)
    g_lam_log, g_lam_im, g_w_re, g_w_im = (g.T for g in grads[:4])
    g_gain, g_bias, g_dt, g_skip, g_b = (v.reshape(-1) for v in grads[4:])

    return (
        out,
        grad_tokens,
        g_gain,
        g_bias,
        g_lam_log,
        g_lam_im,
        g_w_re,
        g_w_im,
        g_dt,
        g_skip,
        grad_w_out,
        g_b,
    )


def solution(mesh):
    big = P("dp", "tensor", None)
    grid = P("tensor", "dp")
    line = P("dp")
    return jax.shard_map(
        partial(local, mesh.shape["dp"], mesh.shape["tensor"]),
        mesh=mesh,
        in_specs=(big, big, P(), line, line, grid, grid, grid, grid, line, line, grid, line),
        out_specs=(big, big, line, line, grid, grid, grid, grid, line, line, grid, line),
        check_vma=False,
    )
```

```python
from functools import partial

import jax
import jax.numpy as jnp
import ml_dtypes
import numpy as np
from jax import lax
from jax.experimental import pallas as pl
from jax.experimental.pallas import tpu as pltpu
from jax.sharding import PartitionSpec as P

epsilon = 1e-05
f32 = jnp.float32
bf16 = jnp.bfloat16


def params(mib):
    return pltpu.CompilerParams(vmem_limit_bytes=mib * 1024 * 1024)


def cost(us):
    return pl.CostEstimate(flops=0, bytes_accessed=int(us * 1e4), transcendentals=0)


def keep(shape, dtype):
    return pltpu.VMEM(shape, dtype)


def held_in_vmem(*arrays):
    return [pltpu.with_memory_space_constraint(a, pltpu.VMEM) for a in arrays]


def hbm(shape, dtype):
    return pltpu.HBM(shape, dtype)


def hspec():
    return pl.BlockSpec(memory_space=pltpu.HBM)


def copies(sems, index, block, j, pairs):
    at = pl.ds(j * block if isinstance(j, int) else pl.multiple_of(j * block, block), block)
    return [
        pltpu.make_async_copy(src.at[at], dst.at[at], sems.at[index + k, j])
        for k, (src, dst) in enumerate(pairs)
    ]


def gather_rows(rank, pieces, whole, sems):
    n = len(pieces)
    if n == 1:
        return [pltpu.make_async_copy(pieces[0], whole, sems.at[0])]
    rows = whole.shape[0] // n
    moves = []
    for s, piece in enumerate(pieces):
        to = pl.ds(pl.multiple_of(lax.rem(rank - s + n, n) * rows, rows), rows)
        moves.append(pltpu.make_async_copy(piece.at[pl.ds(0, rows)], whole.at[to], sems.at[s]))
    return moves


def held_in_hbm(*arrays):
    return [pltpu.with_memory_space_constraint(a, pltpu.HBM) for a in arrays]


def vspec():
    return pl.BlockSpec(memory_space=pltpu.VMEM)


def sspec():
    return pl.BlockSpec(memory_space=pltpu.SMEM)


def basis(block):
    freq = np.concatenate([np.arange(0, block, 2), np.arange(1, block, 2)])
    angle = np.pi * (2 * freq[:, None] + 1) * np.arange(block)[None, :] / (2 * block)
    forward = np.concatenate([np.cos(angle), -np.sin(angle)], axis=0)
    return forward.astype(np.float32)


def two_parts(value):
    high = value.astype(ml_dtypes.bfloat16)
    low = (value - high.astype(np.float32)).astype(ml_dtypes.bfloat16)
    return jnp.asarray(high), jnp.asarray(low)


def shift_exchange(pieces, axis, size):
    out = [pieces[0]]
    for s in range(1, size):
        out.append(lax.ppermute(pieces[s], axis, [(k, (k + s) % size) for k in range(size)]))
    return out


def flip_bit(value, axis, size, bit):
    return lax.ppermute(value, axis, [(k, k ^ bit) for k in range(size)])


WIDE = 128


def pad_to(value, multiple):
    return -(-value // multiple) * multiple


def planes(value):
    parts = []
    for _ in range(3):
        part = value.astype(bf16)
        parts.append(part)
        value = value - part.astype(f32)
    return parts


def split_kernel(rows_f, *refs):
    parts, vecs, w_ref, out, held = refs[:4], refs[4:9], refs[9], refs[10], refs[11]
    states, channels = parts[0].shape
    held[...] = jnp.zeros_like(held)
    for k, ref in enumerate(parts):
        held[k * states : (k + 1) * states, :channels] = ref[...]
    flat = 0
    for ref in vecs:
        row, lane = divmod(flat, WIDE)
        size = ref.shape[1]
        held[4 * states + row : 4 * states + row + 1, lane : lane + size] = ref[...]
        flat += size
    for p, plane in enumerate(planes(held[...])):
        out[0, p * rows_f : (p + 1) * rows_f, :] = plane
    if w_ref.shape[1] < WIDE:
        out[0, 3 * rows_f :, :] = jnp.zeros((w_ref.shape[0], WIDE), bf16)
    out[0, 3 * rows_f :, : w_ref.shape[1]] = w_ref[...]


def float_rows(states, vec_rows):
    return pad_to(4 * states + vec_rows, 8)


def pack(parts, vecs, w):
    vecs = [v.reshape(1, -1) for v in vecs]
    rows_f = float_rows(parts[0].shape[0], -(-sum(v.shape[1] for v in vecs) // WIDE))
    return pl.pallas_call(
        partial(split_kernel, rows_f),
        out_shape=jax.ShapeDtypeStruct((1, 3 * rows_f + w.shape[0], WIDE), bf16),
        in_specs=[vspec()] * 10,
        out_specs=vspec(),
        scratch_shapes=[pltpu.VMEM((rows_f, WIDE), f32)],
        compiler_params=params(4),
        name="pack",
    )(*held_in_hbm(*parts, *vecs, w))


def merge_kernel(which, shift, sc, own, got, out):
    here = (sc[which] >> shift) & 1
    for i in range(own.shape[0]):
        out[2 * i + here] = own[i]
        out[2 * i + 1 - here] = got[i]


def merge(scalars, own, got, which, shift):
    return pl.pallas_call(
        partial(merge_kernel, which, shift),
        out_shape=jax.ShapeDtypeStruct((2 * own.shape[0], *own.shape[1:]), own.dtype),
        in_specs=[sspec(), vspec(), vspec()],
        out_specs=vspec(),
        compiler_params=params(4),
        cost_estimate=cost(1),
        name="merge",
    )(scalars, own, got)


def collect_kernel(blob, out):
    for d in range(out.shape[0]):
        out[d] = blob[d, :, : out.shape[2]]


def collect(blob, channels, cols):
    n, rows, _ = blob.shape
    if (rows - channels) % channels:
        return blob[:, rows - channels :, :cols]
    return pl.pallas_call(
        collect_kernel,
        out_shape=jax.ShapeDtypeStruct((n, channels, cols), bf16),
        grid=(1,),
        in_specs=[pl.BlockSpec((n, channels, WIDE), lambda i: (0, rows // channels - 1, 0))],
        out_specs=pl.BlockSpec((n, channels, cols), lambda i: (0, 0, 0)),
        compiler_params=params(4),
        cost_estimate=cost(1),
        name="collect",
    )(blob)


INNER = 32


def powers(table_r, table_i, zr, zi, count):
    cr, ci = jnp.ones_like(zr), jnp.zeros_like(zi)
    for b in range(count):
        table_r[b] = cr
        table_i[b] = ci
        if b + 1 < count:
            cr, ci = cr * zr - ci * zi, cr * zi + ci * zr


def taps_kernel(n, states, channels, sc, blob, out, par_out, vec_out, b_out, table_r, table_i, part, held):
    rank_t = sc[1]
    per = vec_out.shape[1] // n
    rows_f = float_rows(states, VEC_ROWS(per))
    plane = [blob[:, k * rows_f : (k + 1) * rows_f, :].astype(f32) for k in range(3)]
    held[...] = plane[0] + plane[1] + plane[2]
    for d in range(n):
        for k in range(4):
            par_out[k, d * states : (d + 1) * states, :] = held[d, k * states : (k + 1) * states, :channels]
        top = 4 * states
        for k in range(4):
            row, lane = divmod(k * per, WIDE)
            vec_out[k : k + 1, d * per : (d + 1) * per] = held[d, top + row : top + row + 1, lane : lane + per]
        row, lane = divmod(4 * per, WIDE)
        b_out[:, 2 * d * per : 2 * (d + 1) * per] = held[d, top + row : top + row + 1, lane : lane + 2 * per]
    log_step = vec_out[2:3, 0:channels]
    for t in range(1, vec_out.shape[1] // channels):
        log_step = jnp.where(rank_t == t, vec_out[2:3, t * channels : (t + 1) * channels], log_step)
    vec_out[4:5, 0:channels] = log_step
    step = jnp.exp(log_step)
    decay = jnp.exp(par_out[0]) * step
    turn = par_out[1] * step
    size = jnp.exp(-decay)
    powers(table_r, table_i, size * jnp.cos(turn), size * jnp.sin(turn), INNER)
    far = jnp.exp(-INNER * decay)
    far_r, far_i = far * jnp.cos(INNER * turn), far * jnp.sin(INNER * turn)
    total = decay.shape[0]

    def block(a, carry):
        ar, ai = carry
        for b in range(INNER):
            value = ar * table_r[b] - ai * table_i[b]
            part[b * 8 : (b + 1) * 8, :] = jnp.sum(value.reshape(total // 8, 8, channels), axis=0)
        summed = part[pl.ds(0, INNER, stride=8), :]
        for q in range(1, 8):
            summed = summed + part[pl.ds(q, INNER, stride=8), :]
        out[pl.ds(pl.multiple_of(a * INNER, INNER), INNER), :] = summed.astype(bf16)
        return ar * far_r - ai * far_i, ar * far_i + ai * far_r

    lax.fori_loop(0, out.shape[0] // INNER, block, (par_out[2] * step, par_out[3] * step))


def VEC_ROWS(per):
    return -(-6 * per // WIDE)


def make_taps(scalars, blob, states, length, width, channels):
    n = blob.shape[0]
    total = n * states
    return pl.pallas_call(
        partial(taps_kernel, n, states, channels),
        out_shape=[
            jax.ShapeDtypeStruct((length, channels), bf16),
            jax.ShapeDtypeStruct((4, total, channels), f32),
            jax.ShapeDtypeStruct((8, width), f32),
            jax.ShapeDtypeStruct((1, 2 * width), f32),
        ],
        in_specs=[sspec(), vspec()],
        out_specs=[vspec()] * 4,
        scratch_shapes=[
            pltpu.VMEM((INNER, total, channels), f32),
            pltpu.VMEM((INNER, total, channels), f32),
            pltpu.VMEM((INNER * 8, channels), f32),
            pltpu.VMEM((n, float_rows(states, VEC_ROWS(width // n)), WIDE), f32),
        ],
        compiler_params=params(8),
        cost_estimate=cost(7),
        name="taps",
    )(scalars, blob)


def taps_back_kernel(
    n, states, sc, par, vec, grad_a, grad_b, gain8, bias8, out8, keep_out, send_out, vec_sum, table_r, table_i, summed, held, msg
):
    rank_t = sc[1]
    length, channels = summed.shape
    width = vec.shape[1]
    rate = jnp.exp(par[0])
    step = jnp.exp(vec[4:5, 0:channels])
    decay = rate * step
    turn = par[1] * step
    w_re, w_im = par[2], par[3]
    size = jnp.exp(-decay)
    powers(table_r, table_i, size * jnp.cos(turn), size * jnp.sin(turn), INNER)
    far = jnp.exp(-INNER * decay)
    far_r, far_i = far * jnp.cos(INNER * turn), far * jnp.sin(INNER * turn)
    total = decay.shape[0]
    summed[...] = grad_a[:length, :].astype(f32) + grad_b[:length, :].astype(f32)
    zero = jnp.zeros((total, channels), f32)

    def block(k, carry):
        a = length // INNER - 1 - k
        s0r, s0i, s1r, s1i = [held[q] for q in range(4)]
        s1r, s1i = s1r + INNER * s0r, s1i + INNER * s0i
        s0r, s0i = s0r * far_r - s0i * far_i, s0r * far_i + s0i * far_r
        s1r, s1i = s1r * far_r - s1i * far_i, s1r * far_i + s1i * far_r
        for q, value in enumerate((s0r, s0i, s1r, s1i)):
            held[q] = value
        rows = summed[pl.ds(pl.multiple_of(a * INNER, INNER), INNER), :]
        group = min(32, total)
        for c in range(total // group):
            here = slice(c * group, (c + 1) * group)
            u0r, u0i, u1r, u1i = [held[q, here, :] for q in range(4)]
            tail_r = tail_i = jnp.zeros((group, channels), f32)
            for b in reversed(range(INNER)):
                g = jnp.broadcast_to(rows[b : b + 1, :], (group, channels))
                if b:
                    tail_r, tail_i = tail_r + g * table_r[b, here, :], tail_i + g * table_i[b, here, :]
                    u1r, u1i = u1r + tail_r, u1i + tail_i
                else:
                    tail_r = tail_r + g
            u0r, u0i = u0r + tail_r, u0i + tail_i
            for q, value in enumerate((u0r, u0i, u1r, u1i)):
                held[q, here, :] = value
        return carry

    for q in range(4):
        held[q] = zero
    lax.fori_loop(0, length // INNER, block, 0)
    s0r, s0i, s1r, s1i = [held[q] for q in range(4)]
    wr0 = w_re * s0r - w_im * s0i
    wr1 = w_re * s1r - w_im * s1i
    wi1 = w_re * s1i + w_im * s1r
    dt = jnp.sum(step * (wr0 - decay * wr1 - turn * wi1), axis=0, keepdims=True)
    held[0], held[1] = -step * decay * wr1, -step * step * wi1
    held[2], held[3] = step * s0r, -step * s0i
    rows_w = channels
    lines = width // WIDE
    msg[...] = jnp.zeros_like(msg)
    for d in range(n):
        for k in range(4):
            msg[d, rows_w + k * states : rows_w + (k + 1) * states, :channels] = held[
                k, d * states : (d + 1) * states, :
            ].astype(bf16)
    gain_sum, bias_sum, out_sum = gain8[0:1, :], bias8[0:1, :], out8[0:1, :]
    copies = WIDE // channels
    lane = lax.broadcasted_iota(jnp.int32, (1, WIDE), 1) // channels
    skip_row = jnp.concatenate([summed[0:1, :]] * copies, axis=1) if copies > 1 else summed[0:1, :]
    dt_row = jnp.concatenate([dt] * copies, axis=1) if copies > 1 else dt
    for line in range(lines):
        at = slice(line * WIDE, (line + 1) * WIDE)
        mine = lane + line * copies == rank_t
        rows = [
            gain_sum[:, at],
            bias_sum[:, at],
            jnp.where(mine, dt_row, 0.0),
            jnp.where(mine, skip_row, 0.0),
            out_sum[:, at],
            out_sum[:, width + line * WIDE : width + (line + 1) * WIDE],
        ]
        for k, row in enumerate(rows):
            vec_sum[k * lines + line : k * lines + line + 1, :] = row
    here = sc[0] & 1
    for i in range(n // 2):
        keep_out[i] = msg[2 * i + here]
        send_out[i] = msg[2 * i + 1 - here]


def taps_back(scalars, par, vec, grads, gain8, bias8, out8, length, n, states):
    channels = grads[0].shape[1]
    width = vec.shape[1]
    total = par.shape[1]
    rows = pad_to(channels + 4 * states, 16)
    return pl.pallas_call(
        partial(taps_back_kernel, n, states),
        out_shape=[jax.ShapeDtypeStruct((n // 2, rows, WIDE), bf16)] * 2
        + [jax.ShapeDtypeStruct((6 * (width // WIDE), WIDE), f32)],
        in_specs=[sspec()] + [vspec()] * 7,
        out_specs=[vspec()] * 3,
        scratch_shapes=[
            pltpu.VMEM((INNER, total, channels), f32),
            pltpu.VMEM((INNER, total, channels), f32),
            pltpu.VMEM((length, channels), f32),
            pltpu.VMEM((4, total, channels), f32),
            pltpu.VMEM((n, rows, WIDE), bf16),
        ],
        compiler_params=params(10),
        cost_estimate=cost(10),
        name="taps_back",
    )(scalars, par, vec, *grads, gain8, bias8, out8)


ROWS = 32
TILE = 16
LANES = 128


def chunks(block, width):
    step = min(64, block)
    for r in range(block // step):
        for c in range(width // LANES):
            yield slice(r * step, (r + 1) * step), slice(c * LANES, (c + 1) * LANES)


def row_sums(x):
    ones = jnp.ones((x.shape[1], LANES), bf16)
    return jnp.dot(x, ones, preferred_element_type=f32)


def column_sums(x):
    ones = jnp.ones((8, x.shape[0]), bf16)
    return jnp.dot(ones, x, preferred_element_type=f32)


def whole_block(base, block):
    return pl.ds(base if isinstance(base, int) else pl.multiple_of(base, block), block)


def shifted(rows, base):
    size = rows.stop - rows.start
    if isinstance(base, int):
        return pl.ds(base + rows.start, size)
    return pl.ds(pl.multiple_of(base + rows.start, size), size)


def tiles(first, last, width, body):
    def step(r, carry):
        row = pl.multiple_of(r * TILE, TILE)
        for c in range(width // LANES):
            body(row, slice(c * LANES, (c + 1) * LANES))
        return carry

    lax.fori_loop(first // TILE, last // TILE, step, 0)


def enter_kernel(n, blocks, block, sc, vec, basis_ref, basis_low, *refs):
    pieces = refs[:n]
    tok_all, sig, xs, sig_out, xhat_out, scale_out = refs[n : n + 6]
    xhat, scale, mean, square, sems, sem_in = refs[n + 6 :]
    length, width = tok_all.shape
    moves = gather_rows(sc[0], pieces, tok_all, sem_in)
    for move in moves:
        move.start()
    for move in moves:
        move.wait()
    saves = [(sig, sig_out), (xhat, xhat_out), (scale, scale_out)]

    def transform(j, carry):
        base = j * block
        side = j % 2
        at = whole_block(base, block)
        mean[side] = row_sums(tok_all[at, :]) * (1.0 / width)
        for r, c in chunks(block, width):
            centred = tok_all[shifted(r, base), c].astype(f32) - mean[side, r, :]
            square[side, r, c] = (centred * centred).astype(bf16)
        scale[at, :] = lax.rsqrt(row_sums(square[side]) * (1.0 / width) + epsilon)
        for r, c in chunks(block, width):
            to = shifted(r, base)
            value = (tok_all[to, c].astype(f32) - mean[side, r, :]) * scale[to, :]
            xhat[to, c] = value.astype(bf16)
            sig[to, c] = (value * vec[0:1, c] + vec[1:2, c]).astype(bf16)
        for copy in copies(sems, 0, block, j, saves):
            copy.start()
        value = sig[at, :]
        xs[j] = jnp.dot(basis_ref[...], value, preferred_element_type=f32) + jnp.dot(
            basis_low[...], value, preferred_element_type=f32
        )
        return carry

    for j in range(blocks):
        transform(j, 0)
    for j in range(blocks):
        for copy in copies(sems, 0, block, j, saves):
            copy.wait()


def enter(scalars, vec, pieces, length, block):
    n = len(pieces)
    width = pieces[0].shape[1]
    blocks = length // block
    return pl.pallas_call(
        partial(enter_kernel, n, blocks, block),
        out_shape=[
            keep((length, width), bf16),
            keep((length, width), bf16),
            keep((blocks, 2 * block, width), f32),
            hbm((length, width), bf16),
            hbm((length, width), bf16),
            hbm((length, LANES), f32),
        ],
        in_specs=[sspec()] + [vspec()] * 3 + [hspec()] * n,
        out_specs=[vspec()] * 3 + [hspec()] * 3,
        scratch_shapes=[
            pltpu.VMEM((length, width), bf16),
            pltpu.VMEM((length, LANES), f32),
            pltpu.VMEM((2, block, LANES), f32),
            pltpu.VMEM((2, block, width), bf16),
            pltpu.SemaphoreType.DMA((3, blocks)),
            pltpu.SemaphoreType.DMA((n,)),
        ],
        compiler_params=params(8),
        cost_estimate=cost(7),
        name="enter",
    )(scalars, vec, *two_parts(basis(block)), *pieces)


def forward_kernel(n, n_t, blocks, block, sc, lengths, vec, b_out, basis_ref, basis_low, basis_t, basis_t_low, tok_all, sig, xs, *refs):
    tap_parts, w_parts = refs[:n_t], refs[n_t : 2 * n_t]
    out_h, spec_h, w_h, active_h, slope_h, val_h, gate_h = refs[2 * n_t : 2 * n_t + 7]
    taps, raw, zs, zs_low, mix, pre, spec, w, out, active, slope, val_a, gate, sems, sem_w = refs[2 * n_t + 7 :]
    rank_t = sc[1]
    seq_len = lengths[rank_t * n + sc[0]]
    results = [(out, out_h), (active, active_h), (slope, slope_h), (val_a, val_h), (gate, gate_h)]
    length, width = tok_all.shape
    channels = width // n_t
    half = block // 2
    scale = 1.0 / block
    for e in range(n_t):
        owner = rank_t ^ e
        at = pl.ds(pl.multiple_of(owner * channels, channels), channels)
        if channels % LANES == 0:
            taps[:, at] = tap_parts[e][...]
        else:
            for t in range(n_t):

                @pl.when(owner == t)
                def _(e=e, t=t):
                    taps[:, t * channels : (t + 1) * channels] = tap_parts[e][...]

        count, _, cols = w_parts[e].shape
        for d in range(count):
            w[at, d * cols : (d + 1) * cols] = w_parts[e][d]
    copy_w = pltpu.make_async_copy(w, w_h, sem_w.at[0])
    copy_w.start()

    def spectrum(d, carry):
        at = whole_block(d * block, block)
        value = taps[at, :]
        raw[d] = jnp.dot(basis_ref[...], value, preferred_element_type=f32) + jnp.dot(
            basis_low[...], value, preferred_element_type=f32
        )
        return carry

    for d in range(blocks):
        spectrum(d, 0)

    def product(sign, row, lanes):
        re, im = pl.ds(row, TILE), pl.ds(pl.multiple_of(row + block, TILE), TILE)
        xr = [xs[j, re, lanes] for j in range(blocks)]
        xi = [xs[j, im, lanes] for j in range(blocks)]
        kr, ki = [], []
        for d in range(blocks):
            r, i = raw[d, re, lanes], raw[d, im, lanes]
            if d:
                pr, pi = raw[d - 1, re, lanes], raw[d - 1, im, lanes]
                r, i = (r - pi, i + pr) if sign > 0 else (r + pi, i - pr)
            kr.append(r * scale)
            ki.append(i * scale)
            spec[d, re, lanes] = kr[d].astype(bf16)
            spec[d, im, lanes] = ki[d].astype(bf16)
        for m in range(blocks):
            zr = zi = None
            for j in range(m + 1):
                d = m - j
                pr = xr[j] * kr[d] - xi[j] * ki[d]
                pi = xr[j] * ki[d] + xi[j] * kr[d]
                zr = pr if zr is None else zr + pr
                zi = pi if zi is None else zi + pi
            for at, value in ((re, zr), (im, zi)):
                high = value.astype(bf16)
                zs[m, at, lanes] = high
                zs_low[m, at, lanes] = (value - high.astype(f32)).astype(bf16)

    tiles(0, half, width, partial(product, 1))
    tiles(half, block, width, partial(product, -1))
    copy_spec = pltpu.make_async_copy(spec, spec_h, sem_w.at[1])
    copy_spec.start()

    def tail(j, carry):
        value = zs[j]
        rest = jnp.dot(basis_t_low[...], value, preferred_element_type=f32) + jnp.dot(
            basis_t[...], zs_low[j], preferred_element_type=f32
        )
        side = j % 2
        mix[side] = jnp.dot(basis_t[...], value, preferred_element_type=f32) + rest

        base = j * block
        for r, c in chunks(block, width):
            to = shifted(r, base)
            v = mix[side, r, c] + vec[3:4, c] * sig[to, c].astype(f32)
            sq = v * v
            t = jnp.tanh(v * (0.7978845608 + (0.7978845608 * 0.044715) * sq))
            half_t = 0.5 + 0.5 * t
            active[to, c] = (v * half_t).astype(bf16)
            inner = 0.7978845608 * 0.5 + (0.7978845608 * 1.5 * 0.044715) * sq
            slope[to, c] = (half_t + v * (1.0 - t * t) * inner).astype(bf16)
        whole = whole_block(base, block)
        pre[side] = jnp.dot(active[whole, :], w[...], preferred_element_type=f32)
        for r, c in chunks(block, width):
            to = shifted(r, base)
            far = slice(width + c.start, width + c.stop)
            a = pre[side, r, c] + b_out[:, c]
            t = 0.5 * jnp.tanh(0.5 * (pre[side, r, far] + b_out[:, far]))
            g = 0.5 + t
            place = base + r.start + lax.broadcasted_iota(jnp.int32, a.shape, 0)
            add = jnp.where(place < seq_len, a * g, 0.0)
            out[to, c] = (tok_all[to, c].astype(f32) + add).astype(bf16)
            val_a[to, c] = (a * (0.5 - t)).astype(bf16)
            gate[to, c] = g.astype(bf16)
        for c in copies(sems, 0, block, j, results):
            c.start()
        return carry

    for j in range(blocks):
        tail(j, 0)
    copy_w.wait()
    copy_spec.wait()
    for j in range(blocks):
        for c in copies(sems, 0, block, j, results):
            c.wait()


def forward(scalars, lengths, vec, b_out, entered, tap_parts, w_parts, n, block):
    tok_all, sig, xs = entered
    n_t = len(tap_parts)
    length, width = tok_all.shape
    blocks = length // block
    table = basis(block)
    full = hbm((length, width), bf16)
    buffer = pltpu.VMEM((length, width), bf16)
    return pl.pallas_call(
        partial(forward_kernel, n, n_t, blocks, block),
        out_shape=[
            full,
            hbm((blocks, 2 * block, width), bf16),
            hbm((width, 2 * width), bf16),
            full,
            full,
            full,
            full,
        ],
        in_specs=[sspec()] * 2 + [vspec()] * (9 + 2 * n_t),
        out_specs=[hspec()] * 7,
        scratch_shapes=[
            buffer,
            pltpu.VMEM((blocks, 2 * block, width), f32),
            pltpu.VMEM((blocks, 2 * block, width), bf16),
            pltpu.VMEM((blocks, 2 * block, width), bf16),
            pltpu.VMEM((2, block, width), f32),
            pltpu.VMEM((2, block, 2 * width), f32),
            pltpu.VMEM((blocks, 2 * block, width), bf16),
            pltpu.VMEM((width, 2 * width), bf16),
            buffer,
            buffer,
            buffer,
            buffer,
            buffer,
            pltpu.SemaphoreType.DMA((5, blocks)),
            pltpu.SemaphoreType.DMA((2,)),
        ],
        compiler_params=params(26),
        cost_estimate=cost(15),
        name="forward",
    )(
        scalars,
        lengths,
        vec,
        b_out,
        *two_parts(table),
        *two_parts(table.T),
        *held_in_vmem(tok_all, sig, xs),
        *tap_parts,
        *w_parts,
    )


def mix_back_kernel(n, n_t, blocks, block, sc, lengths, basis_ref, basis_t, w_h, *refs):
    inputs, pieces = refs[:4], refs[4:5]
    kept, sent, grad_pre, grad_mix, spec_g, bias_grad = refs[5:11]
    val_a, gate, slope, sig, w, cot, xs, act_f, comb, sems, sem_w, sem_in = refs[11:]
    loads = list(zip(inputs, (val_a, gate, slope, sig)))
    seq_len, core = lengths[sc[1] * n + sc[0]], sc[1] & 1
    moves = gather_rows(sc[0], pieces, cot, sem_in)
    for move in moves:
        move.start()
    for c in copies(sems, 0, block, 0, loads):
        c.start()
    copy_w = pltpu.make_async_copy(w_h, w, sem_w.at[0])
    copy_w.start()
    for j in range(1, blocks):
        for c in copies(sems, 0, block, j, loads):
            c.start()
    for move in moves:
        move.wait()
    length, width = cot.shape
    half = block // 2
    bias_grad[...] = jnp.zeros_like(bias_grad)

    def front(j, carry):
        for c in copies(sems, 0, block, j, loads):
            c.wait()

        base = j * block
        for r, c in chunks(block, width):
            to = shifted(r, base)
            far = slice(width + c.start, width + c.stop)
            q = cot[to, c].astype(f32)
            place = base + r.start + lax.broadcasted_iota(jnp.int32, q.shape, 0)
            g = gate[to, c].astype(f32)
            qg = jnp.where(place < seq_len, q * g, 0.0)
            grad_pre[to, c] = qg.astype(bf16)
            grad_pre[to, far] = (qg * val_a[to, c].astype(f32)).astype(bf16)

        @pl.when(j == 0)
        def _():
            copy_w.wait()

        whole = whole_block(base, block)
        bias_grad[...] += column_sums(grad_pre[whole, :])
        xs[j] = jnp.dot(basis_ref[...], sig[whole, :], preferred_element_type=f32)
        act_f[...] = lax.dot_general(
            grad_pre[whole, :], w[...], (((1,), (1,)), ((), ())), preferred_element_type=f32
        )

        for r, c in chunks(block, width):
            to = shifted(r, base)
            grad = act_f[r, c].astype(bf16).astype(f32) * slope[to, c].astype(f32)
            grad_mix[to, c] = grad.astype(bf16)
        spec_g[j] = jnp.dot(basis_ref[...], grad_mix[whole, :], preferred_element_type=f32)
        return carry

    lax.fori_loop(0, blocks, front, 0)

    def correlate(sign, row, lanes):
        re, im = pl.ds(row, TILE), pl.ds(pl.multiple_of(row + block, TILE), TILE)
        xr = [xs[j, re, lanes] for j in range(blocks)]
        xi = [xs[j, im, lanes] for j in range(blocks)]
        gr = [spec_g[j, re, lanes] for j in range(blocks)]
        gi = [spec_g[j, im, lanes] for j in range(blocks)]
        next_r = next_i = None
        for d in reversed(range(blocks)):
            dr = di = None
            for m in range(d, blocks):
                j = m - d
                pr = xr[j] * gr[m] + xi[j] * gi[m]
                pi = xr[j] * gi[m] - xi[j] * gr[m]
                dr = pr if dr is None else dr + pr
                di = pi if di is None else di + pi
            cr, ci = dr, di
            if next_r is not None:
                cr = dr + next_i if sign > 0 else dr - next_i
                ci = di - next_r if sign > 0 else di + next_r
            comb[d, re, lanes] = cr.astype(bf16)
            comb[d, im, lanes] = ci.astype(bf16)
            next_r, next_i = dr, di

    tiles(0, half, width, partial(correlate, 1))
    tiles(half, block, width, partial(correlate, -1))
    channels = width // n_t

    def store(t, to, value):
        @pl.when(core == t & 1)
        def _():
            kept[t >> 1, to, : value.shape[1]] = value

        @pl.when(core != t & 1)
        def _():
            sent[t >> 1, to, : value.shape[1]] = value

    def finish(d, carry):
        act_f[...] = jnp.dot(basis_t[...], comb[d], preferred_element_type=f32)
        to = pl.ds(pl.multiple_of(d * block, block), block)
        for t in range(n_t):
            part = act_f[:, t * channels : (t + 1) * channels] * (1.0 / block)
            store(t, to, part.astype(bf16))
        return carry

    lax.fori_loop(0, blocks, finish, 0)

def mix_back(scalars, lengths, w, saved, cot, block, n, n_t):
    length, width = saved[0].shape
    blocks = length // block
    channels = width // n_t
    table = basis(block)
    halves = jax.ShapeDtypeStruct((n_t // 2, length, channels), bf16)
    buffer = pltpu.VMEM((length, width), bf16)
    return pl.pallas_call(
        partial(mix_back_kernel, n, n_t, blocks, block),
        out_shape=[
            halves,
            halves,
            keep((length, 2 * width), bf16),
            keep((length, width), bf16),
            keep((blocks, 2 * block, width), f32),
            jax.ShapeDtypeStruct((8, 2 * width), f32),
        ],
        in_specs=[sspec()] * 2 + [vspec()] * 2 + [hspec()] * 6,
        out_specs=[vspec()] * 6,
        scratch_shapes=[
            buffer,
            buffer,
            buffer,
            buffer,
            pltpu.VMEM((width, 2 * width), bf16),
            buffer,
            pltpu.VMEM((blocks, 2 * block, width), f32),
            pltpu.VMEM((block, width), f32),
            pltpu.VMEM((blocks, 2 * block, width), bf16),
            pltpu.SemaphoreType.DMA((4, blocks)),
            pltpu.SemaphoreType.DMA((1,)),
            pltpu.SemaphoreType.DMA((1,)),
        ],
        compiler_params=params(20),
        cost_estimate=cost(12),
        name="mix_back",
    )(
        scalars,
        lengths,
        jnp.asarray(table, bf16),
        jnp.asarray(table.T, bf16),
        *held_in_hbm(w, *saved, cot),
    )


def weight_back_kernel(n, sc, active, grad_pre, w_keep, w_send):
    core = sc[1] & 1
    groups, _, channels, cols = w_keep.shape
    for t in range(2 * groups):
        value = lax.dot_general(
            active[:, t * channels : (t + 1) * channels],
            grad_pre[...],
            (((0,), (0,)), ((), ())),
            preferred_element_type=f32,
        ).astype(bf16)

        @pl.when(core == t & 1)
        def _(t=t, value=value):
            for d in range(n):
                w_keep[t >> 1, d] = value[:, d * cols : (d + 1) * cols]

        @pl.when(core != t & 1)
        def _(t=t, value=value):
            for d in range(n):
                w_send[t >> 1, d] = value[:, d * cols : (d + 1) * cols]


def weight_back(scalars, active, grad_pre, n, n_t):
    width = active.shape[1]
    halves = jax.ShapeDtypeStruct((n_t // 2, n, width // n_t, 2 * width // n), bf16)
    return pl.pallas_call(
        partial(weight_back_kernel, n),
        out_shape=[halves, halves],
        in_specs=[sspec()] + [vspec()] * 2,
        out_specs=[vspec()] * 2,
        compiler_params=params(8),
        cost_estimate=cost(3),
        name="weight_back",
    )(scalars, active, *held_in_vmem(grad_pre))


def join_kernel(sc, part_keep, part_send, w_a, w_b, keep_out, send_out):
    here = sc[0] & 1
    _, channels, cols = w_a.shape
    for i in range(keep_out.shape[0]):
        for ref, part, k in ((keep_out, part_keep, here), (send_out, part_send, 1 - here)):
            ref[i] = part[i]
            value = w_a[2 * i + k].astype(f32) + w_b[2 * i + k].astype(f32)
            ref[i, 0:channels, :cols] = value.astype(bf16)


def join(scalars, kept, sent, w_a, w_b):
    shape = jax.ShapeDtypeStruct(kept.shape, bf16)
    return pl.pallas_call(
        join_kernel,
        out_shape=[shape, shape],
        in_specs=[sspec()] + [vspec()] * 4,
        out_specs=[vspec()] * 2,
        compiler_params=params(6),
        cost_estimate=cost(1),
        name="join",
    )(scalars, kept, sent, w_a, w_b)


def norm_back_kernel(blocks, block, sc, vec, basis_t, spec_g, grad_mix, spec_h, xhat_h, scale_h, *refs):
    pieces, (res_h, gain_grad, bias_grad) = refs[:1], refs[1:4]
    comb, sig_f, res, spec, xhat, scale, cot_all, grad, cross, mean_g, mean_c, gain_all, sems, sem_w, sem_in = refs[4:]
    loads = [(xhat_h, xhat), (scale_h, scale)]
    copy_spec = pltpu.make_async_copy(spec_h, spec, sem_w.at[0])
    copy_spec.start()
    for j in range(blocks):
        for c in copies(sems, 0, block, j, loads):
            c.start()
    moves = gather_rows(sc[0], pieces, cot_all, sem_in)
    for move in moves:
        move.start()
    copy_spec.wait()
    for move in moves:
        move.wait()
    length, width = xhat.shape
    for k in range(width // LANES):
        gain_all[k * LANES : (k + 1) * LANES, :] = jnp.broadcast_to(
            vec[0:1, k * LANES : (k + 1) * LANES], (LANES, LANES)
        ).T.astype(bf16)
    gain_grad[...] = jnp.zeros_like(gain_grad)
    bias_grad[...] = jnp.zeros_like(bias_grad)

    def correlate(row, lanes):
        re, im = pl.ds(row, TILE), pl.ds(pl.multiple_of(row + block, TILE), TILE)
        kr = [spec[j, re, lanes].astype(f32) for j in range(blocks)]
        ki = [spec[j, im, lanes].astype(f32) for j in range(blocks)]
        gr = [spec_g[j, re, lanes] for j in range(blocks)]
        gi = [spec_g[j, im, lanes] for j in range(blocks)]
        for j in range(blocks):
            dr = di = None
            for m in range(j, blocks):
                d = m - j
                pr = kr[d] * gr[m] + ki[d] * gi[m]
                pi = kr[d] * gi[m] - ki[d] * gr[m]
                dr = pr if dr is None else dr + pr
                di = pi if di is None else di + pi
            comb[j, re, lanes] = dr.astype(bf16)
            comb[j, im, lanes] = di.astype(bf16)

    tiles(0, block, width, correlate)

    def finish(j, carry):
        for c in copies(sems, 0, block, j, loads):
            c.wait()
        sig_f[...] = jnp.dot(basis_t[...], comb[j], preferred_element_type=f32)

        base = j * block
        for r, c in chunks(block, width):
            to = shifted(r, base)
            value = sig_f[r, c] + vec[3:4, c] * grad_mix[to, c].astype(f32)
            value = value.astype(bf16)
            grad[r, c] = value
            cross[r, c] = (value.astype(f32) * xhat[to, c].astype(f32)).astype(bf16)
        gain_grad[...] += column_sums(cross[...])
        bias_grad[...] += column_sums(grad[...])
        weights = gain_all[...]
        mean_g[...] = jnp.dot(grad[...], weights, preferred_element_type=f32) * (1.0 / width)
        mean_c[...] = jnp.dot(cross[...], weights, preferred_element_type=f32) * (1.0 / width)
        for r, c in chunks(block, width):
            to = shifted(r, base)
            g = grad[r, c].astype(f32) * vec[0:1, c]
            g = g - mean_g[r, :] - xhat[to, c].astype(f32) * mean_c[r, :]
            res[to, c] = (cot_all[to, c].astype(f32) + g * scale[to, :]).astype(bf16)
        for copy in copies(sems, 2, block, j, [(res, res_h)]):
            copy.start()
        return carry

    lax.fori_loop(0, blocks, finish, 0)
    for j in range(blocks):
        for copy in copies(sems, 2, block, j, [(res, res_h)]):
            copy.wait()


def norm_back(scalars, vec, spec, spec_g, grad_mix, xhat, scale, cot, block):
    length, width = xhat.shape
    blocks = length // block
    buffer = pltpu.VMEM((length, width), bf16)
    return pl.pallas_call(
        partial(norm_back_kernel, blocks, block),
        out_shape=[hbm((length, width), bf16)] + [jax.ShapeDtypeStruct((8, width), f32)] * 2,
        in_specs=[sspec()] + [vspec()] * 4 + [hspec()] * 4,
        out_specs=[hspec()] + [vspec()] * 2,
        scratch_shapes=[
            pltpu.VMEM((blocks, 2 * block, width), bf16),
            pltpu.VMEM((block, width), f32),
            buffer,
            pltpu.VMEM((blocks, 2 * block, width), bf16),
            buffer,
            pltpu.VMEM((length, LANES), f32),
            buffer,
            pltpu.VMEM((block, width), bf16),
            pltpu.VMEM((block, width), bf16),
            pltpu.VMEM((block, LANES), f32),
            pltpu.VMEM((block, LANES), f32),
            pltpu.VMEM((width, LANES), bf16),
            pltpu.SemaphoreType.DMA((3, blocks)),
            pltpu.SemaphoreType.DMA((1,)),
            pltpu.SemaphoreType.DMA((1,)),
        ],
        compiler_params=params(14),
        cost_estimate=cost(10),
        name="norm_back",
    )(
        scalars,
        vec,
        jnp.asarray(basis(block).T, bf16),
        *held_in_vmem(spec_g, grad_mix),
        *held_in_hbm(spec, xhat, scale, cot),
    )


def halve_kernel(which, shift, sc, kept, got, keep_out, send_out):
    here = (sc[which] >> shift) & 1
    for i in range(keep_out.shape[0]):
        for k in range(2):
            value = (kept[2 * i + k].astype(f32) + got[2 * i + k].astype(f32)).astype(bf16)

            @pl.when(here == k)
            def _(i=i, value=value):
                keep_out[i] = value

            @pl.when(here != k)
            def _(i=i, value=value):
                send_out[i] = value


def deal_kernel(shift, place, vectors, sc, kept, got, *refs):
    vecs, outs = refs[:vectors], refs[vectors:]
    here = sc[0] >> shift
    vec = vecs[0][...]
    for ref in vecs[1:]:
        vec = vec + ref[...]
    for e, out in enumerate(outs):
        out[: kept.shape[1], :] = (kept[here ^ e].astype(f32) + got[here ^ e].astype(f32)).astype(bf16)
        out[place : place + vec.shape[0], :] = vec.astype(bf16)


def deal(scalars, kept, got, vecs, shift, place):
    rows = pad_to(place + vecs[0].shape[0], 16)
    shape = jax.ShapeDtypeStruct((rows, kept.shape[2]), bf16)
    return pl.pallas_call(
        partial(deal_kernel, shift, place, len(vecs)),
        out_shape=[shape] * kept.shape[0],
        in_specs=[sspec()] + [vspec()] * (2 + len(vecs)),
        out_specs=[vspec()] * kept.shape[0],
        compiler_params=params(5),
        cost_estimate=cost(1),
        name="deal",
    )(scalars, kept, got, *vecs)


def halve(scalars, kept, got, which, shift):
    shape = jax.ShapeDtypeStruct((kept.shape[0] // 2, *kept.shape[1:]), bf16)
    return pl.pallas_call(
        partial(halve_kernel, which, shift),
        out_shape=[shape, shape],
        in_specs=[sspec(), vspec(), vspec()],
        out_specs=[vspec()] * 2,
        compiler_params=params(5),
        cost_estimate=cost(1),
        name="halve",
    )(scalars, kept, got)


def weave_kernel(n, whole, sc, *refs):
    if whole:
        pieces, out, held = [refs[0].at[s] for s in range(n)], refs[1], refs[2]
    else:
        pieces, out, held = refs[:n], refs[n], refs[n + 1]
    rank = sc[0]
    rows, width = pieces[0].shape
    step = min(rows, 32)

    def part(r, carry):
        at = pl.ds(pl.multiple_of(r * step, step), step)
        for s in range(n):
            src = s if whole else lax.rem(rank - s + n, n)
            for c in range(width // LANES):
                lanes = slice(c * LANES, (c + 1) * LANES)
                held[c, pl.ds(src, step, stride=n), :] = pieces[s][at, lanes].astype(f32)
        for c in range(width // LANES):
            lanes = slice(c * LANES, (c + 1) * LANES)
            out[at, :, lanes] = held[c].reshape(step, n, LANES).astype(bf16)
        return carry

    lax.fori_loop(0, rows // step, part, 0)


def weave(scalars, pieces):
    whole = not isinstance(pieces, list)
    n = pieces.shape[0] if whole else len(pieces)
    rows, width = pieces[0].shape
    args = [pieces] if whole else pieces
    return pl.pallas_call(
        partial(weave_kernel, n, whole),
        out_shape=jax.ShapeDtypeStruct((rows, n, width), bf16),
        in_specs=[sspec()] + [vspec()] * len(args),
        out_specs=vspec(),
        scratch_shapes=[pltpu.VMEM((width // LANES, min(rows, 32) * n, LANES), f32)],
        compiler_params=params(8),
        cost_estimate=cost(3),
        name="weave",
    )(scalars, *args)


def part_kernel(n, ordered, sc, whole, *refs):
    if ordered:
        outs, held = [refs[0].at[s] for s in range(n)], refs[1]
    else:
        outs, held = refs[-n - 1 : -1], refs[-1]
    rank = sc[0]
    rows, _, width = whole.shape
    step = min(rows, 32)

    def part(r, carry):
        at = pl.ds(pl.multiple_of(r * step, step), step)
        for c in range(width // LANES):
            lanes = slice(c * LANES, (c + 1) * LANES)
            held[c] = whole[at, :, lanes].astype(f32).reshape(step * n, LANES)
        for s in range(n):
            dst = s if ordered else lax.rem(rank + s, n)
            for c in range(width // LANES):
                lanes = slice(c * LANES, (c + 1) * LANES)
                outs[s][at, lanes] = held[c, pl.ds(dst, step, stride=n), :].astype(bf16)
        return carry

    lax.fori_loop(0, rows // step, part, 0)
    if not ordered and len(refs) > n + 1:
        for s in range(n):
            outs[s][rows:, :] = refs[0][...]


def part(scalars, whole, *extra, ordered=False):
    rows, n, width = whole.shape
    more = extra[0].shape[0] if extra else 0
    if ordered:
        shapes = [jax.ShapeDtypeStruct((n, rows, width), bf16)]
    else:
        shapes = [jax.ShapeDtypeStruct((rows + more, width), bf16)] * n
    return pl.pallas_call(
        partial(part_kernel, n, ordered),
        out_shape=shapes,
        in_specs=[sspec(), vspec()] + [vspec()] * len(extra),
        out_specs=[vspec()] * len(shapes),
        scratch_shapes=[pltpu.VMEM((width // LANES, min(rows, 32) * n, LANES), f32)],
        compiler_params=params(8),
        cost_estimate=cost(3),
        name="part",
    )(scalars, *held_in_hbm(whole, *extra))


def total_kernel(states, lines, count, sc, *refs):
    w_out, *grads = refs[count : count + 5]
    outs = refs[count + 5 :]
    channels, cols = w_out.shape
    rank = sc[0]
    total = refs[0][...].astype(f32)
    for ref in refs[1:count]:
        total = total + ref[...].astype(f32)
    w_out[...] = total[:channels, :cols]
    for k, ref in enumerate(grads):
        ref[...] = total[channels + k * states : channels + (k + 1) * states, :channels]
    top = channels + 4 * states
    for k, out in enumerate(outs):
        per = out.shape[1]
        slots = (2 * lines if k == 4 else lines) * WIDE // per
        value = jnp.zeros((1, per), f32)
        for slot in range(slots):
            line, lane = divmod(slot * per, WIDE)
            row = top + k * lines + line
            value = jnp.where(rank == slot, total[row : row + 1, lane : lane + per], value)
        out[...] = value


def totals(scalars, terms, channels, cols, states, per, lines):
    grad = jax.ShapeDtypeStruct((states, channels), f32)
    one = jax.ShapeDtypeStruct((1, per), f32)
    return pl.pallas_call(
        partial(total_kernel, states, lines, len(terms)),
        out_shape=[jax.ShapeDtypeStruct((channels, cols), f32)]
        + [grad] * 4
        + [one] * 4
        + [jax.ShapeDtypeStruct((1, 2 * per), f32)],
        in_specs=[sspec()] + [vspec()] * len(terms),
        out_specs=[vspec()] * 10,
        compiler_params=params(4),
        cost_estimate=cost(1),
        name="totals",
    )(scalars, *terms)


def local(n_dp, n_t, tokens, cotangent, lengths, ln_gain, ln_bias, lam_log, lam_im, w_re, w_im, log_dt, skip_gain, w_out, b_out):
    rows, seqs, width = tokens.shape
    assert seqs == n_dp
    length = rows * n_dp
    block = min(256, length)
    rank = lax.axis_index("dp")
    rank_t = lax.axis_index("tensor")
    channels, states = lam_log.shape
    cols = w_out.shape[1]
    per = width // n_dp
    bits = [1 << k for k in range(n_t.bit_length() - 1)]
    scalars = jnp.stack([rank, rank_t]).astype(jnp.int32)

    after = lambda value, *others: lax.optimization_barrier((value, others))[0]
    pieces = list(part(scalars, tokens))
    vecs = [after(ln_gain, pieces), ln_bias, log_dt, skip_gain, b_out]
    blob = pack([lam_log.T, lam_im.T, w_re.T, w_im.T], vecs, w_out)
    tok_pieces = dict(enumerate(pieces[:1]))
    waits, needs = {0: [], 1: [1], 2: [2, 3, 4]}, {5: 0, 6: 0, 7: 1}
    merges = {-1: ()}
    steps = n_dp.bit_length() - 1

    def send(s):
        if s not in tok_pieces and s < n_dp:
            piece = after(pieces[s], merges[min(needs.get(s, -1), steps - 1)])
            pairs = [(k, (k + s) % n_dp) for k in range(n_dp)]
            tok_pieces[s] = lax.ppermute(piece, "dp", pairs)
        return tok_pieces.get(s, ())

    for k in range(steps):
        got = flip_bit(blob, "dp", n_dp, n_dp >> (k + 1))
        before = [send(s) for s in waits.get(k, [])]
        blob = merge(scalars, after(blob, before), got, 0, steps - 1 - k)
        merges[k] = blob
    tok_pieces = [send(s) for s in range(n_dp)]
    w_own = collect(blob, channels, cols)
    taps, par_all, vec, b_full = make_taps(
        scalars, after(blob, w_own), states, length, width, channels
    )
    cot = after(part(scalars, cotangent, ordered=True)[0], blob, tok_pieces)
    cot = lax.all_to_all(cot, "dp", 0, 0, tiled=True).reshape(length, width)
    tok_all, sig, xs, sig_keep, xhat, scale = enter(scalars, vec, tok_pieces, length, block)

    def spread(own):
        parts = {0: own}
        for bit in reversed(bits):
            for e in list(parts):
                value = after(parts[e], sig) if bit == 1 else parts[e]
                parts[e | bit] = flip_bit(value, "tensor", n_t, bit)
        return [parts[e] for e in range(n_t)]

    tap_parts = spread(taps)
    w_parts = spread(w_own)

    out_t, spec, w_full, *saved = forward(
        scalars, lengths, vec, b_full, (tok_all, sig, xs), tap_parts, w_parts, n_dp, block
    )
    active, slope, val_a, gate = saved
    out_back = lax.all_to_all(out_t.reshape(n_dp, rows, width), "dp", 0, 0, tiled=True)
    saved = [val_a, gate, slope, sig_keep]
    kept, sent, grad_pre, grad_mix, spec_g, out8 = mix_back(
        scalars, lengths, w_full, saved, cot, block, n_dp, n_t
    )

    def reduce_groups(kept, sent, axis, size, which, hook=lambda value: value):
        got = hook(flip_bit(sent, axis, size, 1))
        for shift in range(1, size.bit_length() - 1):
            kept, sent = halve(scalars, kept, got, which, shift)
            got = flip_bit(sent, axis, size, 1 << shift)
        return kept[0], got[0], sent

    w_keep, w_send = weight_back(scalars, active, grad_pre, n_dp, n_t)
    *grads, sent = reduce_groups(
        kept, sent, "tensor", n_t, 1, lambda got: after(got, w_keep)
    )
    spec_g = after(spec_g, sent)
    grad_rows, gain8, bias8 = norm_back(
        scalars, vec, spec, spec_g, grad_mix, xhat, scale, cot, block
    )
    *w_two, w_sent = reduce_groups(w_keep, w_send, "tensor", n_t, 1)
    grad_rows = after(grad_rows, out_back, grads, w_sent)
    grad_back = lax.all_to_all(grad_rows.reshape(n_dp, rows, width), "dp", 0, 0, tiled=True)
    kept, sent, vec_sum = taps_back(
        scalars, par_all, vec, grads, gain8, bias8, out8, length, n_dp, states
    )
    out = weave(scalars, after(out_back, kept))
    kept, sent = join(scalars, kept, sent, *w_two)
    others = [
        lax.ppermute(vec_sum, "tensor", [(k, k ^ e) for k in range(n_t)]) for e in range(1, n_t)
    ]
    vec_sum = sum(others, vec_sum)
    got = flip_bit(sent, "dp", n_dp, 1)
    got_vec = flip_bit(vec_sum, "dp", n_dp, 1)
    shift = 1
    while kept.shape[0] > 4:
        kept, sent = halve(scalars, after(kept, out), got, 0, shift)
        got = flip_bit(sent, "dp", n_dp, 1 << shift)
        vec_sum = vec_sum + got_vec
        got_vec = flip_bit(vec_sum, "dp", n_dp, 1 << shift)
        shift += 1
    vecs = [vec_sum, got_vec]
    terms = deal(scalars, after(kept, out), got, vecs, shift, channels + 4 * states)
    terms = list(terms[:1]) + [
        flip_bit(terms[e], "dp", n_dp, e << shift) for e in range(1, len(terms))
    ]
    grad_tokens = weave(scalars, after(grad_back, terms[0]))
    terms[0] = after(terms[0], grad_tokens)
    grad_w_out, *grads = totals(scalars, terms, channels, cols, states, per, width // WIDE)
    g_lam_log, g_lam_im, g_w_re, g_w_im = (g.T for g in grads[:4])
    g_gain, g_bias, g_dt, g_skip, g_b = (v.reshape(-1) for v in grads[4:])

    return (
        out,
        grad_tokens,
        g_gain,
        g_bias,
        g_lam_log,
        g_lam_im,
        g_w_re,
        g_w_im,
        g_dt,
        g_skip,
        grad_w_out,
        g_b,
    )


def solution(mesh):
    big = P("dp", "tensor", None)
    grid = P("tensor", "dp")
    line = P("dp")
    return jax.shard_map(
        partial(local, mesh.shape["dp"], mesh.shape["tensor"]),
        mesh=mesh,
        in_specs=(big, big, P(), line, line, grid, grid, grid, grid, line, line, grid, line),
        out_specs=(big, big, line, line, grid, grid, grid, grid, line, line, grid, line),
        check_vma=False,
    )
```

```python
from functools import partial

import jax
import jax.numpy as jnp
import ml_dtypes
import numpy as np
from jax import lax
from jax.experimental import pallas as pl
from jax.experimental.pallas import tpu as pltpu
from jax.sharding import PartitionSpec as P

epsilon = 1e-05
f32 = jnp.float32
bf16 = jnp.bfloat16


def params(mib):
    return pltpu.CompilerParams(vmem_limit_bytes=mib * 1024 * 1024)


def cost(us):
    return pl.CostEstimate(flops=0, bytes_accessed=int(us * 1e4), transcendentals=0)


def keep(shape, dtype):
    return pltpu.VMEM(shape, dtype)


def held_in_vmem(*arrays):
    return [pltpu.with_memory_space_constraint(a, pltpu.VMEM) for a in arrays]


def hbm(shape, dtype):
    return pltpu.HBM(shape, dtype)


def hspec():
    return pl.BlockSpec(memory_space=pltpu.HBM)


def copies(sems, index, block, j, pairs):
    at = pl.ds(j * block if isinstance(j, int) else pl.multiple_of(j * block, block), block)
    return [
        pltpu.make_async_copy(src.at[at], dst.at[at], sems.at[index + k, j])
        for k, (src, dst) in enumerate(pairs)
    ]


def gather_rows(rank, pieces, whole, sems):
    n = len(pieces)
    if n == 1:
        return [pltpu.make_async_copy(pieces[0], whole, sems.at[0])]
    rows = whole.shape[0] // n
    moves = []
    for s, piece in enumerate(pieces):
        to = pl.ds(pl.multiple_of(lax.rem(rank - s + n, n) * rows, rows), rows)
        moves.append(pltpu.make_async_copy(piece.at[pl.ds(0, rows)], whole.at[to], sems.at[s]))
    return moves


def held_in_hbm(*arrays):
    return [pltpu.with_memory_space_constraint(a, pltpu.HBM) for a in arrays]


def vspec():
    return pl.BlockSpec(memory_space=pltpu.VMEM)


def sspec():
    return pl.BlockSpec(memory_space=pltpu.SMEM)


def basis(block):
    freq = np.concatenate([np.arange(0, block, 2), np.arange(1, block, 2)])
    angle = np.pi * (2 * freq[:, None] + 1) * np.arange(block)[None, :] / (2 * block)
    forward = np.concatenate([np.cos(angle), -np.sin(angle)], axis=0)
    return forward.astype(np.float32)


def two_parts(value):
    high = value.astype(ml_dtypes.bfloat16)
    low = (value - high.astype(np.float32)).astype(ml_dtypes.bfloat16)
    return jnp.asarray(high), jnp.asarray(low)


def shift_exchange(pieces, axis, size):
    out = [pieces[0]]
    for s in range(1, size):
        out.append(lax.ppermute(pieces[s], axis, [(k, (k + s) % size) for k in range(size)]))
    return out


def flip_bit(value, axis, size, bit):
    return lax.ppermute(value, axis, [(k, k ^ bit) for k in range(size)])


WIDE = 128


def pad_to(value, multiple):
    return -(-value // multiple) * multiple


def planes(value):
    parts = []
    for _ in range(3):
        part = value.astype(bf16)
        parts.append(part)
        value = value - part.astype(f32)
    return parts


def split_kernel(rows_f, *refs):
    parts, vecs, w_ref, out, held = refs[:4], refs[4:9], refs[9], refs[10], refs[11]
    states, channels = parts[0].shape
    held[...] = jnp.zeros_like(held)
    for k, ref in enumerate(parts):
        held[k * states : (k + 1) * states, :channels] = ref[...]
    flat = 0
    for ref in vecs:
        row, lane = divmod(flat, WIDE)
        size = ref.shape[1]
        held[4 * states + row : 4 * states + row + 1, lane : lane + size] = ref[...]
        flat += size
    for p, plane in enumerate(planes(held[...])):
        out[0, p * rows_f : (p + 1) * rows_f, :] = plane
    if w_ref.shape[1] < WIDE:
        out[0, 3 * rows_f :, :] = jnp.zeros((w_ref.shape[0], WIDE), bf16)
    out[0, 3 * rows_f :, : w_ref.shape[1]] = w_ref[...]


def float_rows(states, vec_rows):
    return pad_to(4 * states + vec_rows, 8)


def pack(parts, vecs, w):
    vecs = [v.reshape(1, -1) for v in vecs]
    rows_f = float_rows(parts[0].shape[0], -(-sum(v.shape[1] for v in vecs) // WIDE))
    return pl.pallas_call(
        partial(split_kernel, rows_f),
        out_shape=jax.ShapeDtypeStruct((1, 3 * rows_f + w.shape[0], WIDE), bf16),
        in_specs=[vspec()] * 10,
        out_specs=vspec(),
        scratch_shapes=[pltpu.VMEM((rows_f, WIDE), f32)],
        compiler_params=params(4),
        name="pack",
    )(*held_in_hbm(*parts, *vecs, w))


def merge_kernel(which, shift, sc, own, got, out):
    here = (sc[which] >> shift) & 1
    for i in range(own.shape[0]):
        out[2 * i + here] = own[i]
        out[2 * i + 1 - here] = got[i]


def merge(scalars, own, got, which, shift):
    return pl.pallas_call(
        partial(merge_kernel, which, shift),
        out_shape=jax.ShapeDtypeStruct((2 * own.shape[0], *own.shape[1:]), own.dtype),
        in_specs=[sspec(), vspec(), vspec()],
        out_specs=vspec(),
        compiler_params=params(4),
        cost_estimate=cost(1),
        name="merge",
    )(scalars, own, got)


def collect_kernel(blob, out):
    for d in range(out.shape[0]):
        out[d] = blob[d, :, : out.shape[2]]


def collect(blob, channels, cols):
    n, rows, _ = blob.shape
    if (rows - channels) % channels:
        return blob[:, rows - channels :, :cols]
    return pl.pallas_call(
        collect_kernel,
        out_shape=jax.ShapeDtypeStruct((n, channels, cols), bf16),
        grid=(1,),
        in_specs=[pl.BlockSpec((n, channels, WIDE), lambda i: (0, rows // channels - 1, 0))],
        out_specs=pl.BlockSpec((n, channels, cols), lambda i: (0, 0, 0)),
        compiler_params=params(4),
        cost_estimate=cost(1),
        name="collect",
    )(blob)


INNER = 32


def powers(table_r, table_i, zr, zi, count):
    cr, ci = jnp.ones_like(zr), jnp.zeros_like(zi)
    for b in range(count):
        table_r[b] = cr
        table_i[b] = ci
        if b + 1 < count:
            cr, ci = cr * zr - ci * zi, cr * zi + ci * zr


def taps_kernel(n, states, channels, sc, blob, out, par_out, vec_out, b_out, table_r, table_i, part, held):
    rank_t = sc[1]
    per = vec_out.shape[1] // n
    rows_f = float_rows(states, VEC_ROWS(per))
    plane = [blob[:, k * rows_f : (k + 1) * rows_f, :].astype(f32) for k in range(3)]
    held[...] = plane[0] + plane[1] + plane[2]
    for d in range(n):
        for k in range(4):
            par_out[k, d * states : (d + 1) * states, :] = held[d, k * states : (k + 1) * states, :channels]
        top = 4 * states
        for k in range(4):
            row, lane = divmod(k * per, WIDE)
            vec_out[k : k + 1, d * per : (d + 1) * per] = held[d, top + row : top + row + 1, lane : lane + per]
        row, lane = divmod(4 * per, WIDE)
        b_out[:, 2 * d * per : 2 * (d + 1) * per] = held[d, top + row : top + row + 1, lane : lane + 2 * per]
    log_step = vec_out[2:3, 0:channels]
    for t in range(1, vec_out.shape[1] // channels):
        log_step = jnp.where(rank_t == t, vec_out[2:3, t * channels : (t + 1) * channels], log_step)
    vec_out[4:5, 0:channels] = log_step
    step = jnp.exp(log_step)
    decay = jnp.exp(par_out[0]) * step
    turn = par_out[1] * step
    size = jnp.exp(-decay)
    powers(table_r, table_i, size * jnp.cos(turn), size * jnp.sin(turn), INNER)
    far = jnp.exp(-INNER * decay)
    far_r, far_i = far * jnp.cos(INNER * turn), far * jnp.sin(INNER * turn)
    total = decay.shape[0]

    def block(a, carry):
        ar, ai = carry
        for b in range(INNER):
            value = ar * table_r[b] - ai * table_i[b]
            part[b * 8 : (b + 1) * 8, :] = jnp.sum(value.reshape(total // 8, 8, channels), axis=0)
        summed = part[pl.ds(0, INNER, stride=8), :]
        for q in range(1, 8):
            summed = summed + part[pl.ds(q, INNER, stride=8), :]
        out[pl.ds(pl.multiple_of(a * INNER, INNER), INNER), :] = summed.astype(bf16)
        return ar * far_r - ai * far_i, ar * far_i + ai * far_r

    lax.fori_loop(0, out.shape[0] // INNER, block, (par_out[2] * step, par_out[3] * step))


def VEC_ROWS(per):
    return -(-6 * per // WIDE)


def make_taps(scalars, blob, states, length, width, channels):
    n = blob.shape[0]
    total = n * states
    return pl.pallas_call(
        partial(taps_kernel, n, states, channels),
        out_shape=[
            jax.ShapeDtypeStruct((length, channels), bf16),
            jax.ShapeDtypeStruct((4, total, channels), f32),
            jax.ShapeDtypeStruct((8, width), f32),
            jax.ShapeDtypeStruct((1, 2 * width), f32),
        ],
        in_specs=[sspec(), vspec()],
        out_specs=[vspec()] * 4,
        scratch_shapes=[
            pltpu.VMEM((INNER, total, channels), f32),
            pltpu.VMEM((INNER, total, channels), f32),
            pltpu.VMEM((INNER * 8, channels), f32),
            pltpu.VMEM((n, float_rows(states, VEC_ROWS(width // n)), WIDE), f32),
        ],
        compiler_params=params(8),
        cost_estimate=cost(7),
        name="taps",
    )(scalars, blob)


def taps_back_kernel(
    n, states, sc, par, vec, grad_a, grad_b, gain8, bias8, out8, keep_out, send_out, vec_sum, table_r, table_i, summed, held, msg
):
    rank_t = sc[1]
    length, channels = summed.shape
    width = vec.shape[1]
    rate = jnp.exp(par[0])
    step = jnp.exp(vec[4:5, 0:channels])
    decay = rate * step
    turn = par[1] * step
    w_re, w_im = par[2], par[3]
    size = jnp.exp(-decay)
    powers(table_r, table_i, size * jnp.cos(turn), size * jnp.sin(turn), INNER)
    far = jnp.exp(-INNER * decay)
    far_r, far_i = far * jnp.cos(INNER * turn), far * jnp.sin(INNER * turn)
    total = decay.shape[0]
    summed[...] = grad_a[:length, :].astype(f32) + grad_b[:length, :].astype(f32)
    zero = jnp.zeros((total, channels), f32)

    def block(k, carry):
        a = length // INNER - 1 - k
        s0r, s0i, s1r, s1i = [held[q] for q in range(4)]
        s1r, s1i = s1r + INNER * s0r, s1i + INNER * s0i
        s0r, s0i = s0r * far_r - s0i * far_i, s0r * far_i + s0i * far_r
        s1r, s1i = s1r * far_r - s1i * far_i, s1r * far_i + s1i * far_r
        for q, value in enumerate((s0r, s0i, s1r, s1i)):
            held[q] = value
        rows = summed[pl.ds(pl.multiple_of(a * INNER, INNER), INNER), :]
        group = min(32, total)
        for c in range(total // group):
            here = slice(c * group, (c + 1) * group)
            u0r, u0i, u1r, u1i = [held[q, here, :] for q in range(4)]
            tail_r = tail_i = jnp.zeros((group, channels), f32)
            for b in reversed(range(INNER)):
                g = jnp.broadcast_to(rows[b : b + 1, :], (group, channels))
                if b:
                    tail_r, tail_i = tail_r + g * table_r[b, here, :], tail_i + g * table_i[b, here, :]
                    u1r, u1i = u1r + tail_r, u1i + tail_i
                else:
                    tail_r = tail_r + g
            u0r, u0i = u0r + tail_r, u0i + tail_i
            for q, value in enumerate((u0r, u0i, u1r, u1i)):
                held[q, here, :] = value
        return carry

    for q in range(4):
        held[q] = zero
    lax.fori_loop(0, length // INNER, block, 0)
    s0r, s0i, s1r, s1i = [held[q] for q in range(4)]
    wr0 = w_re * s0r - w_im * s0i
    wr1 = w_re * s1r - w_im * s1i
    wi1 = w_re * s1i + w_im * s1r
    dt = jnp.sum(step * (wr0 - decay * wr1 - turn * wi1), axis=0, keepdims=True)
    held[0], held[1] = -step * decay * wr1, -step * step * wi1
    held[2], held[3] = step * s0r, -step * s0i
    rows_w = channels
    lines = width // WIDE
    msg[...] = jnp.zeros_like(msg)
    for d in range(n):
        for k in range(4):
            msg[d, rows_w + k * states : rows_w + (k + 1) * states, :channels] = held[
                k, d * states : (d + 1) * states, :
            ].astype(bf16)
    gain_sum, bias_sum, out_sum = gain8[0:1, :], bias8[0:1, :], out8[0:1, :]
    copies = WIDE // channels
    lane = lax.broadcasted_iota(jnp.int32, (1, WIDE), 1) // channels
    skip_row = jnp.concatenate([summed[0:1, :]] * copies, axis=1) if copies > 1 else summed[0:1, :]
    dt_row = jnp.concatenate([dt] * copies, axis=1) if copies > 1 else dt
    for line in range(lines):
        at = slice(line * WIDE, (line + 1) * WIDE)
        mine = lane + line * copies == rank_t
        rows = [
            gain_sum[:, at],
            bias_sum[:, at],
            jnp.where(mine, dt_row, 0.0),
            jnp.where(mine, skip_row, 0.0),
            out_sum[:, at],
            out_sum[:, width + line * WIDE : width + (line + 1) * WIDE],
        ]
        for k, row in enumerate(rows):
            vec_sum[k * lines + line : k * lines + line + 1, :] = row
    here = sc[0] & 1
    for i in range(n // 2):
        keep_out[i] = msg[2 * i + here]
        send_out[i] = msg[2 * i + 1 - here]


def taps_back(scalars, par, vec, grads, gain8, bias8, out8, length, n, states):
    channels = grads[0].shape[1]
    width = vec.shape[1]
    total = par.shape[1]
    rows = pad_to(channels + 4 * states, 16)
    return pl.pallas_call(
        partial(taps_back_kernel, n, states),
        out_shape=[jax.ShapeDtypeStruct((n // 2, rows, WIDE), bf16)] * 2
        + [jax.ShapeDtypeStruct((6 * (width // WIDE), WIDE), f32)],
        in_specs=[sspec()] + [vspec()] * 7,
        out_specs=[vspec()] * 3,
        scratch_shapes=[
            pltpu.VMEM((INNER, total, channels), f32),
            pltpu.VMEM((INNER, total, channels), f32),
            pltpu.VMEM((length, channels), f32),
            pltpu.VMEM((4, total, channels), f32),
            pltpu.VMEM((n, rows, WIDE), bf16),
        ],
        compiler_params=params(10),
        cost_estimate=cost(10),
        name="taps_back",
    )(scalars, par, vec, *grads, gain8, bias8, out8)


ROWS = 32
TILE = 16
LANES = 128


def chunks(block, width):
    step = min(64, block)
    for r in range(block // step):
        for c in range(width // LANES):
            yield slice(r * step, (r + 1) * step), slice(c * LANES, (c + 1) * LANES)


def row_sums(x):
    ones = jnp.ones((x.shape[1], LANES), bf16)
    return jnp.dot(x, ones, preferred_element_type=f32)


def column_sums(x):
    ones = jnp.ones((8, x.shape[0]), bf16)
    return jnp.dot(ones, x, preferred_element_type=f32)


def whole_block(base, block):
    return pl.ds(base if isinstance(base, int) else pl.multiple_of(base, block), block)


def shifted(rows, base):
    size = rows.stop - rows.start
    if isinstance(base, int):
        return pl.ds(base + rows.start, size)
    return pl.ds(pl.multiple_of(base + rows.start, size), size)


def tiles(first, last, width, body):
    def step(r, carry):
        row = pl.multiple_of(r * TILE, TILE)
        for c in range(width // LANES):
            body(row, slice(c * LANES, (c + 1) * LANES))
        return carry

    lax.fori_loop(first // TILE, last // TILE, step, 0)


def enter_kernel(n, blocks, block, sc, vec, basis_ref, basis_low, *refs):
    pieces = refs[:n]
    tok_all, sig, xs, sig_out, xhat_out, scale_out = refs[n : n + 6]
    xhat, scale, mean, square, sems, sem_in = refs[n + 6 :]
    length, width = tok_all.shape
    moves = gather_rows(sc[0], pieces, tok_all, sem_in)
    for move in moves:
        move.start()
    for move in moves:
        move.wait()
    saves = [(sig, sig_out), (xhat, xhat_out), (scale, scale_out)]

    def transform(j, carry):
        base = j * block
        side = j % 2
        at = whole_block(base, block)
        mean[side] = row_sums(tok_all[at, :]) * (1.0 / width)
        for r, c in chunks(block, width):
            centred = tok_all[shifted(r, base), c].astype(f32) - mean[side, r, :]
            square[side, r, c] = (centred * centred).astype(bf16)
        scale[at, :] = lax.rsqrt(row_sums(square[side]) * (1.0 / width) + epsilon)
        for r, c in chunks(block, width):
            to = shifted(r, base)
            value = (tok_all[to, c].astype(f32) - mean[side, r, :]) * scale[to, :]
            xhat[to, c] = value.astype(bf16)
            sig[to, c] = (value * vec[0:1, c] + vec[1:2, c]).astype(bf16)
        for copy in copies(sems, 0, block, j, saves):
            copy.start()
        value = sig[at, :]
        xs[j] = jnp.dot(basis_ref[...], value, preferred_element_type=f32) + jnp.dot(
            basis_low[...], value, preferred_element_type=f32
        )
        return carry

    for j in range(blocks):
        transform(j, 0)
    for j in range(blocks):
        for copy in copies(sems, 0, block, j, saves):
            copy.wait()


def enter(scalars, vec, pieces, length, block):
    n = len(pieces)
    width = pieces[0].shape[1]
    blocks = length // block
    return pl.pallas_call(
        partial(enter_kernel, n, blocks, block),
        out_shape=[
            keep((length, width), bf16),
            keep((length, width), bf16),
            keep((blocks, 2 * block, width), f32),
            hbm((length, width), bf16),
            hbm((length, width), bf16),
            hbm((length, LANES), f32),
        ],
        in_specs=[sspec()] + [vspec()] * 3 + [hspec()] * n,
        out_specs=[vspec()] * 3 + [hspec()] * 3,
        scratch_shapes=[
            pltpu.VMEM((length, width), bf16),
            pltpu.VMEM((length, LANES), f32),
            pltpu.VMEM((2, block, LANES), f32),
            pltpu.VMEM((2, block, width), bf16),
            pltpu.SemaphoreType.DMA((3, blocks)),
            pltpu.SemaphoreType.DMA((n,)),
        ],
        compiler_params=params(8),
        cost_estimate=cost(7),
        name="enter",
    )(scalars, vec, *two_parts(basis(block)), *pieces)


def forward_kernel(n, n_t, blocks, block, sc, lengths, vec, b_out, basis_ref, basis_low, basis_t, basis_t_low, tok_all, sig, xs, *refs):
    tap_parts, w_parts = refs[:n_t], refs[n_t : 2 * n_t]
    out_h, spec_h, w_h, active_h, slope_h, val_h, gate_h = refs[2 * n_t : 2 * n_t + 7]
    taps, raw, zs, zs_low, mix, pre, spec, w, out, active, slope, val_a, gate, sems, sem_w = refs[2 * n_t + 7 :]
    rank_t = sc[1]
    seq_len = lengths[rank_t * n + sc[0]]
    results = [(out, out_h), (active, active_h), (slope, slope_h), (val_a, val_h), (gate, gate_h)]
    length, width = tok_all.shape
    channels = width // n_t
    half = block // 2
    scale = 1.0 / block
    for e in range(n_t):
        owner = rank_t ^ e
        at = pl.ds(pl.multiple_of(owner * channels, channels), channels)
        if channels % LANES == 0:
            taps[:, at] = tap_parts[e][...]
        else:
            for t in range(n_t):

                @pl.when(owner == t)
                def _(e=e, t=t):
                    taps[:, t * channels : (t + 1) * channels] = tap_parts[e][...]

        count, _, cols = w_parts[e].shape
        for d in range(count):
            w[at, d * cols : (d + 1) * cols] = w_parts[e][d]
    copy_w = pltpu.make_async_copy(w, w_h, sem_w.at[0])
    copy_w.start()

    def spectrum(d, carry):
        at = whole_block(d * block, block)
        value = taps[at, :]
        raw[d] = jnp.dot(basis_ref[...], value, preferred_element_type=f32) + jnp.dot(
            basis_low[...], value, preferred_element_type=f32
        )
        return carry

    for d in range(blocks):
        spectrum(d, 0)

    def product(sign, row, lanes):
        re, im = pl.ds(row, TILE), pl.ds(pl.multiple_of(row + block, TILE), TILE)
        xr = [xs[j, re, lanes] for j in range(blocks)]
        xi = [xs[j, im, lanes] for j in range(blocks)]
        kr, ki = [], []
        for d in range(blocks):
            r, i = raw[d, re, lanes], raw[d, im, lanes]
            if d:
                pr, pi = raw[d - 1, re, lanes], raw[d - 1, im, lanes]
                r, i = (r - pi, i + pr) if sign > 0 else (r + pi, i - pr)
            kr.append(r * scale)
            ki.append(i * scale)
            spec[d, re, lanes] = kr[d].astype(bf16)
            spec[d, im, lanes] = ki[d].astype(bf16)
        for m in range(blocks):
            zr = zi = None
            for j in range(m + 1):
                d = m - j
                pr = xr[j] * kr[d] - xi[j] * ki[d]
                pi = xr[j] * ki[d] + xi[j] * kr[d]
                zr = pr if zr is None else zr + pr
                zi = pi if zi is None else zi + pi
            for at, value in ((re, zr), (im, zi)):
                high = value.astype(bf16)
                zs[m, at, lanes] = high
                zs_low[m, at, lanes] = (value - high.astype(f32)).astype(bf16)

    tiles(0, half, width, partial(product, 1))
    tiles(half, block, width, partial(product, -1))
    copy_spec = pltpu.make_async_copy(spec, spec_h, sem_w.at[1])
    copy_spec.start()

    def tail(j, carry):
        value = zs[j]
        rest = jnp.dot(basis_t_low[...], value, preferred_element_type=f32) + jnp.dot(
            basis_t[...], zs_low[j], preferred_element_type=f32
        )
        side = j % 2
        mix[side] = jnp.dot(basis_t[...], value, preferred_element_type=f32) + rest

        base = j * block
        for r, c in chunks(block, width):
            to = shifted(r, base)
            v = mix[side, r, c] + vec[3:4, c] * sig[to, c].astype(f32)
            sq = v * v
            t = jnp.tanh(v * (0.7978845608 + (0.7978845608 * 0.044715) * sq))
            half_t = 0.5 + 0.5 * t
            active[to, c] = (v * half_t).astype(bf16)
            inner = 0.7978845608 * 0.5 + (0.7978845608 * 1.5 * 0.044715) * sq
            slope[to, c] = (half_t + v * (1.0 - t * t) * inner).astype(bf16)
        whole = whole_block(base, block)
        pre[side] = jnp.dot(active[whole, :], w[...], preferred_element_type=f32)
        for r, c in chunks(block, width):
            to = shifted(r, base)
            far = slice(width + c.start, width + c.stop)
            a = pre[side, r, c] + b_out[:, c]
            t = 0.5 * jnp.tanh(0.5 * (pre[side, r, far] + b_out[:, far]))
            g = 0.5 + t
            place = base + r.start + lax.broadcasted_iota(jnp.int32, a.shape, 0)
            add = jnp.where(place < seq_len, a * g, 0.0)
            out[to, c] = (tok_all[to, c].astype(f32) + add).astype(bf16)
            val_a[to, c] = (a * (0.5 - t)).astype(bf16)
            gate[to, c] = g.astype(bf16)
        for c in copies(sems, 0, block, j, results):
            c.start()
        return carry

    for j in range(blocks):
        tail(j, 0)
    copy_w.wait()
    copy_spec.wait()
    for j in range(blocks):
        for c in copies(sems, 0, block, j, results):
            c.wait()


def forward(scalars, lengths, vec, b_out, entered, tap_parts, w_parts, n, block):
    tok_all, sig, xs = entered
    n_t = len(tap_parts)
    length, width = tok_all.shape
    blocks = length // block
    table = basis(block)
    full = hbm((length, width), bf16)
    buffer = pltpu.VMEM((length, width), bf16)
    return pl.pallas_call(
        partial(forward_kernel, n, n_t, blocks, block),
        out_shape=[
            full,
            hbm((blocks, 2 * block, width), bf16),
            hbm((width, 2 * width), bf16),
            full,
            full,
            full,
            full,
        ],
        in_specs=[sspec()] * 2 + [vspec()] * (9 + 2 * n_t),
        out_specs=[hspec()] * 7,
        scratch_shapes=[
            buffer,
            pltpu.VMEM((blocks, 2 * block, width), f32),
            pltpu.VMEM((blocks, 2 * block, width), bf16),
            pltpu.VMEM((blocks, 2 * block, width), bf16),
            pltpu.VMEM((2, block, width), f32),
            pltpu.VMEM((2, block, 2 * width), f32),
            pltpu.VMEM((blocks, 2 * block, width), bf16),
            pltpu.VMEM((width, 2 * width), bf16),
            buffer,
            buffer,
            buffer,
            buffer,
            buffer,
            pltpu.SemaphoreType.DMA((5, blocks)),
            pltpu.SemaphoreType.DMA((2,)),
        ],
        compiler_params=params(26),
        cost_estimate=cost(15),
        name="forward",
    )(
        scalars,
        lengths,
        vec,
        b_out,
        *two_parts(table),
        *two_parts(table.T),
        *held_in_vmem(tok_all, sig, xs),
        *tap_parts,
        *w_parts,
    )


def mix_back_kernel(n, n_t, blocks, block, sc, lengths, basis_ref, basis_t, w_h, *refs):
    inputs, pieces = refs[:4], refs[4:5]
    kept, sent, grad_pre, grad_mix, spec_g, bias_grad = refs[5:11]
    val_a, gate, slope, sig, w, cot, xs, act_f, comb, sems, sem_w, sem_in = refs[11:]
    loads = list(zip(inputs, (val_a, gate, slope, sig)))
    seq_len, core = lengths[sc[1] * n + sc[0]], sc[1] & 1
    moves = gather_rows(sc[0], pieces, cot, sem_in)
    for move in moves:
        move.start()
    for c in copies(sems, 0, block, 0, loads):
        c.start()
    copy_w = pltpu.make_async_copy(w_h, w, sem_w.at[0])
    copy_w.start()
    for j in range(1, blocks):
        for c in copies(sems, 0, block, j, loads):
            c.start()
    for move in moves:
        move.wait()
    length, width = cot.shape
    half = block // 2
    bias_grad[...] = jnp.zeros_like(bias_grad)

    def front(j, carry):
        for c in copies(sems, 0, block, j, loads):
            c.wait()

        base = j * block
        for r, c in chunks(block, width):
            to = shifted(r, base)
            far = slice(width + c.start, width + c.stop)
            q = cot[to, c].astype(f32)
            place = base + r.start + lax.broadcasted_iota(jnp.int32, q.shape, 0)
            g = gate[to, c].astype(f32)
            qg = jnp.where(place < seq_len, q * g, 0.0)
            grad_pre[to, c] = qg.astype(bf16)
            grad_pre[to, far] = (qg * val_a[to, c].astype(f32)).astype(bf16)

        @pl.when(j == 0)
        def _():
            copy_w.wait()

        whole = whole_block(base, block)
        bias_grad[...] += column_sums(grad_pre[whole, :])
        xs[j] = jnp.dot(basis_ref[...], sig[whole, :], preferred_element_type=f32)
        act_f[...] = lax.dot_general(
            grad_pre[whole, :], w[...], (((1,), (1,)), ((), ())), preferred_element_type=f32
        )

        for r, c in chunks(block, width):
            to = shifted(r, base)
            grad = act_f[r, c].astype(bf16).astype(f32) * slope[to, c].astype(f32)
            grad_mix[to, c] = grad.astype(bf16)
        spec_g[j] = jnp.dot(basis_ref[...], grad_mix[whole, :], preferred_element_type=f32)
        return carry

    lax.fori_loop(0, blocks, front, 0)

    def correlate(sign, row, lanes):
        re, im = pl.ds(row, TILE), pl.ds(pl.multiple_of(row + block, TILE), TILE)
        xr = [xs[j, re, lanes] for j in range(blocks)]
        xi = [xs[j, im, lanes] for j in range(blocks)]
        gr = [spec_g[j, re, lanes] for j in range(blocks)]
        gi = [spec_g[j, im, lanes] for j in range(blocks)]
        next_r = next_i = None
        for d in reversed(range(blocks)):
            dr = di = None
            for m in range(d, blocks):
                j = m - d
                pr = xr[j] * gr[m] + xi[j] * gi[m]
                pi = xr[j] * gi[m] - xi[j] * gr[m]
                dr = pr if dr is None else dr + pr
                di = pi if di is None else di + pi
            cr, ci = dr, di
            if next_r is not None:
                cr = dr + next_i if sign > 0 else dr - next_i
                ci = di - next_r if sign > 0 else di + next_r
            comb[d, re, lanes] = cr.astype(bf16)
            comb[d, im, lanes] = ci.astype(bf16)
            next_r, next_i = dr, di

    tiles(0, half, width, partial(correlate, 1))
    tiles(half, block, width, partial(correlate, -1))
    channels = width // n_t

    def store(t, to, value):
        @pl.when(core == t & 1)
        def _():
            kept[t >> 1, to, : value.shape[1]] = value

        @pl.when(core != t & 1)
        def _():
            sent[t >> 1, to, : value.shape[1]] = value

    def finish(d, carry):
        act_f[...] = jnp.dot(basis_t[...], comb[d], preferred_element_type=f32)
        to = pl.ds(pl.multiple_of(d * block, block), block)
        for t in range(n_t):
            part = act_f[:, t * channels : (t + 1) * channels] * (1.0 / block)
            store(t, to, part.astype(bf16))
        return carry

    lax.fori_loop(0, blocks, finish, 0)

def mix_back(scalars, lengths, w, saved, cot, block, n, n_t):
    length, width = saved[0].shape
    blocks = length // block
    channels = width // n_t
    table = basis(block)
    halves = jax.ShapeDtypeStruct((n_t // 2, length, channels), bf16)
    buffer = pltpu.VMEM((length, width), bf16)
    return pl.pallas_call(
        partial(mix_back_kernel, n, n_t, blocks, block),
        out_shape=[
            halves,
            halves,
            keep((length, 2 * width), bf16),
            keep((length, width), bf16),
            keep((blocks, 2 * block, width), f32),
            jax.ShapeDtypeStruct((8, 2 * width), f32),
        ],
        in_specs=[sspec()] * 2 + [vspec()] * 2 + [hspec()] * 6,
        out_specs=[vspec()] * 6,
        scratch_shapes=[
            buffer,
            buffer,
            buffer,
            buffer,
            pltpu.VMEM((width, 2 * width), bf16),
            buffer,
            pltpu.VMEM((blocks, 2 * block, width), f32),
            pltpu.VMEM((block, width), f32),
            pltpu.VMEM((blocks, 2 * block, width), bf16),
            pltpu.SemaphoreType.DMA((4, blocks)),
            pltpu.SemaphoreType.DMA((1,)),
            pltpu.SemaphoreType.DMA((1,)),
        ],
        compiler_params=params(20),
        cost_estimate=cost(12),
        name="mix_back",
    )(
        scalars,
        lengths,
        jnp.asarray(table, bf16),
        jnp.asarray(table.T, bf16),
        *held_in_hbm(w, *saved, cot),
    )


def weight_back_kernel(n, sc, active, grad_pre, w_keep, w_send):
    core = sc[1] & 1
    groups, _, channels, cols = w_keep.shape
    for t in range(2 * groups):
        value = lax.dot_general(
            active[:, t * channels : (t + 1) * channels],
            grad_pre[...],
            (((0,), (0,)), ((), ())),
            preferred_element_type=f32,
        ).astype(bf16)

        @pl.when(core == t & 1)
        def _(t=t, value=value):
            for d in range(n):
                w_keep[t >> 1, d] = value[:, d * cols : (d + 1) * cols]

        @pl.when(core != t & 1)
        def _(t=t, value=value):
            for d in range(n):
                w_send[t >> 1, d] = value[:, d * cols : (d + 1) * cols]


def weight_back(scalars, active, grad_pre, n, n_t):
    width = active.shape[1]
    halves = jax.ShapeDtypeStruct((n_t // 2, n, width // n_t, 2 * width // n), bf16)
    return pl.pallas_call(
        partial(weight_back_kernel, n),
        out_shape=[halves, halves],
        in_specs=[sspec()] + [vspec()] * 2,
        out_specs=[vspec()] * 2,
        compiler_params=params(8),
        cost_estimate=cost(3),
        name="weight_back",
    )(scalars, active, *held_in_vmem(grad_pre))


def join_kernel(sc, part_keep, part_send, w_a, w_b, keep_out, send_out):
    here = sc[0] & 1
    _, channels, cols = w_a.shape
    for i in range(keep_out.shape[0]):
        for ref, part, k in ((keep_out, part_keep, here), (send_out, part_send, 1 - here)):
            ref[i] = part[i]
            value = w_a[2 * i + k].astype(f32) + w_b[2 * i + k].astype(f32)
            ref[i, 0:channels, :cols] = value.astype(bf16)


def join(scalars, kept, sent, w_a, w_b):
    shape = jax.ShapeDtypeStruct(kept.shape, bf16)
    return pl.pallas_call(
        join_kernel,
        out_shape=[shape, shape],
        in_specs=[sspec()] + [vspec()] * 4,
        out_specs=[vspec()] * 2,
        compiler_params=params(6),
        cost_estimate=cost(1),
        name="join",
    )(scalars, kept, sent, w_a, w_b)


def norm_back_kernel(blocks, block, sc, vec, basis_t, spec_g, grad_mix, spec_h, xhat_h, scale_h, *refs):
    pieces, (res_h, gain_grad, bias_grad) = refs[:1], refs[1:4]
    comb, sig_f, res, spec, xhat, scale, cot_all, grad, cross, mean_g, mean_c, gain_all, sems, sem_w, sem_in = refs[4:]
    loads = [(xhat_h, xhat), (scale_h, scale)]
    copy_spec = pltpu.make_async_copy(spec_h, spec, sem_w.at[0])
    copy_spec.start()
    for j in range(blocks):
        for c in copies(sems, 0, block, j, loads):
            c.start()
    moves = gather_rows(sc[0], pieces, cot_all, sem_in)
    for move in moves:
        move.start()
    copy_spec.wait()
    for move in moves:
        move.wait()
    length, width = xhat.shape
    for k in range(width // LANES):
        gain_all[k * LANES : (k + 1) * LANES, :] = jnp.broadcast_to(
            vec[0:1, k * LANES : (k + 1) * LANES], (LANES, LANES)
        ).T.astype(bf16)
    gain_grad[...] = jnp.zeros_like(gain_grad)
    bias_grad[...] = jnp.zeros_like(bias_grad)

    def correlate(row, lanes):
        re, im = pl.ds(row, TILE), pl.ds(pl.multiple_of(row + block, TILE), TILE)
        kr = [spec[j, re, lanes].astype(f32) for j in range(blocks)]
        ki = [spec[j, im, lanes].astype(f32) for j in range(blocks)]
        gr = [spec_g[j, re, lanes] for j in range(blocks)]
        gi = [spec_g[j, im, lanes] for j in range(blocks)]
        for j in range(blocks):
            dr = di = None
            for m in range(j, blocks):
                d = m - j
                pr = kr[d] * gr[m] + ki[d] * gi[m]
                pi = kr[d] * gi[m] - ki[d] * gr[m]
                dr = pr if dr is None else dr + pr
                di = pi if di is None else di + pi
            comb[j, re, lanes] = dr.astype(bf16)
            comb[j, im, lanes] = di.astype(bf16)

    tiles(0, block, width, correlate)

    def finish(j, carry):
        for c in copies(sems, 0, block, j, loads):
            c.wait()
        sig_f[...] = jnp.dot(basis_t[...], comb[j], preferred_element_type=f32)

        base = j * block
        for r, c in chunks(block, width):
            to = shifted(r, base)
            value = sig_f[r, c] + vec[3:4, c] * grad_mix[to, c].astype(f32)
            value = value.astype(bf16)
            grad[r, c] = value
            cross[r, c] = (value.astype(f32) * xhat[to, c].astype(f32)).astype(bf16)
        gain_grad[...] += column_sums(cross[...])
        bias_grad[...] += column_sums(grad[...])
        weights = gain_all[...]
        mean_g[...] = jnp.dot(grad[...], weights, preferred_element_type=f32) * (1.0 / width)
        mean_c[...] = jnp.dot(cross[...], weights, preferred_element_type=f32) * (1.0 / width)
        for r, c in chunks(block, width):
            to = shifted(r, base)
            g = grad[r, c].astype(f32) * vec[0:1, c]
            g = g - mean_g[r, :] - xhat[to, c].astype(f32) * mean_c[r, :]
            res[to, c] = (cot_all[to, c].astype(f32) + g * scale[to, :]).astype(bf16)
        for copy in copies(sems, 2, block, j, [(res, res_h)]):
            copy.start()
        return carry

    lax.fori_loop(0, blocks, finish, 0)
    for j in range(blocks):
        for copy in copies(sems, 2, block, j, [(res, res_h)]):
            copy.wait()


def norm_back(scalars, vec, spec, spec_g, grad_mix, xhat, scale, cot, block):
    length, width = xhat.shape
    blocks = length // block
    buffer = pltpu.VMEM((length, width), bf16)
    return pl.pallas_call(
        partial(norm_back_kernel, blocks, block),
        out_shape=[hbm((length, width), bf16)] + [jax.ShapeDtypeStruct((8, width), f32)] * 2,
        in_specs=[sspec()] + [vspec()] * 4 + [hspec()] * 4,
        out_specs=[hspec()] + [vspec()] * 2,
        scratch_shapes=[
            pltpu.VMEM((blocks, 2 * block, width), bf16),
            pltpu.VMEM((block, width), f32),
            buffer,
            pltpu.VMEM((blocks, 2 * block, width), bf16),
            buffer,
            pltpu.VMEM((length, LANES), f32),
            buffer,
            pltpu.VMEM((block, width), bf16),
            pltpu.VMEM((block, width), bf16),
            pltpu.VMEM((block, LANES), f32),
            pltpu.VMEM((block, LANES), f32),
            pltpu.VMEM((width, LANES), bf16),
            pltpu.SemaphoreType.DMA((3, blocks)),
            pltpu.SemaphoreType.DMA((1,)),
            pltpu.SemaphoreType.DMA((1,)),
        ],
        compiler_params=params(14),
        cost_estimate=cost(10),
        name="norm_back",
    )(
        scalars,
        vec,
        jnp.asarray(basis(block).T, bf16),
        *held_in_vmem(spec_g, grad_mix),
        *held_in_hbm(spec, xhat, scale, cot),
    )


def halve_kernel(which, shift, sc, kept, got, keep_out, send_out):
    here = (sc[which] >> shift) & 1
    for i in range(keep_out.shape[0]):
        for k in range(2):
            value = (kept[2 * i + k].astype(f32) + got[2 * i + k].astype(f32)).astype(bf16)

            @pl.when(here == k)
            def _(i=i, value=value):
                keep_out[i] = value

            @pl.when(here != k)
            def _(i=i, value=value):
                send_out[i] = value


def deal_kernel(shift, place, vectors, sc, kept, got, *refs):
    vecs, outs = refs[:vectors], refs[vectors:]
    here = sc[0] >> shift
    vec = vecs[0][...]
    for ref in vecs[1:]:
        vec = vec + ref[...]
    for e, out in enumerate(outs):
        out[: kept.shape[1], :] = (kept[here ^ e].astype(f32) + got[here ^ e].astype(f32)).astype(bf16)
        out[place : place + vec.shape[0], :] = vec.astype(bf16)


def deal(scalars, kept, got, vecs, shift, place):
    rows = pad_to(place + vecs[0].shape[0], 16)
    shape = jax.ShapeDtypeStruct((rows, kept.shape[2]), bf16)
    return pl.pallas_call(
        partial(deal_kernel, shift, place, len(vecs)),
        out_shape=[shape] * kept.shape[0],
        in_specs=[sspec()] + [vspec()] * (2 + len(vecs)),
        out_specs=[vspec()] * kept.shape[0],
        compiler_params=params(5),
        cost_estimate=cost(1),
        name="deal",
    )(scalars, kept, got, *vecs)


def halve(scalars, kept, got, which, shift):
    shape = jax.ShapeDtypeStruct((kept.shape[0] // 2, *kept.shape[1:]), bf16)
    return pl.pallas_call(
        partial(halve_kernel, which, shift),
        out_shape=[shape, shape],
        in_specs=[sspec(), vspec(), vspec()],
        out_specs=[vspec()] * 2,
        compiler_params=params(5),
        cost_estimate=cost(1),
        name="halve",
    )(scalars, kept, got)


def weave_kernel(n, whole, sc, *refs):
    if whole:
        pieces, out, held = [refs[0].at[s] for s in range(n)], refs[1], refs[2]
    else:
        pieces, out, held = refs[:n], refs[n], refs[n + 1]
    rank = sc[0]
    rows, width = pieces[0].shape
    step = min(rows, 32)

    def part(r, carry):
        at = pl.ds(pl.multiple_of(r * step, step), step)
        for s in range(n):
            src = s if whole else lax.rem(rank - s + n, n)
            for c in range(width // LANES):
                lanes = slice(c * LANES, (c + 1) * LANES)
                held[c, pl.ds(src, step, stride=n), :] = pieces[s][at, lanes].astype(f32)
        for c in range(width // LANES):
            lanes = slice(c * LANES, (c + 1) * LANES)
            out[at, :, lanes] = held[c].reshape(step, n, LANES).astype(bf16)
        return carry

    lax.fori_loop(0, rows // step, part, 0)


def weave(scalars, pieces):
    whole = not isinstance(pieces, list)
    n = pieces.shape[0] if whole else len(pieces)
    rows, width = pieces[0].shape
    args = [pieces] if whole else pieces
    return pl.pallas_call(
        partial(weave_kernel, n, whole),
        out_shape=jax.ShapeDtypeStruct((rows, n, width), bf16),
        in_specs=[sspec()] + [vspec()] * len(args),
        out_specs=vspec(),
        scratch_shapes=[pltpu.VMEM((width // LANES, min(rows, 32) * n, LANES), f32)],
        compiler_params=params(8),
        cost_estimate=cost(3),
        name="weave",
    )(scalars, *args)


def part_kernel(n, ordered, sc, whole, *refs):
    if ordered:
        outs, held = [refs[0].at[s] for s in range(n)], refs[1]
    else:
        outs, held = refs[-n - 1 : -1], refs[-1]
    rank = sc[0]
    rows, _, width = whole.shape
    step = min(rows, 32)

    def part(r, carry):
        at = pl.ds(pl.multiple_of(r * step, step), step)
        for c in range(width // LANES):
            lanes = slice(c * LANES, (c + 1) * LANES)
            held[c] = whole[at, :, lanes].astype(f32).reshape(step * n, LANES)
        for s in range(n):
            dst = s if ordered else lax.rem(rank + s, n)
            for c in range(width // LANES):
                lanes = slice(c * LANES, (c + 1) * LANES)
                outs[s][at, lanes] = held[c, pl.ds(dst, step, stride=n), :].astype(bf16)
        return carry

    lax.fori_loop(0, rows // step, part, 0)
    if not ordered and len(refs) > n + 1:
        for s in range(n):
            outs[s][rows:, :] = refs[0][...]


def part(scalars, whole, *extra, ordered=False):
    rows, n, width = whole.shape
    more = extra[0].shape[0] if extra else 0
    if ordered:
        shapes = [jax.ShapeDtypeStruct((n, rows, width), bf16)]
    else:
        shapes = [jax.ShapeDtypeStruct((rows + more, width), bf16)] * n
    return pl.pallas_call(
        partial(part_kernel, n, ordered),
        out_shape=shapes,
        in_specs=[sspec(), vspec()] + [vspec()] * len(extra),
        out_specs=[vspec()] * len(shapes),
        scratch_shapes=[pltpu.VMEM((width // LANES, min(rows, 32) * n, LANES), f32)],
        compiler_params=params(8),
        cost_estimate=cost(3),
        name="part",
    )(scalars, *held_in_hbm(whole, *extra))


def total_kernel(states, lines, count, sc, *refs):
    w_out, *grads = refs[count : count + 5]
    outs = refs[count + 5 :]
    channels, cols = w_out.shape
    rank = sc[0]
    total = refs[0][...].astype(f32)
    for ref in refs[1:count]:
        total = total + ref[...].astype(f32)
    w_out[...] = total[:channels, :cols]
    for k, ref in enumerate(grads):
        ref[...] = total[channels + k * states : channels + (k + 1) * states, :channels]
    top = channels + 4 * states
    for k, out in enumerate(outs):
        per = out.shape[1]
        slots = (2 * lines if k == 4 else lines) * WIDE // per
        value = jnp.zeros((1, per), f32)
        for slot in range(slots):
            line, lane = divmod(slot * per, WIDE)
            row = top + k * lines + line
            value = jnp.where(rank == slot, total[row : row + 1, lane : lane + per], value)
        out[...] = value


def totals(scalars, terms, channels, cols, states, per, lines):
    grad = jax.ShapeDtypeStruct((states, channels), f32)
    one = jax.ShapeDtypeStruct((1, per), f32)
    return pl.pallas_call(
        partial(total_kernel, states, lines, len(terms)),
        out_shape=[jax.ShapeDtypeStruct((channels, cols), f32)]
        + [grad] * 4
        + [one] * 4
        + [jax.ShapeDtypeStruct((1, 2 * per), f32)],
        in_specs=[sspec()] + [vspec()] * len(terms),
        out_specs=[vspec()] * 10,
        compiler_params=params(4),
        cost_estimate=cost(1),
        name="totals",
    )(scalars, *terms)


def local(n_dp, n_t, tokens, cotangent, lengths, ln_gain, ln_bias, lam_log, lam_im, w_re, w_im, log_dt, skip_gain, w_out, b_out):
    rows, seqs, width = tokens.shape
    assert seqs == n_dp
    length = rows * n_dp
    block = min(256, length)
    rank = lax.axis_index("dp")
    rank_t = lax.axis_index("tensor")
    channels, states = lam_log.shape
    cols = w_out.shape[1]
    per = width // n_dp
    bits = [1 << k for k in range(n_t.bit_length() - 1)]
    scalars = jnp.stack([rank, rank_t]).astype(jnp.int32)

    after = lambda value, *others: lax.optimization_barrier((value, others))[0]
    pieces = list(part(scalars, tokens))
    vecs = [after(ln_gain, pieces), ln_bias, log_dt, skip_gain, b_out]
    blob = pack([lam_log.T, lam_im.T, w_re.T, w_im.T], vecs, w_out)
    tok_pieces = dict(enumerate(pieces[:1]))
    waits, needs = {0: [], 1: [1], 2: [2, 3, 4]}, {5: 0, 6: 0, 7: 1}
    merges = {-1: ()}
    steps = n_dp.bit_length() - 1

    def send(s):
        if s not in tok_pieces and s < n_dp:
            piece = after(pieces[s], merges[min(needs.get(s, -1), steps - 1)])
            pairs = [(k, (k + s) % n_dp) for k in range(n_dp)]
            tok_pieces[s] = lax.ppermute(piece, "dp", pairs)
        return tok_pieces.get(s, ())

    for k in range(steps):
        got = flip_bit(blob, "dp", n_dp, n_dp >> (k + 1))
        before = [send(s) for s in waits.get(k, [])]
        blob = merge(scalars, after(blob, before), got, 0, steps - 1 - k)
        merges[k] = blob
    tok_pieces = [send(s) for s in range(n_dp)]
    w_own = collect(blob, channels, cols)
    taps, par_all, vec, b_full = make_taps(
        scalars, after(blob, w_own), states, length, width, channels
    )
    cot = after(part(scalars, cotangent, ordered=True)[0], blob, tok_pieces)
    cot = lax.all_to_all(cot, "dp", 0, 0, tiled=True).reshape(length, width)
    tok_all, sig, xs, sig_keep, xhat, scale = enter(scalars, vec, tok_pieces, length, block)

    def spread(own):
        parts = {0: own}
        for bit in reversed(bits):
            for e in list(parts):
                value = after(parts[e], sig) if bit == 1 else parts[e]
                parts[e | bit] = flip_bit(value, "tensor", n_t, bit)
        return [parts[e] for e in range(n_t)]

    tap_parts = spread(taps)
    w_parts = spread(w_own)

    out_t, spec, w_full, *saved = forward(
        scalars, lengths, vec, b_full, (tok_all, sig, xs), tap_parts, w_parts, n_dp, block
    )
    active, slope, val_a, gate = saved
    out_back = lax.all_to_all(out_t.reshape(n_dp, rows, width), "dp", 0, 0, tiled=True)
    saved = [val_a, gate, slope, sig_keep]
    kept, sent, grad_pre, grad_mix, spec_g, out8 = mix_back(
        scalars, lengths, w_full, saved, cot, block, n_dp, n_t
    )

    def reduce_groups(kept, sent, axis, size, which, hook=lambda value: value):
        got = hook(flip_bit(sent, axis, size, 1))
        for shift in range(1, size.bit_length() - 1):
            kept, sent = halve(scalars, kept, got, which, shift)
            got = flip_bit(sent, axis, size, 1 << shift)
        return kept[0], got[0], sent

    w_keep, w_send = weight_back(scalars, active, grad_pre, n_dp, n_t)
    *grads, sent = reduce_groups(
        kept, sent, "tensor", n_t, 1, lambda got: after(got, w_keep)
    )
    spec_g = after(spec_g, sent)
    grad_rows, gain8, bias8 = norm_back(
        scalars, vec, spec, spec_g, grad_mix, xhat, scale, cot, block
    )
    *w_two, w_sent = reduce_groups(w_keep, w_send, "tensor", n_t, 1)
    grad_rows = after(grad_rows, out_back, grads, w_sent)
    grad_back = lax.all_to_all(grad_rows.reshape(n_dp, rows, width), "dp", 0, 0, tiled=True)
    kept, sent, vec_sum = taps_back(
        scalars, par_all, vec, grads, gain8, bias8, out8, length, n_dp, states
    )
    out = weave(scalars, after(out_back, kept))
    kept, sent = join(scalars, kept, sent, *w_two)
    vec_sum = after(vec_sum, sent)
    others = [
        lax.ppermute(vec_sum, "tensor", [(k, k ^ e) for k in range(n_t)]) for e in range(1, n_t)
    ]
    vec_sum = sum(others, vec_sum)
    got = flip_bit(sent, "dp", n_dp, 1)
    got_vec = flip_bit(vec_sum, "dp", n_dp, 1)
    shift = 1
    while kept.shape[0] > 4:
        kept, sent = halve(scalars, after(kept, out), got, 0, shift)
        got = flip_bit(sent, "dp", n_dp, 1 << shift)
        vec_sum = vec_sum + got_vec
        got_vec = flip_bit(vec_sum, "dp", n_dp, 1 << shift)
        shift += 1
    vecs = [vec_sum, got_vec]
    terms = deal(scalars, after(kept, out), got, vecs, shift, channels + 4 * states)
    terms = list(terms[:1]) + [
        flip_bit(terms[e], "dp", n_dp, e << shift) for e in range(1, len(terms))
    ]
    grad_tokens = weave(scalars, after(grad_back, terms[0]))
    terms[0] = after(terms[0], grad_tokens)
    grad_w_out, *grads = totals(scalars, terms, channels, cols, states, per, width // WIDE)
    g_lam_log, g_lam_im, g_w_re, g_w_im = (g.T for g in grads[:4])
    g_gain, g_bias, g_dt, g_skip, g_b = (v.reshape(-1) for v in grads[4:])

    return (
        out,
        grad_tokens,
        g_gain,
        g_bias,
        g_lam_log,
        g_lam_im,
        g_w_re,
        g_w_im,
        g_dt,
        g_skip,
        grad_w_out,
        g_b,
    )


def solution(mesh):
    big = P("dp", "tensor", None)
    grid = P("tensor", "dp")
    line = P("dp")
    return jax.shard_map(
        partial(local, mesh.shape["dp"], mesh.shape["tensor"]),
        mesh=mesh,
        in_specs=(big, big, P(), line, line, grid, grid, grid, grid, line, line, grid, line),
        out_specs=(big, big, line, line, grid, grid, grid, grid, line, line, grid, line),
        check_vma=False,
    )
```
